512 devices in a mesh: wide: 128 (over z, x, core), narrow: 4 (over y).
Axes of the slice: x: 4, y: 4, z: 16, core: 2. Of those that a mesh axis runs over, the one named last changes fastest.
Arguments:
- tokens_in: bfloat16 [16384, 2560], P('wide', 'narrow'), may hold values from -6 to 6
- norm_gain: bfloat16 [2560], replicated, may hold values from 0.099609375 to 1.8984375
- query_weight: bfloat16 [2560, 2560], P('wide', 'narrow'), may hold values from -0.25 to 0.25
- key_weight: bfloat16 [2560, 640], P('wide', 'narrow'), may hold values from -0.125 to 0.125
- value_weight: bfloat16 [2560, 640], P('wide', 'narrow'), may hold values from -0.5 to 0.5
- out_weight: bfloat16 [2560, 2560], P('wide', 'narrow'), may hold values from -0.125 to 0.125
- cache_keys: bfloat16 [640, 131072], P('narrow', 'wide'), may hold values from -64 to 64
- cache_values: bfloat16 [640, 131072], P('narrow', 'wide'), may hold values from -24 to 24
- cached_len: int32 [32], replicated, may hold values from 1 to 4096, as said below
- append_slot: int32 [32], replicated, may hold values from 0 to 4095
- shard_owner: int32 [32], replicated, may hold values from 0 to 3
Outputs:
- attention_update: bfloat16 [16384, 2560], P('wide', 'narrow')
- appended_keys: bfloat16 [640, 131072], P('narrow', 'wide')
- appended_values: bfloat16 [640, 131072], P('narrow', 'wide')
The draws below stay inside these ranges and needn't reach their ends.
Inputs may be any that keep to these rules, and one draw needn't show every extreme that they name: `cached_len`: each request's number of cached keys; some request holds 4096.
All inputs are finite; a program needn't handle non-finite values.
Results may differ from the reference program's by a relative error of at most 0.012.
The reference program's roundings to bfloat16 on the way count: a program that leaves them out, or rounds other values in their place, can miss the bound.
Values may be sent and summed in bfloat16 or wider, within the bound.
A program may use at most 64 MiB of HBM per device.

```python
import jax
import jax.numpy as jnp
from jax import lax

D = 2560
HEADS = 32
KV_HEADS = 8
HEAD_DIM = 80
WIN = 4096
GROUP = 4
NEW = 512
REQS = 32
TOKENS = 16384


def draw_cached_len(key, part):
    key_len, key_pick = jax.random.split(key)
    lengths = jax.random.randint(key_len, (REQS,), 1, WIN + 1)
    chosen = jax.random.randint(key_pick, (), 0, REQS)
    return jnp.where(jnp.arange(REQS) == chosen, WIN, lengths).astype(jnp.int32)


def draw_cache_keys(key, part):
    key_base = jax.random.fold_in(jax.random.fold_in(key, 11), 0)
    width = KV_HEADS * HEAD_DIM
    return jax.random.normal(key_base, (REQS * WIN, width), jnp.float32).T.astype(jnp.bfloat16)


def with_ends(values, own_key, least, high):
    spot = [jax.random.randint(jax.random.fold_in(own_key, axis), (), 0, length) for axis, length in enumerate(values.shape)]
    widest = values.shape.index(max(values.shape))
    beside = spot[:widest] + [(spot[widest] + 1) % values.shape[widest]] + spot[widest + 1:]
    return values.at[tuple(spot)].set(least).at[tuple(beside)].set(high)


def block_scale(key, shape, pieces, least, largest):
    def one(dim, blocks):
        heights = jax.random.uniform(jax.random.fold_in(jax.random.fold_in(key, 6), dim), (blocks,), jnp.float32, least / len(pieces), largest / len(pieces))
        return jnp.repeat(jnp.exp(heights), shape[dim] // blocks).reshape((-1,) + (1,) * (len(shape) - dim - 1))

    loudness = one(*pieces[0])
    for cut in pieces[1:]:
        loudness = loudness * one(*cut)
    return loudness


def centred(stream_key, dims, scale, reach, shards=(), held_as=jnp.bfloat16):
    loudness = block_scale(stream_key, dims, shards, -0.22, 0.18) if shards else 1.0
    result = jax.random.normal(stream_key, dims, jnp.float32) * scale * loudness
    return jnp.minimum(jnp.maximum(result, -reach), reach).astype(held_as)


def setup_inputs(seed: int = 0) -> dict:
    arg_keys = jax.random.split(jax.random.key(seed), 12)
    tokens_in = centred(arg_keys[0], (TOKENS, D), 1.0, 6.0, ((0, 128), (1, 4)))
    norm_gain = jnp.clip(1.0 + 0.18 * jax.random.normal(arg_keys[1], (D,), jnp.float32), 0.099609375, 1.8984375).astype(jnp.bfloat16)
    query_weight = centred(arg_keys[2], (D, HEADS * HEAD_DIM), (D // 4) ** -0.5, 0.25, ((0, 128), (1, 4)))
    key_weight = centred(arg_keys[3], (D, KV_HEADS * HEAD_DIM), D ** -0.5, 0.125, ((0, 128), (1, 4)))
    value_weight = centred(arg_keys[4], (D, KV_HEADS * HEAD_DIM), (D // 16) ** -0.5, 0.5, ((0, 128), (1, 4)))
    out_weight = centred(arg_keys[5], (HEADS * HEAD_DIM, D), (HEADS * HEAD_DIM) ** -0.5, 0.125, ((0, 128), (1, 4)))
    cache_keys = draw_cache_keys(jax.random.fold_in(arg_keys[11], 71), 0)
    cache_values = centred(arg_keys[7], (KV_HEADS * HEAD_DIM, REQS * WIN), 4.0, 24.0, ((0, 4), (1, 128)))
    cached_len = draw_cached_len(jax.random.fold_in(arg_keys[11], 71), 0)
    append_slot = with_ends(jax.random.randint(arg_keys[9], (REQS,), 0, WIN), jax.random.fold_in(arg_keys[9], 1), 0, WIN - 1).astype(jnp.int32)
    shard_owner = with_ends(jax.random.randint(arg_keys[10], (REQS,), 0, GROUP), jax.random.fold_in(arg_keys[10], 1), 0, GROUP - 1).astype(jnp.int32)
    return dict(tokens_in=tokens_in, norm_gain=norm_gain, query_weight=query_weight, key_weight=key_weight, value_weight=value_weight, out_weight=out_weight, cache_keys=cache_keys, cache_values=cache_values, cached_len=cached_len, append_slot=append_slot, shard_owner=shard_owner)


EPSILON = 1e-05
ROPE_BASE = 10000.0

def rms_normed(rows_in, gain):
    values = rows_in.astype(jnp.float32)
    scaling = lax.rsqrt(lax.optimization_barrier(jnp.mean(values * values, axis=-1, keepdims=True)) + EPSILON)
    return (values * scaling * gain.astype(jnp.float32)).astype(jnp.bfloat16)

def rotate(values, positions):
    half_dim = values.shape[-1] // 2
    inverse = ROPE_BASE ** (-(jnp.arange(half_dim, dtype=jnp.float32) * (2.0 / values.shape[-1])))
    angles = positions.astype(jnp.float32)[:, None] * inverse[None, :]
    cos_part = jnp.cos(angles)[:, None, :]
    sin_part = jnp.sin(angles)[:, None, :]
    lower = values[..., :half_dim]
    higher = values[..., half_dim:]
    return jnp.concatenate([lower * cos_part - higher * sin_part, higher * cos_part + lower * sin_part], axis=-1)

def reference(tokens_in, norm_gain, query_weight, key_weight, value_weight, out_weight, cache_keys, cache_values, cached_len, append_slot, shard_owner):
    normed = rms_normed(tokens_in, norm_gain)
    repeats = HEADS // KV_HEADS
    shard_rows = WIN // GROUP
    kv_width = KV_HEADS * HEAD_DIM
    new_steps = jnp.arange(NEW, dtype=jnp.int32)
    positions = jnp.repeat(cached_len, NEW, total_repeat_length=TOKENS) + jnp.tile(new_steps, REQS)
    query_all = jnp.dot(normed, query_weight, preferred_element_type=jnp.float32).reshape(TOKENS, HEADS, HEAD_DIM)
    query_all = rotate(query_all, positions).astype(jnp.bfloat16)
    key_all = jnp.dot(normed, key_weight, preferred_element_type=jnp.float32).reshape(TOKENS, KV_HEADS, HEAD_DIM)
    key_all = rotate(key_all, positions).astype(jnp.bfloat16).reshape(TOKENS, kv_width)
    value_all = jnp.dot(normed, value_weight, preferred_element_type=jnp.float32).astype(jnp.bfloat16)
    storage = jnp.arange(WIN, dtype=jnp.int32)
    scale = HEAD_DIM ** (-0.5)

    def per_request(request):
        length = cached_len[request]
        offset = append_slot[request]
        owner = shard_owner[request]
        cycle = (storage // shard_rows - owner) % GROUP * shard_rows + storage % shard_rows
        cached_pos = (cycle - offset + length) % WIN
        cached_ok = cached_pos < length
        first_row = (request * WIN).astype(jnp.int32)
        old_keys = lax.dynamic_slice_in_dim(cache_keys, first_row, WIN, 1).T
        old_values = lax.dynamic_slice_in_dim(cache_values, first_row, WIN, 1).T
        first_new = (request * NEW).astype(jnp.int32)
        fresh_keys = lax.dynamic_slice_in_dim(key_all, first_new, NEW, 0)
        fresh_values = lax.dynamic_slice_in_dim(value_all, first_new, NEW, 0)
        req_queries = lax.dynamic_slice_in_dim(query_all, first_new, NEW, 0)
        keys_joined = jnp.concatenate([old_keys, fresh_keys], axis=0).reshape(WIN + NEW, KV_HEADS, HEAD_DIM)
        values_joined = jnp.concatenate([old_values, fresh_values], axis=0).reshape(WIN + NEW, KV_HEADS, HEAD_DIM)
        key_pos = jnp.concatenate([cached_pos, length + new_steps])
        key_ok = jnp.concatenate([cached_ok, jnp.ones((NEW,), dtype=bool)])
        query_pos = length + new_steps
        allowed = key_ok[None, :] & (key_pos[None, :] <= query_pos[:, None]) & (query_pos[:, None] - key_pos[None, :] < WIN)

        def per_group(group):
            group_queries = lax.dynamic_slice_in_dim(req_queries, group * repeats, repeats, 1).astype(jnp.float32)
            group_keys = lax.dynamic_slice_in_dim(keys_joined, group, 1, 1)[:, 0].astype(jnp.float32)
            group_values = lax.dynamic_slice_in_dim(values_joined, group, 1, 1)[:, 0].astype(jnp.float32)
            scores = jnp.einsum('trd,kd->rtk', group_queries, group_keys) * scale
            masked = jnp.where(allowed[None], scores, -jnp.inf)
            top_score = lax.optimization_barrier(jnp.max(masked, axis=-1, keepdims=True))
            weights = jnp.exp(masked - top_score)
            total = lax.optimization_barrier(jnp.sum(weights, axis=-1))
            rounded = lax.optimization_barrier(weights.astype(jnp.bfloat16))
            mixed = jnp.einsum('rtk,kd->rtd', rounded.astype(jnp.float32), group_values)
            return mixed / total[:, :, None]
        per_head = lax.map(per_group, jnp.arange(KV_HEADS, dtype=jnp.int32))
        attended = jnp.transpose(per_head, (2, 0, 1, 3)).reshape(NEW, HEADS * HEAD_DIM).astype(jnp.bfloat16)
        new_index = (cycle - offset) % WIN
        written = new_index < NEW
        take_rows = jnp.minimum(new_index, NEW - 1)
        put_keys = jnp.where(written[:, None], fresh_keys[take_rows], old_keys)
        put_values = jnp.where(written[:, None], fresh_values[take_rows], old_values)
        return (attended, put_keys, put_values)
    attended, put_keys, put_values = lax.map(per_request, jnp.arange(REQS, dtype=jnp.int32))
    attended = attended.reshape(TOKENS, HEADS * HEAD_DIM)
    update = jnp.dot(attended, out_weight, preferred_element_type=jnp.float32).astype(jnp.bfloat16)
    return (update, put_keys.reshape(REQS * WIN, kv_width).T, put_values.reshape(REQS * WIN, kv_width).T)
```

```python
import math

import numpy as np
import jax
import jax.numpy as jnp
from jax import lax
from jax.sharding import Mesh, PartitionSpec as P

HEAD_DIM = 80
WIN = 4096
GROUP_BITS = 2
GROUP = 4


EPSILON = 1e-05
ROPE_BASE = 10000.0
LOWEST = -1e30


def from_partner(block, axis, bit):
    count = lax.psum(1, axis)
    route = []
    for low in range(count):
        high = low | 1 << bit
        if high != low and high < count:
            route += [(low, high), (high, low)]
    return lax.ppermute(block, axis, route)


WIDE = ("z", "x", "c")


def gather_rows(block):
    rows = block.shape[0]
    plane = lax.all_gather(block, ("z", "x"), axis=0, tiled=False)
    both = lax.all_gather(plane, "c", axis=0, tiled=False)
    both = jnp.transpose(both, (1, 0, 2, 3))
    return both.reshape(-1, block.shape[1])


def rms_normed(rows_in, gain):
    values = rows_in.astype(jnp.float32)
    scaling = lax.rsqrt(jnp.mean(values * values, axis=-1, keepdims=True) + EPSILON)
    return (values * scaling * gain.astype(jnp.float32)).astype(jnp.bfloat16)


def rotate(values, positions):
    half_dim = values.shape[-1] // 2
    inverse = ROPE_BASE ** (-(jnp.arange(half_dim, dtype=jnp.float32) * (2.0 / values.shape[-1])))
    angles = positions.astype(jnp.float32)[:, None] * inverse[None, :]
    cos_part = jnp.cos(angles)[:, None, :]
    sin_part = jnp.sin(angles)[:, None, :]
    lower = values[..., :half_dim]
    higher = values[..., half_dim:]
    return jnp.concatenate(
        [lower * cos_part - higher * sin_part, higher * cos_part + lower * sin_part], axis=-1
    )


def ordered(mine, other, upper, along):
    first_half = jnp.where(upper, other, mine)
    second_half = jnp.where(upper, mine, other)
    return jnp.concatenate([first_half, second_half], axis=along)


def empty_state(row_count, groups, repeats):
    return (
        jnp.zeros((row_count, groups, repeats, HEAD_DIM), jnp.float32),
        jnp.full((row_count, groups, repeats), LOWEST, jnp.float32),
        jnp.zeros((row_count, groups, repeats), jnp.float32),
    )


def fold_keys(state, queries, query_pos, keys, values, key_pos, key_ok, widest):
    key_count = keys.shape[1]
    groups = queries.shape[1]
    block = math.gcd(key_count, widest)
    keys_split = keys.reshape(groups, HEAD_DIM, key_count)
    values_split = values.reshape(groups, HEAD_DIM, key_count)
    scale = HEAD_DIM ** (-0.5)

    def step(index, carry):
        accum, top_old, sum_old = carry
        start = index * block
        block_keys = lax.dynamic_slice_in_dim(keys_split, start, block, 2)
        block_values = lax.dynamic_slice_in_dim(values_split, start, block, 2)
        block_pos = lax.dynamic_slice_in_dim(key_pos, start, block, 0)
        block_ok = lax.dynamic_slice_in_dim(key_ok, start, block, 0)
        scores = (
            jnp.einsum("tgrd,gdk->tgrk", queries, block_keys, preferred_element_type=jnp.float32)
            * scale
        )
        allowed = (
            block_ok[None, :]
            & (block_pos[None, :] <= query_pos[:, None])
            & (query_pos[:, None] - block_pos[None, :] < WIN)
        )
        allowed = allowed[:, None, None, :]
        top_new = jnp.maximum(top_old, jnp.max(jnp.where(allowed, scores, LOWEST), axis=-1))
        weights = jnp.where(allowed, jnp.exp(scores - top_new[..., None]), 0.0)
        rescale = jnp.exp(top_old - top_new)
        sum_new = sum_old * rescale + jnp.sum(weights, axis=-1)
        mixed = jnp.einsum(
            "tgrk,gdk->tgrd",
            weights.astype(jnp.bfloat16),
            block_values,
            preferred_element_type=jnp.float32,
        )
        return (accum * rescale[..., None] + mixed, top_new, sum_new)

    return lax.fori_loop(0, key_count // block, step, state)


def shards(
    tokens_in,
    norm_gain,
    query_weight,
    key_weight,
    value_weight,
    out_weight,
    cache_keys,
    cache_values,
    cached_len,
    append_slot,
    shard_owner,
):
    whole = lax.all_gather(tokens_in, "narrow", axis=1, tiled=True)
    normed = rms_normed(whole, norm_gain)
    tok_rows = whole.shape[0]
    query_width = query_weight.shape[1]
    kv_width = key_weight.shape[1]
    local_heads = query_width // HEAD_DIM
    local_groups = kv_width // HEAD_DIM
    repeats = local_heads // local_groups
    columns = normed
    qkv = gather_rows(jnp.concatenate([query_weight, key_weight, value_weight], axis=1))
    qkv_sum = jnp.dot(columns, qkv, preferred_element_type=jnp.float32)
    query_sum = qkv_sum[:, :query_width]
    key_sum = qkv_sum[:, query_width : query_width + kv_width]
    value_sum = qkv_sum[:, query_width + kv_width :]
    position = lax.axis_index(WIDE)
    request = position // GROUP
    place = position % GROUP
    length = cached_len[request]
    offset = append_slot[request]
    owner = shard_owner[request]
    query_pos = length + place * tok_rows + jnp.arange(tok_rows, dtype=jnp.int32)
    queries = rotate(query_sum.reshape(tok_rows, local_heads, HEAD_DIM), query_pos).astype(
        jnp.bfloat16
    )
    queries = queries.reshape(tok_rows, local_groups, repeats, HEAD_DIM)
    new_keys = (
        rotate(key_sum.reshape(tok_rows, local_groups, HEAD_DIM), query_pos)
        .astype(jnp.bfloat16)
        .reshape(tok_rows, kv_width)
    )
    new_values = value_sum.astype(jnp.bfloat16)
    shard_rows = cache_keys.shape[1]
    within = jnp.arange(shard_rows, dtype=jnp.int32)
    cycle_mine = (place - owner) % GROUP * shard_rows + within
    old_keys, old_values = (cache_keys, cache_values)
    for bit in range(GROUP_BITS):
        upper = place // 2**bit % 2 == 1
        other_keys, other_values, other_old_keys, other_old_values = from_partner(
            (new_keys, new_values, old_keys, old_values), WIDE, bit
        )
        new_keys = ordered(new_keys, other_keys, upper, 0)
        new_values = ordered(new_values, other_values, upper, 0)
        old_keys = ordered(old_keys, other_old_keys, upper, 1)
        old_values = ordered(old_values, other_old_values, upper, 1)
    slot_index = jnp.arange(old_keys.shape[1], dtype=jnp.int32)
    cycle = (slot_index // shard_rows - owner) % GROUP * shard_rows + slot_index % shard_rows
    cached_pos = (cycle - offset + length) % WIN
    state = fold_keys(
        empty_state(tok_rows, local_groups, repeats),
        queries,
        query_pos,
        old_keys,
        old_values,
        cached_pos,
        cached_pos < length,
        512,
    )
    key_cols = new_keys.T
    value_cols = new_values.T
    new_count = key_cols.shape[1]
    new_pos = length + jnp.arange(new_count, dtype=jnp.int32)
    state = fold_keys(
        state,
        queries,
        query_pos,
        key_cols,
        value_cols,
        new_pos,
        jnp.ones((new_count,), dtype=bool),
        512,
    )
    accum, top_score, total = state
    attended = (accum / total[..., None]).astype(jnp.bfloat16).reshape(tok_rows, query_width)
    all_heads = lax.all_gather(attended, "narrow", axis=1, tiled=True)
    columns = all_heads
    update = jnp.dot(
        columns,
        gather_rows(out_weight),
        preferred_element_type=jnp.float32,
    ).astype(jnp.bfloat16)
    new_index = (cycle_mine - offset) % WIN
    written = new_index < new_count
    take_rows = jnp.minimum(new_index, new_count - 1)
    put_keys = jnp.where(written[None, :], jnp.take(key_cols, take_rows, axis=1), cache_keys)
    put_values = jnp.where(written[None, :], jnp.take(value_cols, take_rows, axis=1), cache_values)
    return (update, put_keys, put_values)


def solution(mesh):
    devices = mesh.devices
    wide_devices = devices[:, 0]
    xs = sorted({d.coords[0] for d in wide_devices})
    cores = sorted({getattr(d, "core_on_chip", 0) for d in wide_devices})
    n_x, n_c = len(xs), len(cores)
    n_z = devices.shape[0] // (n_x * n_c)
    fine = Mesh(devices.reshape(n_z, n_x, n_c, devices.shape[1]), ("z", "x", "c", "narrow"))
    rows = P(WIDE, "narrow")
    cols = P("narrow", WIDE)
    in_specs = (rows, P(), rows, rows, rows, rows, cols, cols, P(), P(), P())
    out_specs = (rows, cols, cols)
    return jax.shard_map(shards, mesh=fine, in_specs=in_specs, out_specs=out_specs, check_vma=False)
```

```python
import functools
import math

import numpy as np
import jax
import jax.numpy as jnp
from jax import lax
from jax.experimental import pallas as pl
from jax.experimental.pallas import tpu as pltpu
from jax.sharding import Mesh, PartitionSpec as P

MESH_ID = pl.DeviceIdType.MESH

HEAD_DIM = 80
WIN = 4096
GROUP_BITS = 2
GROUP = 4


EPSILON = 1e-05
ROPE_BASE = 10000.0
LOWEST = -1e30


def from_partner(block, axis, bit):
    count = lax.psum(1, axis)
    route = []
    for low in range(count):
        high = low | 1 << bit
        if high != low and high < count:
            route += [(low, high), (high, low)]
    return lax.ppermute(block, axis, route)


WIDE = ("z", "x", "c")


def gather_kernel(nz, nx, nc, blk_ref, out_ref, plane_send, plane_recv, ring_send, ring_recv, die_send, die_recv, local_sem):
    z = lax.axis_index("z")
    x = lax.axis_index("x")
    c = lax.axis_index("c")
    n = lax.axis_index("narrow")
    per_plane = nx * nc
    me_xc = x * nc + c
    me = z * per_plane + me_xc
    half = nz // 2
    step_dir = 1 - 2 * c
    dst_z = lax.rem(z + step_dir + nz, nz)
    src_z = lax.rem(z - step_dir + nz, nz)
    partner = (z, x, 1 - c, n)

    def plane_slot(pz):
        return out_ref.at[pl.ds(pl.multiple_of(pz * per_plane, per_plane), per_plane)]

    barrier = pltpu.get_barrier_semaphore()
    for k in range(1, per_plane):
        peer = lax.rem(me_xc + k, per_plane)
        pl.semaphore_signal(barrier, inc=1, device_id=(z, peer // nc, lax.rem(peer, nc), n), device_id_type=MESH_ID)
    for zz in (dst_z, src_z):
        pl.semaphore_signal(barrier, inc=1, device_id=(zz, x, c, n), device_id_type=MESH_ID)
    pl.semaphore_wait(barrier, per_plane + 1)

    local = pltpu.make_async_copy(blk_ref, out_ref.at[me], local_sem)
    local.start()
    sends = []
    for k in range(1, per_plane):
        peer = lax.rem(me_xc + k, per_plane)
        cp = pltpu.make_async_remote_copy(
            src_ref=blk_ref, dst_ref=out_ref.at[me],
            send_sem=plane_send.at[k], recv_sem=plane_recv.at[k],
            device_id=(z, peer // nc, lax.rem(peer, nc), n), device_id_type=MESH_ID)
        cp.start()
        sends.append(cp)
    for k in range(1, per_plane):
        sender = lax.rem(me_xc - k + per_plane, per_plane)
        pltpu.make_async_remote_copy(
            src_ref=blk_ref, dst_ref=out_ref.at[z * per_plane + sender],
            send_sem=plane_send.at[k], recv_sem=plane_recv.at[k],
            device_id=(z, x, c, n), device_id_type=MESH_ID).wait_recv()
    local.wait()

    for s in range(1, half + 1):
        send_z = lax.rem(z - step_dir * (s - 1) + 2 * nz, nz)
        cp = pltpu.make_async_remote_copy(
            src_ref=plane_slot(send_z), dst_ref=plane_slot(send_z),
            send_sem=ring_send.at[s - 1], recv_sem=ring_recv.at[s - 1],
            device_id=(dst_z, x, c, n), device_id_type=MESH_ID)
        cp.start()
        sends.append(cp)
        recv_z = lax.rem(z - step_dir * s + 2 * nz, nz)
        pltpu.make_async_remote_copy(
            src_ref=plane_slot(recv_z), dst_ref=plane_slot(recv_z),
            send_sem=ring_send.at[s - 1], recv_sem=ring_recv.at[s - 1],
            device_id=(src_z, x, c, n), device_id_type=MESH_ID).wait_recv()
        if s < half:
            dp = pltpu.make_async_remote_copy(
                src_ref=plane_slot(recv_z), dst_ref=plane_slot(recv_z),
                send_sem=die_send.at[s - 1], recv_sem=die_recv.at[s - 1],
                device_id=partner, device_id_type=MESH_ID)
            dp.start()
            sends.append(dp)
    for s in range(1, half):
        other_z = lax.rem(z + step_dir * s + 2 * nz, nz)
        pltpu.make_async_remote_copy(
            src_ref=plane_slot(other_z), dst_ref=plane_slot(other_z),
            send_sem=die_send.at[s - 1], recv_sem=die_recv.at[s - 1],
            device_id=partner, device_id_type=MESH_ID).wait_recv()
    for cp in sends:
        cp.wait_send()


def gather_wide(block, nz, nx, nc):
    count = nz * nx * nc
    half = nz // 2
    per_plane = nx * nc
    nbytes = block.size * block.dtype.itemsize
    return pl.pallas_call(
        functools.partial(gather_kernel, nz, nx, nc),
        out_shape=jax.ShapeDtypeStruct((count,) + block.shape, block.dtype),
        in_specs=[pl.BlockSpec(memory_space=pl.ANY)],
        out_specs=pl.BlockSpec(memory_space=pl.ANY),
        scratch_shapes=[
            pltpu.SemaphoreType.DMA((per_plane,)),
            pltpu.SemaphoreType.DMA((per_plane,)),
            pltpu.SemaphoreType.DMA((half,)),
            pltpu.SemaphoreType.DMA((half,)),
            pltpu.SemaphoreType.DMA((half,)),
            pltpu.SemaphoreType.DMA((half,)),
            pltpu.SemaphoreType.DMA(()),
        ],
        compiler_params=pltpu.CompilerParams(collective_id=0, has_side_effects=True),
        cost_estimate=pl.CostEstimate(flops=0, transcendentals=0, bytes_accessed=2 * count * nbytes),
    )(block)


def gather_rows(block):
    rows = block.shape[0]
    plane = lax.all_gather(block, ("z", "x"), axis=0, tiled=False)
    both = lax.all_gather(plane, "c", axis=0, tiled=False)
    both = jnp.transpose(both, (1, 0, 2, 3))
    return both.reshape(-1, block.shape[1])


def rms_normed(rows_in, gain):
    values = rows_in.astype(jnp.float32)
    scaling = lax.rsqrt(jnp.mean(values * values, axis=-1, keepdims=True) + EPSILON)
    return (values * scaling * gain.astype(jnp.float32)).astype(jnp.bfloat16)


def rotate(values, positions):
    half_dim = values.shape[-1] // 2
    inverse = ROPE_BASE ** (-(jnp.arange(half_dim, dtype=jnp.float32) * (2.0 / values.shape[-1])))
    angles = positions.astype(jnp.float32)[:, None] * inverse[None, :]
    cos_part = jnp.cos(angles)[:, None, :]
    sin_part = jnp.sin(angles)[:, None, :]
    lower = values[..., :half_dim]
    higher = values[..., half_dim:]
    return jnp.concatenate(
        [lower * cos_part - higher * sin_part, higher * cos_part + lower * sin_part], axis=-1
    )


def ordered(mine, other, upper, along):
    first_half = jnp.where(upper, other, mine)
    second_half = jnp.where(upper, mine, other)
    return jnp.concatenate([first_half, second_half], axis=along)


def empty_state(row_count, groups, repeats):
    return (
        jnp.zeros((row_count, groups, repeats, HEAD_DIM), jnp.float32),
        jnp.full((row_count, groups, repeats), LOWEST, jnp.float32),
        jnp.zeros((row_count, groups, repeats), jnp.float32),
    )


def fold_keys(state, queries, query_pos, keys, values, key_pos, key_ok, widest):
    key_count = keys.shape[1]
    groups = queries.shape[1]
    block = math.gcd(key_count, widest)
    keys_split = keys.reshape(groups, HEAD_DIM, key_count)
    values_split = values.reshape(groups, HEAD_DIM, key_count)
    scale = HEAD_DIM ** (-0.5)

    def step(index, carry):
        accum, top_old, sum_old = carry
        start = index * block
        block_keys = lax.dynamic_slice_in_dim(keys_split, start, block, 2)
        block_values = lax.dynamic_slice_in_dim(values_split, start, block, 2)
        block_pos = lax.dynamic_slice_in_dim(key_pos, start, block, 0)
        block_ok = lax.dynamic_slice_in_dim(key_ok, start, block, 0)
        scores = (
            jnp.einsum("tgrd,gdk->tgrk", queries, block_keys, preferred_element_type=jnp.float32)
            * scale
        )
        allowed = (
            block_ok[None, :]
            & (block_pos[None, :] <= query_pos[:, None])
            & (query_pos[:, None] - block_pos[None, :] < WIN)
        )
        allowed = allowed[:, None, None, :]
        top_new = jnp.maximum(top_old, jnp.max(jnp.where(allowed, scores, LOWEST), axis=-1))
        weights = jnp.where(allowed, jnp.exp(scores - top_new[..., None]), 0.0)
        rescale = jnp.exp(top_old - top_new)
        sum_new = sum_old * rescale + jnp.sum(weights, axis=-1)
        mixed = jnp.einsum(
            "tgrk,gdk->tgrd",
            weights.astype(jnp.bfloat16),
            block_values,
            preferred_element_type=jnp.float32,
        )
        return (accum * rescale[..., None] + mixed, top_new, sum_new)

    return lax.fori_loop(0, key_count // block, step, state)


def shards(
    tokens_in,
    norm_gain,
    query_weight,
    key_weight,
    value_weight,
    out_weight,
    cache_keys,
    cache_values,
    cached_len,
    append_slot,
    shard_owner,
):
    whole = lax.all_gather(tokens_in, "narrow", axis=1, tiled=True)
    normed = rms_normed(whole, norm_gain)
    tok_rows = whole.shape[0]
    query_width = query_weight.shape[1]
    kv_width = key_weight.shape[1]
    local_heads = query_width // HEAD_DIM
    local_groups = kv_width // HEAD_DIM
    repeats = local_heads // local_groups
    columns = normed
    sizes = (query_weight.shape[1], key_weight.shape[1], value_weight.shape[1], out_weight.shape[1])
    joined = jnp.concatenate([query_weight, key_weight, value_weight, out_weight], axis=1)
    block_rows, joined_width = joined.shape
    dims = (lax.psum(1, "z"), lax.psum(1, "x"), lax.psum(1, "c"))
    gathered = gather_wide(joined.reshape(-1, 128), *dims)
    all_weights = gathered.reshape(-1, joined_width)
    qkv = all_weights[:, : sum(sizes[:3])]
    out_rows = all_weights[:, sum(sizes[:3]) :]
    qkv_sum = jnp.dot(columns, qkv, preferred_element_type=jnp.float32)
    query_sum = qkv_sum[:, :query_width]
    key_sum = qkv_sum[:, query_width : query_width + kv_width]
    value_sum = qkv_sum[:, query_width + kv_width :]
    position = lax.axis_index(WIDE)
    request = position // GROUP
    place = position % GROUP
    length = cached_len[request]
    offset = append_slot[request]
    owner = shard_owner[request]
    query_pos = length + place * tok_rows + jnp.arange(tok_rows, dtype=jnp.int32)
    queries = rotate(query_sum.reshape(tok_rows, local_heads, HEAD_DIM), query_pos).astype(
        jnp.bfloat16
    )
    queries = queries.reshape(tok_rows, local_groups, repeats, HEAD_DIM)
    new_keys = (
        rotate(key_sum.reshape(tok_rows, local_groups, HEAD_DIM), query_pos)
        .astype(jnp.bfloat16)
        .reshape(tok_rows, kv_width)
    )
    new_values = value_sum.astype(jnp.bfloat16)
    shard_rows = cache_keys.shape[1]
    within = jnp.arange(shard_rows, dtype=jnp.int32)
    cycle_mine = (place - owner) % GROUP * shard_rows + within
    old_keys, old_values = (cache_keys, cache_values)
    for bit in range(GROUP_BITS):
        upper = place // 2**bit % 2 == 1
        other_keys, other_values, other_old_keys, other_old_values = from_partner(
            (new_keys, new_values, old_keys, old_values), WIDE, bit
        )
        new_keys = ordered(new_keys, other_keys, upper, 0)
        new_values = ordered(new_values, other_values, upper, 0)
        old_keys = ordered(old_keys, other_old_keys, upper, 1)
        old_values = ordered(old_values, other_old_values, upper, 1)
    slot_index = jnp.arange(old_keys.shape[1], dtype=jnp.int32)
    cycle = (slot_index // shard_rows - owner) % GROUP * shard_rows + slot_index % shard_rows
    cached_pos = (cycle - offset + length) % WIN
    state = fold_keys(
        empty_state(tok_rows, local_groups, repeats),
        queries,
        query_pos,
        old_keys,
        old_values,
        cached_pos,
        cached_pos < length,
        512,
    )
    key_cols = new_keys.T
    value_cols = new_values.T
    new_count = key_cols.shape[1]
    new_pos = length + jnp.arange(new_count, dtype=jnp.int32)
    state = fold_keys(
        state,
        queries,
        query_pos,
        key_cols,
        value_cols,
        new_pos,
        jnp.ones((new_count,), dtype=bool),
        512,
    )
    accum, top_score, total = state
    attended = (accum / total[..., None]).astype(jnp.bfloat16).reshape(tok_rows, query_width)
    all_heads = lax.all_gather(attended, "narrow", axis=1, tiled=True)
    columns = all_heads
    update = jnp.dot(
        columns,
        out_rows,
        preferred_element_type=jnp.float32,
    ).astype(jnp.bfloat16)
    new_index = (cycle_mine - offset) % WIN
    written = new_index < new_count
    take_rows = jnp.minimum(new_index, new_count - 1)
    put_keys = jnp.where(written[None, :], jnp.take(key_cols, take_rows, axis=1), cache_keys)
    put_values = jnp.where(written[None, :], jnp.take(value_cols, take_rows, axis=1), cache_values)
    return (update, put_keys, put_values)


def solution(mesh):
    devices = mesh.devices
    wide_devices = devices[:, 0]
    xs = sorted({d.coords[0] for d in wide_devices})
    cores = sorted({getattr(d, "core_on_chip", 0) for d in wide_devices})
    n_x, n_c = len(xs), len(cores)
    n_z = devices.shape[0] // (n_x * n_c)
    fine = Mesh(devices.reshape(n_z, n_x, n_c, devices.shape[1]), ("z", "x", "c", "narrow"))
    rows = P(WIDE, "narrow")
    cols = P("narrow", WIDE)
    in_specs = (rows, P(), rows, rows, rows, rows, cols, cols, P(), P(), P())
    out_specs = (rows, cols, cols)
    return jax.shard_map(shards, mesh=fine, in_specs=in_specs, out_specs=out_specs, check_vma=False)
```

```python
import functools
import math

import numpy as np
import jax
import jax.numpy as jnp
from jax import lax
from jax.experimental import pallas as pl
from jax.experimental.pallas import tpu as pltpu
from jax.sharding import Mesh, PartitionSpec as P

MESH_ID = pl.DeviceIdType.MESH

HEAD_DIM = 80
WIN = 4096
GROUP_BITS = 2
GROUP = 4


EPSILON = 1e-05
ROPE_BASE = 10000.0
LOWEST = -1e30


def from_partner(block, axis, bit):
    count = lax.psum(1, axis)
    route = []
    for low in range(count):
        high = low | 1 << bit
        if high != low and high < count:
            route += [(low, high), (high, low)]
    return lax.ppermute(block, axis, route)


WIDE = ("z", "x", "c")


def gather_kernel(nz, nx, nc, nn, blk_ref, cache_ref, tok_ref, out_ref, cache_out, tok_out,
                  plane_send, plane_recv, ring_send, ring_recv, die_send, die_recv, local_sem,
                  cache_send, cache_recv, tok_send, tok_recv):
    z = lax.axis_index("z")
    x = lax.axis_index("x")
    c = lax.axis_index("c")
    n = lax.axis_index("narrow")
    per_plane = nx * nc
    me_xc = x * nc + c
    me = z * per_plane + me_xc
    place = lax.rem(x, 2) * nc + c
    x_base = x - lax.rem(x, 2)
    half = nz // 2
    step_dir = 1 - 2 * c
    dst_z = lax.rem(z + step_dir + nz, nz)
    src_z = lax.rem(z - step_dir + nz, nz)
    partner = (z, x, 1 - c, n)

    def plane_slot(pz):
        return out_ref.at[pl.ds(pl.multiple_of(pz * per_plane, per_plane), per_plane)]

    def group_dev(p):
        return (z, x_base + p // nc, lax.rem(p, nc), n)

    barrier = pltpu.get_barrier_semaphore()
    for k in range(1, per_plane):
        peer = lax.rem(me_xc + k, per_plane)
        pl.semaphore_signal(barrier, inc=1, device_id=(z, peer // nc, lax.rem(peer, nc), n), device_id_type=MESH_ID)
    for zz in (dst_z, src_z):
        pl.semaphore_signal(barrier, inc=1, device_id=(zz, x, c, n), device_id_type=MESH_ID)
    for k in range(1, nn):
        pl.semaphore_signal(barrier, inc=1, device_id=(z, x, c, lax.rem(n + k, nn)), device_id_type=MESH_ID)
    pl.semaphore_wait(barrier, per_plane + 1 + nn - 1)

    sends = []
    locals_ = []
    for src, dst in ((blk_ref, out_ref.at[me]), (cache_ref, cache_out.at[place]), (tok_ref, tok_out.at[n])):
        cp = pltpu.make_async_copy(src, dst, local_sem.at[len(locals_)])
        cp.start()
        locals_.append(cp)
    for k in range(1, per_plane):
        peer = lax.rem(me_xc + k, per_plane)
        cp = pltpu.make_async_remote_copy(
            src_ref=blk_ref, dst_ref=out_ref.at[me],
            send_sem=plane_send.at[k], recv_sem=plane_recv.at[k],
            device_id=(z, peer // nc, lax.rem(peer, nc), n), device_id_type=MESH_ID)
        cp.start()
        sends.append(cp)
    for k in range(1, 2 * nc):
        cp = pltpu.make_async_remote_copy(
            src_ref=cache_ref, dst_ref=cache_out.at[place],
            send_sem=cache_send.at[k], recv_sem=cache_recv.at[k],
            device_id=group_dev(place ^ k), device_id_type=MESH_ID)
        cp.start()
        sends.append(cp)
    for k in range(1, nn):
        cp = pltpu.make_async_remote_copy(
            src_ref=tok_ref, dst_ref=tok_out.at[n],
            send_sem=tok_send.at[k], recv_sem=tok_recv.at[k],
            device_id=(z, x, c, lax.rem(n + k, nn)), device_id_type=MESH_ID)
        cp.start()
        sends.append(cp)
    for k in range(1, per_plane):
        sender = lax.rem(me_xc - k + per_plane, per_plane)
        pltpu.make_async_remote_copy(
            src_ref=blk_ref, dst_ref=out_ref.at[z * per_plane + sender],
            send_sem=plane_send.at[k], recv_sem=plane_recv.at[k],
            device_id=(z, x, c, n), device_id_type=MESH_ID).wait_recv()
    locals_[0].wait()

    for s in range(1, half + 1):
        send_z = lax.rem(z - step_dir * (s - 1) + 2 * nz, nz)
        cp = pltpu.make_async_remote_copy(
            src_ref=plane_slot(send_z), dst_ref=plane_slot(send_z),
            send_sem=ring_send.at[s - 1], recv_sem=ring_recv.at[s - 1],
            device_id=(dst_z, x, c, n), device_id_type=MESH_ID)
        cp.start()
        sends.append(cp)
        recv_z = lax.rem(z - step_dir * s + 2 * nz, nz)
        pltpu.make_async_remote_copy(
            src_ref=plane_slot(recv_z), dst_ref=plane_slot(recv_z),
            send_sem=ring_send.at[s - 1], recv_sem=ring_recv.at[s - 1],
            device_id=(src_z, x, c, n), device_id_type=MESH_ID).wait_recv()
        if s < half:
            dp = pltpu.make_async_remote_copy(
                src_ref=plane_slot(recv_z), dst_ref=plane_slot(recv_z),
                send_sem=die_send.at[s - 1], recv_sem=die_recv.at[s - 1],
                device_id=partner, device_id_type=MESH_ID)
            dp.start()
            sends.append(dp)
    for s in range(1, half):
        other_z = lax.rem(z + step_dir * s + 2 * nz, nz)
        pltpu.make_async_remote_copy(
            src_ref=plane_slot(other_z), dst_ref=plane_slot(other_z),
            send_sem=die_send.at[s - 1], recv_sem=die_recv.at[s - 1],
            device_id=partner, device_id_type=MESH_ID).wait_recv()
    for k in range(1, 2 * nc):
        pltpu.make_async_remote_copy(
            src_ref=cache_ref, dst_ref=cache_out.at[place ^ k],
            send_sem=cache_send.at[k], recv_sem=cache_recv.at[k],
            device_id=(z, x, c, n), device_id_type=MESH_ID).wait_recv()
    for k in range(1, nn):
        pltpu.make_async_remote_copy(
            src_ref=tok_ref, dst_ref=tok_out.at[lax.rem(n - k + nn, nn)],
            send_sem=tok_send.at[k], recv_sem=tok_recv.at[k],
            device_id=(z, x, c, n), device_id_type=MESH_ID).wait_recv()
    for cp in locals_[1:]:
        cp.wait()
    for cp in sends:
        cp.wait_send()


def gather_wide(block, cache, tokens, nz, nx, nc, nn):
    count = nz * nx * nc
    half = nz // 2
    per_plane = nx * nc
    group = 2 * nc
    nbytes = block.size * block.dtype.itemsize
    return pl.pallas_call(
        functools.partial(gather_kernel, nz, nx, nc, nn),
        out_shape=(
            jax.ShapeDtypeStruct((count,) + block.shape, block.dtype),
            jax.ShapeDtypeStruct((group,) + cache.shape, cache.dtype),
            jax.ShapeDtypeStruct((nn,) + tokens.shape, tokens.dtype),
        ),
        in_specs=[pl.BlockSpec(memory_space=pl.ANY)] * 3,
        out_specs=[pl.BlockSpec(memory_space=pl.ANY)] * 3,
        scratch_shapes=[
            pltpu.SemaphoreType.DMA((per_plane,)),
            pltpu.SemaphoreType.DMA((per_plane,)),
            pltpu.SemaphoreType.DMA((half,)),
            pltpu.SemaphoreType.DMA((half,)),
            pltpu.SemaphoreType.DMA((half,)),
            pltpu.SemaphoreType.DMA((half,)),
            pltpu.SemaphoreType.DMA((3,)),
            pltpu.SemaphoreType.DMA((group,)),
            pltpu.SemaphoreType.DMA((group,)),
            pltpu.SemaphoreType.DMA((nn,)),
            pltpu.SemaphoreType.DMA((nn,)),
        ],
        compiler_params=pltpu.CompilerParams(collective_id=0, has_side_effects=True),
        cost_estimate=pl.CostEstimate(flops=0, transcendentals=0, bytes_accessed=2 * count * nbytes),
    )(block, cache, tokens)


def gather_rows(block):
    rows = block.shape[0]
    plane = lax.all_gather(block, ("z", "x"), axis=0, tiled=False)
    both = lax.all_gather(plane, "c", axis=0, tiled=False)
    both = jnp.transpose(both, (1, 0, 2, 3))
    return both.reshape(-1, block.shape[1])


def rms_normed(rows_in, gain):
    values = rows_in.astype(jnp.float32)
    scaling = lax.rsqrt(jnp.mean(values * values, axis=-1, keepdims=True) + EPSILON)
    return (values * scaling * gain.astype(jnp.float32)).astype(jnp.bfloat16)


def rotate(values, positions):
    half_dim = values.shape[-1] // 2
    inverse = ROPE_BASE ** (-(jnp.arange(half_dim, dtype=jnp.float32) * (2.0 / values.shape[-1])))
    angles = positions.astype(jnp.float32)[:, None] * inverse[None, :]
    cos_part = jnp.cos(angles)[:, None, :]
    sin_part = jnp.sin(angles)[:, None, :]
    lower = values[..., :half_dim]
    higher = values[..., half_dim:]
    return jnp.concatenate(
        [lower * cos_part - higher * sin_part, higher * cos_part + lower * sin_part], axis=-1
    )


def ordered(mine, other, upper, along):
    first_half = jnp.where(upper, other, mine)
    second_half = jnp.where(upper, mine, other)
    return jnp.concatenate([first_half, second_half], axis=along)


def empty_state(row_count, groups, repeats):
    return (
        jnp.zeros((row_count, groups, repeats, HEAD_DIM), jnp.float32),
        jnp.full((row_count, groups, repeats), LOWEST, jnp.float32),
        jnp.zeros((row_count, groups, repeats), jnp.float32),
    )


def fold_keys(state, queries, query_pos, keys, values, key_pos, key_ok, widest):
    key_count = keys.shape[1]
    groups = queries.shape[1]
    block = math.gcd(key_count, widest)
    keys_split = keys.reshape(groups, HEAD_DIM, key_count)
    values_split = values.reshape(groups, HEAD_DIM, key_count)
    scale = HEAD_DIM ** (-0.5)

    def step(index, carry):
        accum, top_old, sum_old = carry
        start = index * block
        block_keys = lax.dynamic_slice_in_dim(keys_split, start, block, 2)
        block_values = lax.dynamic_slice_in_dim(values_split, start, block, 2)
        block_pos = lax.dynamic_slice_in_dim(key_pos, start, block, 0)
        block_ok = lax.dynamic_slice_in_dim(key_ok, start, block, 0)
        scores = (
            jnp.einsum("tgrd,gdk->tgrk", queries, block_keys, preferred_element_type=jnp.float32)
            * scale
        )
        allowed = (
            block_ok[None, :]
            & (block_pos[None, :] <= query_pos[:, None])
            & (query_pos[:, None] - block_pos[None, :] < WIN)
        )
        allowed = allowed[:, None, None, :]
        top_new = jnp.maximum(top_old, jnp.max(jnp.where(allowed, scores, LOWEST), axis=-1))
        weights = jnp.where(allowed, jnp.exp(scores - top_new[..., None]), 0.0)
        rescale = jnp.exp(top_old - top_new)
        sum_new = sum_old * rescale + jnp.sum(weights, axis=-1)
        mixed = jnp.einsum(
            "tgrk,gdk->tgrd",
            weights.astype(jnp.bfloat16),
            block_values,
            preferred_element_type=jnp.float32,
        )
        return (accum * rescale[..., None] + mixed, top_new, sum_new)

    return lax.fori_loop(0, key_count // block, step, state)


def exchange(block, axis, count, pairing):
    pieces = [block]
    for k in range(1, count):
        route = [(src, pairing(src, k)) for src in range(count)]
        route = [(dst, src) for src, dst in route]
        pieces.append(lax.ppermute(block, axis, [(pairing(d, k), d) for d in range(count)]))
    return jnp.stack(pieces)


def in_member_order(stacked, me, pairing, along):
    count = stacked.shape[0]
    parts = [stacked[pairing(me, q)] for q in range(count)]
    return jnp.concatenate(parts, axis=along)


def shift_pair(me, k):
    return (me - k) % 4


def xor_pair(me, k):
    return me ^ k


def shards(
    tokens_in,
    norm_gain,
    query_weight,
    key_weight,
    value_weight,
    out_weight,
    cache_keys,
    cache_values,
    cached_len,
    append_slot,
    shard_owner,
):
    n_narrow = lax.psum(1, "narrow")
    me_narrow = lax.axis_index("narrow")
    position = lax.axis_index(WIDE)
    request = position // GROUP
    place = position % GROUP

    def narrow_pair(me, k):
        return (me - k) % n_narrow

    def narrow_src(me, q):
        return (me - q) % n_narrow


    def group_pair(d, k):
        return d ^ k

    def group_route_pieces(block):
        pieces = [block]
        for k in range(1, GROUP):
            route = [(src, src ^ k) for src in range(lax.psum(1, WIDE))]
            pieces.append(lax.ppermute(block, WIDE, route))
        return jnp.stack(pieces)


    sizes = (query_weight.shape[1], key_weight.shape[1], value_weight.shape[1], out_weight.shape[1])
    joined = jnp.concatenate([query_weight, key_weight, value_weight, out_weight], axis=1)
    block_rows, joined_width = joined.shape
    dims = (lax.psum(1, "z"), lax.psum(1, "x"), lax.psum(1, "c"))
    gathered, cache_blocks, tok_pieces = gather_wide(
        joined.reshape(-1, 128), jnp.concatenate([cache_keys, cache_values], axis=0), tokens_in,
        *dims, n_narrow)
    whole = jnp.concatenate([tok_pieces[q] for q in range(n_narrow)], axis=1)
    all_weights = gathered.reshape(-1, joined_width)
    qkv = all_weights[:, : sum(sizes[:3])]
    out_rows = all_weights[:, sum(sizes[:3]) :]

    normed = rms_normed(whole, norm_gain)
    tok_rows = whole.shape[0]
    query_width = query_weight.shape[1]
    kv_width = key_weight.shape[1]
    local_heads = query_width // HEAD_DIM
    local_groups = kv_width // HEAD_DIM
    repeats = local_heads // local_groups
    qkv_sum = jnp.dot(normed, qkv, preferred_element_type=jnp.float32)
    query_sum = qkv_sum[:, :query_width]
    key_sum = qkv_sum[:, query_width : query_width + kv_width]
    value_sum = qkv_sum[:, query_width + kv_width :]
    length = cached_len[request]
    offset = append_slot[request]
    owner = shard_owner[request]
    query_pos = length + place * tok_rows + jnp.arange(tok_rows, dtype=jnp.int32)
    queries = rotate(query_sum.reshape(tok_rows, local_heads, HEAD_DIM), query_pos).astype(
        jnp.bfloat16
    )
    queries = queries.reshape(tok_rows, local_groups, repeats, HEAD_DIM)
    new_keys = (
        rotate(key_sum.reshape(tok_rows, local_groups, HEAD_DIM), query_pos)
        .astype(jnp.bfloat16)
        .reshape(tok_rows, kv_width)
    )
    new_values = value_sum.astype(jnp.bfloat16)
    shard_rows = cache_keys.shape[1]

    old_both = jnp.concatenate([cache_blocks[q] for q in range(GROUP)], axis=1)
    old_keys = old_both[:kv_width]
    old_values = old_both[kv_width:]
    new_both = jnp.concatenate([new_keys, new_values], axis=1)
    new_both = in_member_order(group_route_pieces(new_both), place, lambda me, q: me ^ q, 0)
    new_keys = new_both[:, :kv_width]
    new_values = new_both[:, kv_width:]

    slot_index = jnp.arange(old_keys.shape[1], dtype=jnp.int32)
    cycle = (slot_index // shard_rows - owner) % GROUP * shard_rows + slot_index % shard_rows
    cached_pos = (cycle - offset + length) % WIN
    state = fold_keys(
        empty_state(tok_rows, local_groups, repeats),
        queries,
        query_pos,
        old_keys,
        old_values,
        cached_pos,
        cached_pos < length,
        512,
    )
    key_cols = new_keys.T
    value_cols = new_values.T
    new_count = key_cols.shape[1]
    new_pos = length + jnp.arange(new_count, dtype=jnp.int32)
    state = fold_keys(
        state,
        queries,
        query_pos,
        key_cols,
        value_cols,
        new_pos,
        jnp.ones((new_count,), dtype=bool),
        512,
    )
    accum, top_score, total = state
    attended = (accum / total[..., None]).astype(jnp.bfloat16).reshape(tok_rows, query_width)
    head_pieces = exchange(attended, "narrow", n_narrow, lambda d, k: (d - k) % n_narrow)
    all_heads = in_member_order(head_pieces, me_narrow, lambda me, q: (me - q) % n_narrow, 1)
    update = jnp.dot(all_heads, out_rows, preferred_element_type=jnp.float32).astype(jnp.bfloat16)

    first = ((place - owner) % GROUP * shard_rows - offset) % WIN
    keys_ext = jnp.concatenate(
        [key_cols, jnp.zeros((kv_width, WIN - new_count), key_cols.dtype), key_cols,
         jnp.zeros((kv_width, shard_rows - new_count), key_cols.dtype)], axis=1)
    values_ext = jnp.concatenate(
        [value_cols, jnp.zeros((kv_width, WIN - new_count), value_cols.dtype), value_cols,
         jnp.zeros((kv_width, shard_rows - new_count), value_cols.dtype)], axis=1)
    spot = (first + jnp.arange(shard_rows, dtype=jnp.int32)) % WIN
    written = spot < new_count
    put_keys = jnp.where(written[None, :], lax.dynamic_slice_in_dim(keys_ext, first, shard_rows, 1), cache_keys)
    put_values = jnp.where(written[None, :], lax.dynamic_slice_in_dim(values_ext, first, shard_rows, 1), cache_values)
    return (update, put_keys, put_values)


def solution(mesh):
    devices = mesh.devices
    wide_devices = devices[:, 0]
    xs = sorted({d.coords[0] for d in wide_devices})
    cores = sorted({getattr(d, "core_on_chip", 0) for d in wide_devices})
    n_x, n_c = len(xs), len(cores)
    n_z = devices.shape[0] // (n_x * n_c)
    fine = Mesh(devices.reshape(n_z, n_x, n_c, devices.shape[1]), ("z", "x", "c", "narrow"))
    rows = P(WIDE, "narrow")
    cols = P("narrow", WIDE)
    in_specs = (rows, P(), rows, rows, rows, rows, cols, cols, P(), P(), P())
    out_specs = (rows, cols, cols)
    return jax.shard_map(shards, mesh=fine, in_specs=in_specs, out_specs=out_specs, check_vma=False)
```

```python
import functools
import math

import numpy as np
import jax
import jax.numpy as jnp
from jax import lax
from jax.experimental import pallas as pl
from jax.experimental.pallas import tpu as pltpu
from jax.sharding import Mesh, PartitionSpec as P

MESH_ID = pl.DeviceIdType.MESH

HEAD_DIM = 80
WIN = 4096
GROUP_BITS = 2
GROUP = 4


EPSILON = 1e-05
ROPE_BASE = 10000.0
LOWEST = -1e30


def from_partner(block, axis, bit):
    count = lax.psum(1, axis)
    route = []
    for low in range(count):
        high = low | 1 << bit
        if high != low and high < count:
            route += [(low, high), (high, low)]
    return lax.ppermute(block, axis, route)


WIDE = ("z", "x", "c")


def gather_kernel(nz, nx, nc, nn, blk_ref, cache_ref, tok_ref, out_ref, cache_out, tok_out,
                  plane_send, plane_recv, ring_send, ring_recv, die_send, die_recv, local_sem,
                  cache_send, cache_recv, tok_send, tok_recv):
    z = lax.axis_index("z")
    x = lax.axis_index("x")
    c = lax.axis_index("c")
    n = lax.axis_index("narrow")
    per_plane = nx * nc
    me_xc = x * nc + c
    me = z * per_plane + me_xc
    place = lax.rem(x, 2) * nc + c
    x_base = x - lax.rem(x, 2)
    half = nz // 2
    step_dir = 1 - 2 * c
    dst_z = lax.rem(z + step_dir + nz, nz)
    src_z = lax.rem(z - step_dir + nz, nz)
    partner = (z, x, 1 - c, n)

    def plane_slot(pz):
        return out_ref.at[pl.ds(pl.multiple_of(pz * per_plane, per_plane), per_plane)]

    def group_dev(p):
        return (z, x_base + p // nc, lax.rem(p, nc), n)

    barrier = pltpu.get_barrier_semaphore()
    for k in range(1, per_plane):
        peer = lax.rem(me_xc + k, per_plane)
        pl.semaphore_signal(barrier, inc=1, device_id=(z, peer // nc, lax.rem(peer, nc), n), device_id_type=MESH_ID)
    for zz in (dst_z, src_z):
        pl.semaphore_signal(barrier, inc=1, device_id=(zz, x, c, n), device_id_type=MESH_ID)
    for k in range(1, nn):
        pl.semaphore_signal(barrier, inc=1, device_id=(z, x, c, lax.rem(n + k, nn)), device_id_type=MESH_ID)
    pl.semaphore_wait(barrier, per_plane + 1 + nn - 1)

    sends = []
    locals_ = []
    for src, dst in ((blk_ref, out_ref.at[me]), (cache_ref, cache_out.at[place]), (tok_ref, tok_out.at[n])):
        cp = pltpu.make_async_copy(src, dst, local_sem.at[len(locals_)])
        cp.start()
        locals_.append(cp)
    for k in range(1, per_plane):
        peer = lax.rem(me_xc + k, per_plane)
        cp = pltpu.make_async_remote_copy(
            src_ref=blk_ref, dst_ref=out_ref.at[me],
            send_sem=plane_send.at[k], recv_sem=plane_recv.at[k],
            device_id=(z, peer // nc, lax.rem(peer, nc), n), device_id_type=MESH_ID)
        cp.start()
        sends.append(cp)
    for k in range(1, per_plane):
        sender = lax.rem(me_xc - k + per_plane, per_plane)
        pltpu.make_async_remote_copy(
            src_ref=blk_ref, dst_ref=out_ref.at[z * per_plane + sender],
            send_sem=plane_send.at[k], recv_sem=plane_recv.at[k],
            device_id=(z, x, c, n), device_id_type=MESH_ID).wait_recv()
    locals_[0].wait()
    for k in range(1, 2 * nc):
        cp = pltpu.make_async_remote_copy(
            src_ref=cache_ref, dst_ref=cache_out.at[place],
            send_sem=cache_send.at[k], recv_sem=cache_recv.at[k],
            device_id=group_dev(place ^ k), device_id_type=MESH_ID)
        cp.start()
        sends.append(cp)
    for k in range(1, nn):
        cp = pltpu.make_async_remote_copy(
            src_ref=tok_ref, dst_ref=tok_out.at[n],
            send_sem=tok_send.at[k], recv_sem=tok_recv.at[k],
            device_id=(z, x, c, lax.rem(n + k, nn)), device_id_type=MESH_ID)
        cp.start()
        sends.append(cp)

    for s in range(1, half + 1):
        send_z = lax.rem(z - step_dir * (s - 1) + 2 * nz, nz)
        cp = pltpu.make_async_remote_copy(
            src_ref=plane_slot(send_z), dst_ref=plane_slot(send_z),
            send_sem=ring_send.at[s - 1], recv_sem=ring_recv.at[s - 1],
            device_id=(dst_z, x, c, n), device_id_type=MESH_ID)
        cp.start()
        sends.append(cp)
        recv_z = lax.rem(z - step_dir * s + 2 * nz, nz)
        pltpu.make_async_remote_copy(
            src_ref=plane_slot(recv_z), dst_ref=plane_slot(recv_z),
            send_sem=ring_send.at[s - 1], recv_sem=ring_recv.at[s - 1],
            device_id=(src_z, x, c, n), device_id_type=MESH_ID).wait_recv()
        if s < half:
            dp = pltpu.make_async_remote_copy(
                src_ref=plane_slot(recv_z), dst_ref=plane_slot(recv_z),
                send_sem=die_send.at[s - 1], recv_sem=die_recv.at[s - 1],
                device_id=partner, device_id_type=MESH_ID)
            dp.start()
            sends.append(dp)
    for s in range(1, half):
        other_z = lax.rem(z + step_dir * s + 2 * nz, nz)
        pltpu.make_async_remote_copy(
            src_ref=plane_slot(other_z), dst_ref=plane_slot(other_z),
            send_sem=die_send.at[s - 1], recv_sem=die_recv.at[s - 1],
            device_id=partner, device_id_type=MESH_ID).wait_recv()
    for k in range(1, 2 * nc):
        pltpu.make_async_remote_copy(
            src_ref=cache_ref, dst_ref=cache_out.at[place ^ k],
            send_sem=cache_send.at[k], recv_sem=cache_recv.at[k],
            device_id=(z, x, c, n), device_id_type=MESH_ID).wait_recv()
    for k in range(1, nn):
        pltpu.make_async_remote_copy(
            src_ref=tok_ref, dst_ref=tok_out.at[lax.rem(n - k + nn, nn)],
            send_sem=tok_send.at[k], recv_sem=tok_recv.at[k],
            device_id=(z, x, c, n), device_id_type=MESH_ID).wait_recv()
    for cp in locals_[1:]:
        cp.wait()
    for cp in sends:
        cp.wait_send()


def swap_kernel(kind, count, src_ref, out_ref, send_sem, recv_sem, local_sem):
    z = lax.axis_index("z")
    x = lax.axis_index("x")
    c = lax.axis_index("c")
    n = lax.axis_index("narrow")
    if kind == "narrow":
        me = n

        def device(k):
            return (z, x, c, lax.rem(n + k, count))

        def sender(k):
            return lax.rem(n - k + count, count)
    else:
        me = lax.rem(x, 2) * 2 + c
        x_base = x - lax.rem(x, 2)

        def device(k):
            p = me ^ k
            return (z, x_base + p // 2, lax.rem(p, 2), n)

        def sender(k):
            return me ^ k

    barrier = pltpu.get_barrier_semaphore()
    for k in range(1, count):
        pl.semaphore_signal(barrier, inc=1, device_id=device(k), device_id_type=MESH_ID)
    pl.semaphore_wait(barrier, count - 1)
    local = pltpu.make_async_copy(src_ref, out_ref.at[me], local_sem)
    local.start()
    sends = []
    for k in range(1, count):
        cp = pltpu.make_async_remote_copy(
            src_ref=src_ref, dst_ref=out_ref.at[me],
            send_sem=send_sem.at[k], recv_sem=recv_sem.at[k],
            device_id=device(k), device_id_type=MESH_ID)
        cp.start()
        sends.append(cp)
    for k in range(1, count):
        pltpu.make_async_remote_copy(
            src_ref=src_ref, dst_ref=out_ref.at[sender(k)],
            send_sem=send_sem.at[k], recv_sem=recv_sem.at[k],
            device_id=(z, x, c, n), device_id_type=MESH_ID).wait_recv()
    local.wait()
    for cp in sends:
        cp.wait_send()


def swap(block, kind, count, ident):
    return pl.pallas_call(
        functools.partial(swap_kernel, kind, count),
        out_shape=jax.ShapeDtypeStruct((count,) + block.shape, block.dtype),
        in_specs=[pl.BlockSpec(memory_space=pltpu.VMEM)],
        out_specs=pl.BlockSpec(memory_space=pltpu.VMEM),
        scratch_shapes=[
            pltpu.SemaphoreType.DMA((count,)),
            pltpu.SemaphoreType.DMA((count,)),
            pltpu.SemaphoreType.DMA(()),
        ],
        compiler_params=pltpu.CompilerParams(collective_id=ident, has_side_effects=True),
    )(block)


def gather_wide(block, cache, tokens, nz, nx, nc, nn):
    count = nz * nx * nc
    half = nz // 2
    per_plane = nx * nc
    group = 2 * nc
    nbytes = block.size * block.dtype.itemsize
    return pl.pallas_call(
        functools.partial(gather_kernel, nz, nx, nc, nn),
        out_shape=(
            jax.ShapeDtypeStruct((count,) + block.shape, block.dtype),
            jax.ShapeDtypeStruct((group,) + cache.shape, cache.dtype),
            jax.ShapeDtypeStruct((nn,) + tokens.shape, tokens.dtype),
        ),
        in_specs=[pl.BlockSpec(memory_space=pl.ANY)] * 3,
        out_specs=[pl.BlockSpec(memory_space=pl.ANY)] * 3,
        scratch_shapes=[
            pltpu.SemaphoreType.DMA((per_plane,)),
            pltpu.SemaphoreType.DMA((per_plane,)),
            pltpu.SemaphoreType.DMA((half,)),
            pltpu.SemaphoreType.DMA((half,)),
            pltpu.SemaphoreType.DMA((half,)),
            pltpu.SemaphoreType.DMA((half,)),
            pltpu.SemaphoreType.DMA((3,)),
            pltpu.SemaphoreType.DMA((group,)),
            pltpu.SemaphoreType.DMA((group,)),
            pltpu.SemaphoreType.DMA((nn,)),
            pltpu.SemaphoreType.DMA((nn,)),
        ],
        compiler_params=pltpu.CompilerParams(collective_id=0, has_side_effects=True),
        cost_estimate=pl.CostEstimate(flops=0, transcendentals=0, bytes_accessed=2 * count * nbytes),
    )(block, cache, tokens)


def gather_rows(block):
    rows = block.shape[0]
    plane = lax.all_gather(block, ("z", "x"), axis=0, tiled=False)
    both = lax.all_gather(plane, "c", axis=0, tiled=False)
    both = jnp.transpose(both, (1, 0, 2, 3))
    return both.reshape(-1, block.shape[1])


def rms_normed(rows_in, gain):
    values = rows_in.astype(jnp.float32)
    scaling = lax.rsqrt(jnp.mean(values * values, axis=-1, keepdims=True) + EPSILON)
    return (values * scaling * gain.astype(jnp.float32)).astype(jnp.bfloat16)


def rotate(values, positions):
    half_dim = values.shape[-1] // 2
    inverse = ROPE_BASE ** (-(jnp.arange(half_dim, dtype=jnp.float32) * (2.0 / values.shape[-1])))
    angles = positions.astype(jnp.float32)[:, None] * inverse[None, :]
    cos_part = jnp.cos(angles)[:, None, :]
    sin_part = jnp.sin(angles)[:, None, :]
    lower = values[..., :half_dim]
    higher = values[..., half_dim:]
    return jnp.concatenate(
        [lower * cos_part - higher * sin_part, higher * cos_part + lower * sin_part], axis=-1
    )


def ordered(mine, other, upper, along):
    first_half = jnp.where(upper, other, mine)
    second_half = jnp.where(upper, mine, other)
    return jnp.concatenate([first_half, second_half], axis=along)


def empty_state(row_count, groups, repeats):
    return (
        jnp.zeros((row_count, groups, repeats, HEAD_DIM), jnp.float32),
        jnp.full((row_count, groups, repeats), LOWEST, jnp.float32),
        jnp.zeros((row_count, groups, repeats), jnp.float32),
    )


def fold_keys(state, queries, query_pos, keys, values, key_pos, key_ok, widest):
    key_count = keys.shape[1]
    groups = queries.shape[1]
    block = math.gcd(key_count, widest)
    keys_split = keys.reshape(groups, HEAD_DIM, key_count)
    values_split = values.reshape(groups, HEAD_DIM, key_count)
    scale = HEAD_DIM ** (-0.5)

    def step(index, carry):
        accum, top_old, sum_old = carry
        start = index * block
        block_keys = lax.dynamic_slice_in_dim(keys_split, start, block, 2)
        block_values = lax.dynamic_slice_in_dim(values_split, start, block, 2)
        block_pos = lax.dynamic_slice_in_dim(key_pos, start, block, 0)
        block_ok = lax.dynamic_slice_in_dim(key_ok, start, block, 0)
        scores = (
            jnp.einsum("tgrd,gdk->tgrk", queries, block_keys, preferred_element_type=jnp.float32)
            * scale
        )
        allowed = (
            block_ok[None, :]
            & (block_pos[None, :] <= query_pos[:, None])
            & (query_pos[:, None] - block_pos[None, :] < WIN)
        )
        allowed = allowed[:, None, None, :]
        top_new = jnp.maximum(top_old, jnp.max(jnp.where(allowed, scores, LOWEST), axis=-1))
        weights = jnp.where(allowed, jnp.exp(scores - top_new[..., None]), 0.0)
        rescale = jnp.exp(top_old - top_new)
        sum_new = sum_old * rescale + jnp.sum(weights, axis=-1)
        mixed = jnp.einsum(
            "tgrk,gdk->tgrd",
            weights.astype(jnp.bfloat16),
            block_values,
            preferred_element_type=jnp.float32,
        )
        return (accum * rescale[..., None] + mixed, top_new, sum_new)

    return lax.fori_loop(0, key_count // block, step, state)


def exchange(block, axis, count, pairing):
    pieces = [block]
    for k in range(1, count):
        route = [(src, pairing(src, k)) for src in range(count)]
        route = [(dst, src) for src, dst in route]
        pieces.append(lax.ppermute(block, axis, [(pairing(d, k), d) for d in range(count)]))
    return jnp.stack(pieces)


def in_member_order(stacked, me, pairing, along):
    count = stacked.shape[0]
    parts = [stacked[pairing(me, q)] for q in range(count)]
    return jnp.concatenate(parts, axis=along)


def shift_pair(me, k):
    return (me - k) % 4


def xor_pair(me, k):
    return me ^ k


def shards(
    tokens_in,
    norm_gain,
    query_weight,
    key_weight,
    value_weight,
    out_weight,
    cache_keys,
    cache_values,
    cached_len,
    append_slot,
    shard_owner,
):
    n_narrow = lax.psum(1, "narrow")
    me_narrow = lax.axis_index("narrow")
    position = lax.axis_index(WIDE)
    request = position // GROUP
    place = position % GROUP

    def narrow_pair(me, k):
        return (me - k) % n_narrow

    def narrow_src(me, q):
        return (me - q) % n_narrow


    def group_pair(d, k):
        return d ^ k

    def group_route_pieces(block):
        pieces = [block]
        for k in range(1, GROUP):
            route = [(src, src ^ k) for src in range(lax.psum(1, WIDE))]
            pieces.append(lax.ppermute(block, WIDE, route))
        return jnp.stack(pieces)


    sizes = (query_weight.shape[1], key_weight.shape[1], value_weight.shape[1], out_weight.shape[1])
    joined = jnp.concatenate([query_weight, key_weight, value_weight, out_weight], axis=1)
    block_rows, joined_width = joined.shape
    dims = (lax.psum(1, "z"), lax.psum(1, "x"), lax.psum(1, "c"))
    gathered, cache_blocks, tok_pieces = gather_wide(
        joined.reshape(-1, 128), jnp.concatenate([cache_keys, cache_values], axis=0), tokens_in,
        *dims, n_narrow)
    whole = jnp.concatenate([tok_pieces[q] for q in range(n_narrow)], axis=1)
    all_weights = gathered.reshape(-1, joined_width)
    qkv = all_weights[:, : sum(sizes[:3])]
    out_rows = all_weights[:, sum(sizes[:3]) :]

    normed = rms_normed(whole, norm_gain)
    tok_rows = whole.shape[0]
    query_width = query_weight.shape[1]
    kv_width = key_weight.shape[1]
    local_heads = query_width // HEAD_DIM
    local_groups = kv_width // HEAD_DIM
    repeats = local_heads // local_groups
    qkv_sum = jnp.dot(normed, qkv, preferred_element_type=jnp.float32)
    query_sum = qkv_sum[:, :query_width]
    key_sum = qkv_sum[:, query_width : query_width + kv_width]
    value_sum = qkv_sum[:, query_width + kv_width :]
    length = cached_len[request]
    offset = append_slot[request]
    owner = shard_owner[request]
    query_pos = length + place * tok_rows + jnp.arange(tok_rows, dtype=jnp.int32)
    queries = rotate(query_sum.reshape(tok_rows, local_heads, HEAD_DIM), query_pos).astype(
        jnp.bfloat16
    )
    queries = queries.reshape(tok_rows, local_groups, repeats, HEAD_DIM)
    new_keys = (
        rotate(key_sum.reshape(tok_rows, local_groups, HEAD_DIM), query_pos)
        .astype(jnp.bfloat16)
        .reshape(tok_rows, kv_width)
    )
    new_values = value_sum.astype(jnp.bfloat16)
    shard_rows = cache_keys.shape[1]

    old_both = jnp.concatenate([cache_blocks[q] for q in range(GROUP)], axis=1)
    old_keys = old_both[:kv_width]
    old_values = old_both[kv_width:]
    new_both = jnp.concatenate([new_keys, new_values], axis=1)
    new_pieces = swap(new_both, "group", GROUP, 2)
    new_both = jnp.concatenate([new_pieces[q] for q in range(GROUP)], axis=0)
    new_keys = new_both[:, :kv_width]
    new_values = new_both[:, kv_width:]

    slot_index = jnp.arange(old_keys.shape[1], dtype=jnp.int32)
    cycle = (slot_index // shard_rows - owner) % GROUP * shard_rows + slot_index % shard_rows
    cached_pos = (cycle - offset + length) % WIN
    state = fold_keys(
        empty_state(tok_rows, local_groups, repeats),
        queries,
        query_pos,
        old_keys,
        old_values,
        cached_pos,
        cached_pos < length,
        512,
    )
    key_cols = new_keys.T
    value_cols = new_values.T
    new_count = key_cols.shape[1]
    new_pos = length + jnp.arange(new_count, dtype=jnp.int32)
    state = fold_keys(
        state,
        queries,
        query_pos,
        key_cols,
        value_cols,
        new_pos,
        jnp.ones((new_count,), dtype=bool),
        512,
    )
    accum, top_score, total = state
    attended = (accum / total[..., None]).astype(jnp.bfloat16).reshape(tok_rows, query_width)
    head_pieces = swap(attended, "narrow", n_narrow, 1)
    all_heads = jnp.concatenate([head_pieces[q] for q in range(n_narrow)], axis=1)
    update = jnp.dot(all_heads, out_rows, preferred_element_type=jnp.float32).astype(jnp.bfloat16)

    first = ((place - owner) % GROUP * shard_rows - offset) % WIN
    keys_ext = jnp.concatenate(
        [key_cols, jnp.zeros((kv_width, WIN - new_count), key_cols.dtype), key_cols,
         jnp.zeros((kv_width, shard_rows - new_count), key_cols.dtype)], axis=1)
    values_ext = jnp.concatenate(
        [value_cols, jnp.zeros((kv_width, WIN - new_count), value_cols.dtype), value_cols,
         jnp.zeros((kv_width, shard_rows - new_count), value_cols.dtype)], axis=1)
    spot = (first + jnp.arange(shard_rows, dtype=jnp.int32)) % WIN
    written = spot < new_count
    put_keys = jnp.where(written[None, :], lax.dynamic_slice_in_dim(keys_ext, first, shard_rows, 1), cache_keys)
    put_values = jnp.where(written[None, :], lax.dynamic_slice_in_dim(values_ext, first, shard_rows, 1), cache_values)
    return (update, put_keys, put_values)


def solution(mesh):
    devices = mesh.devices
    wide_devices = devices[:, 0]
    xs = sorted({d.coords[0] for d in wide_devices})
    cores = sorted({getattr(d, "core_on_chip", 0) for d in wide_devices})
    n_x, n_c = len(xs), len(cores)
    n_z = devices.shape[0] // (n_x * n_c)
    fine = Mesh(devices.reshape(n_z, n_x, n_c, devices.shape[1]), ("z", "x", "c", "narrow"))
    rows = P(WIDE, "narrow")
    cols = P("narrow", WIDE)
    in_specs = (rows, P(), rows, rows, rows, rows, cols, cols, P(), P(), P())
    out_specs = (rows, cols, cols)
    return jax.shard_map(shards, mesh=fine, in_specs=in_specs, out_specs=out_specs, check_vma=False)
```

```python
import functools
import math

import numpy as np
import jax
import jax.numpy as jnp
from jax import lax
from jax.experimental import pallas as pl
from jax.experimental.pallas import tpu as pltpu
from jax.sharding import Mesh, PartitionSpec as P

MESH_ID = pl.DeviceIdType.MESH

HEAD_DIM = 80
WIN = 4096
GROUP_BITS = 2
GROUP = 4


EPSILON = 1e-05
ROPE_BASE = 10000.0
LOWEST = -1e30


def from_partner(block, axis, bit):
    count = lax.psum(1, axis)
    route = []
    for low in range(count):
        high = low | 1 << bit
        if high != low and high < count:
            route += [(low, high), (high, low)]
    return lax.ppermute(block, axis, route)


WIDE = ("z", "x", "c")
RING_SUBS = 4


def gather_kernel(nz, nx, nc, nn, blk_ref, cache_ref, tok_ref, out_ref, cache_out, tok_out,
                  plane_send, plane_recv, ring_send, ring_recv, die_send, die_recv, local_sem,
                  cache_send, cache_recv, tok_send, tok_recv):
    z = lax.axis_index("z")
    x = lax.axis_index("x")
    c = lax.axis_index("c")
    n = lax.axis_index("narrow")
    per_plane = nx * nc
    me_xc = x * nc + c
    me = z * per_plane + me_xc
    place = lax.rem(x, 2) * nc + c
    x_base = x - lax.rem(x, 2)
    half = nz // 2
    step_dir = 1 - 2 * c
    dst_z = lax.rem(z + step_dir + nz, nz)
    src_z = lax.rem(z - step_dir + nz, nz)
    partner = (z, x, 1 - c, n)

    def plane_slot(pz):
        return out_ref.at[pl.ds(pl.multiple_of(pz * per_plane, per_plane), per_plane)]

    def group_dev(p):
        return (z, x_base + p // nc, lax.rem(p, nc), n)

    barrier = pltpu.get_barrier_semaphore()
    for k in range(1, per_plane):
        peer = lax.rem(me_xc + k, per_plane)
        pl.semaphore_signal(barrier, inc=1, device_id=(z, peer // nc, lax.rem(peer, nc), n), device_id_type=MESH_ID)
    for zz in (dst_z, src_z):
        pl.semaphore_signal(barrier, inc=1, device_id=(zz, x, c, n), device_id_type=MESH_ID)
    for k in range(1, nn):
        pl.semaphore_signal(barrier, inc=1, device_id=(z, x, c, lax.rem(n + k, nn)), device_id_type=MESH_ID)
    pl.semaphore_wait(barrier, per_plane + 1 + nn - 1)

    sends = []
    locals_ = []
    for src, dst in ((blk_ref, out_ref.at[me]), (cache_ref, cache_out.at[place]), (tok_ref, tok_out.at[n])):
        cp = pltpu.make_async_copy(src, dst, local_sem.at[len(locals_)])
        cp.start()
        locals_.append(cp)
    for k in range(1, per_plane):
        peer = lax.rem(me_xc + k, per_plane)
        cp = pltpu.make_async_remote_copy(
            src_ref=blk_ref, dst_ref=out_ref.at[me],
            send_sem=plane_send.at[k], recv_sem=plane_recv.at[k],
            device_id=(z, peer // nc, lax.rem(peer, nc), n), device_id_type=MESH_ID)
        cp.start()
        sends.append(cp)
    for k in range(1, per_plane):
        sender = lax.rem(me_xc - k + per_plane, per_plane)
        pltpu.make_async_remote_copy(
            src_ref=blk_ref, dst_ref=out_ref.at[z * per_plane + sender],
            send_sem=plane_send.at[k], recv_sem=plane_recv.at[k],
            device_id=(z, x, c, n), device_id_type=MESH_ID).wait_recv()
    locals_[0].wait()
    for k in range(1, 2 * nc):
        cp = pltpu.make_async_remote_copy(
            src_ref=cache_ref, dst_ref=cache_out.at[place],
            send_sem=cache_send.at[k], recv_sem=cache_recv.at[k],
            device_id=group_dev(place ^ k), device_id_type=MESH_ID)
        cp.start()
        sends.append(cp)
    for k in range(1, nn):
        cp = pltpu.make_async_remote_copy(
            src_ref=tok_ref, dst_ref=tok_out.at[n],
            send_sem=tok_send.at[k], recv_sem=tok_recv.at[k],
            device_id=(z, x, c, lax.rem(n + k, nn)), device_id_type=MESH_ID)
        cp.start()
        sends.append(cp)

    subs = RING_SUBS
    sub_len = per_plane // subs

    def sub_slot(pz, j):
        return out_ref.at[pl.ds(pl.multiple_of(pz * per_plane + j * sub_len, sub_len), sub_len)]

    def ring_copy(s, j, pz, device):
        return pltpu.make_async_remote_copy(
            src_ref=sub_slot(pz, j), dst_ref=sub_slot(pz, j),
            send_sem=ring_send.at[s - 1, j], recv_sem=ring_recv.at[s - 1, j],
            device_id=device, device_id_type=MESH_ID)

    def die_copy(s, j, pz):
        return pltpu.make_async_remote_copy(
            src_ref=sub_slot(pz, j), dst_ref=sub_slot(pz, j),
            send_sem=die_send.at[s - 1, j], recv_sem=die_recv.at[s - 1, j],
            device_id=partner, device_id_type=MESH_ID)

    for s in range(1, half + 1):
        send_z = lax.rem(z - step_dir * (s - 1) + 2 * nz, nz)
        for j in range(subs):
            if s > 1:
                ring_copy(s - 1, j, send_z, (src_z, x, c, n)).wait_recv()
                if s - 1 < half:
                    dp = die_copy(s - 1, j, send_z)
                    dp.start()
                    sends.append(dp)
            cp = ring_copy(s, j, send_z, (dst_z, x, c, n))
            cp.start()
            sends.append(cp)
    last_z = lax.rem(z - step_dir * half + 2 * nz, nz)
    for j in range(subs):
        ring_copy(half, j, last_z, (src_z, x, c, n)).wait_recv()
    for s in range(1, half):
        other_z = lax.rem(z + step_dir * s + 2 * nz, nz)
        for j in range(subs):
            die_copy(s, j, other_z).wait_recv()
    for k in range(1, 2 * nc):
        pltpu.make_async_remote_copy(
            src_ref=cache_ref, dst_ref=cache_out.at[place ^ k],
            send_sem=cache_send.at[k], recv_sem=cache_recv.at[k],
            device_id=(z, x, c, n), device_id_type=MESH_ID).wait_recv()
    for k in range(1, nn):
        pltpu.make_async_remote_copy(
            src_ref=tok_ref, dst_ref=tok_out.at[lax.rem(n - k + nn, nn)],
            send_sem=tok_send.at[k], recv_sem=tok_recv.at[k],
            device_id=(z, x, c, n), device_id_type=MESH_ID).wait_recv()
    for cp in locals_[1:]:
        cp.wait()
    for cp in sends:
        cp.wait_send()


def gather_wide(block, cache, tokens, nz, nx, nc, nn):
    count = nz * nx * nc
    half = nz // 2
    per_plane = nx * nc
    group = 2 * nc
    nbytes = block.size * block.dtype.itemsize
    return pl.pallas_call(
        functools.partial(gather_kernel, nz, nx, nc, nn),
        out_shape=(
            jax.ShapeDtypeStruct((count,) + block.shape, block.dtype),
            jax.ShapeDtypeStruct((group,) + cache.shape, cache.dtype),
            jax.ShapeDtypeStruct((nn,) + tokens.shape, tokens.dtype),
        ),
        in_specs=[pl.BlockSpec(memory_space=pl.ANY)] * 3,
        out_specs=[pl.BlockSpec(memory_space=pl.ANY)] * 3,
        scratch_shapes=[
            pltpu.SemaphoreType.DMA((per_plane,)),
            pltpu.SemaphoreType.DMA((per_plane,)),
            pltpu.SemaphoreType.DMA((half, RING_SUBS)),
            pltpu.SemaphoreType.DMA((half, RING_SUBS)),
            pltpu.SemaphoreType.DMA((half, RING_SUBS)),
            pltpu.SemaphoreType.DMA((half, RING_SUBS)),
            pltpu.SemaphoreType.DMA((3,)),
            pltpu.SemaphoreType.DMA((group,)),
            pltpu.SemaphoreType.DMA((group,)),
            pltpu.SemaphoreType.DMA((nn,)),
            pltpu.SemaphoreType.DMA((nn,)),
        ],
        compiler_params=pltpu.CompilerParams(collective_id=0, has_side_effects=True),
        cost_estimate=pl.CostEstimate(flops=0, transcendentals=0, bytes_accessed=2 * count * nbytes),
    )(block, cache, tokens)


def gather_rows(block):
    rows = block.shape[0]
    plane = lax.all_gather(block, ("z", "x"), axis=0, tiled=False)
    both = lax.all_gather(plane, "c", axis=0, tiled=False)
    both = jnp.transpose(both, (1, 0, 2, 3))
    return both.reshape(-1, block.shape[1])


def rms_normed(rows_in, gain):
    values = rows_in.astype(jnp.float32)
    scaling = lax.rsqrt(jnp.mean(values * values, axis=-1, keepdims=True) + EPSILON)
    return (values * scaling * gain.astype(jnp.float32)).astype(jnp.bfloat16)


def rotate(values, positions):
    half_dim = values.shape[-1] // 2
    inverse = ROPE_BASE ** (-(jnp.arange(half_dim, dtype=jnp.float32) * (2.0 / values.shape[-1])))
    angles = positions.astype(jnp.float32)[:, None] * inverse[None, :]
    cos_part = jnp.cos(angles)[:, None, :]
    sin_part = jnp.sin(angles)[:, None, :]
    lower = values[..., :half_dim]
    higher = values[..., half_dim:]
    return jnp.concatenate(
        [lower * cos_part - higher * sin_part, higher * cos_part + lower * sin_part], axis=-1
    )


def ordered(mine, other, upper, along):
    first_half = jnp.where(upper, other, mine)
    second_half = jnp.where(upper, mine, other)
    return jnp.concatenate([first_half, second_half], axis=along)


def empty_state(row_count, groups, repeats):
    return (
        jnp.zeros((row_count, groups, repeats, HEAD_DIM), jnp.float32),
        jnp.full((row_count, groups, repeats), LOWEST, jnp.float32),
        jnp.zeros((row_count, groups, repeats), jnp.float32),
    )


def fold_keys(state, queries, query_pos, keys, values, key_pos, key_ok, widest):
    key_count = keys.shape[1]
    groups = queries.shape[1]
    block = math.gcd(key_count, widest)
    keys_split = keys.reshape(groups, HEAD_DIM, key_count)
    values_split = values.reshape(groups, HEAD_DIM, key_count)
    scale = HEAD_DIM ** (-0.5)

    def step(index, carry):
        accum, top_old, sum_old = carry
        start = index * block
        block_keys = lax.dynamic_slice_in_dim(keys_split, start, block, 2)
        block_values = lax.dynamic_slice_in_dim(values_split, start, block, 2)
        block_pos = lax.dynamic_slice_in_dim(key_pos, start, block, 0)
        block_ok = lax.dynamic_slice_in_dim(key_ok, start, block, 0)
        scores = (
            jnp.einsum("tgrd,gdk->tgrk", queries, block_keys, preferred_element_type=jnp.float32)
            * scale
        )
        allowed = (
            block_ok[None, :]
            & (block_pos[None, :] <= query_pos[:, None])
            & (query_pos[:, None] - block_pos[None, :] < WIN)
        )
        allowed = allowed[:, None, None, :]
        top_new = jnp.maximum(top_old, jnp.max(jnp.where(allowed, scores, LOWEST), axis=-1))
        weights = jnp.where(allowed, jnp.exp(scores - top_new[..., None]), 0.0)
        rescale = jnp.exp(top_old - top_new)
        sum_new = sum_old * rescale + jnp.sum(weights, axis=-1)
        mixed = jnp.einsum(
            "tgrk,gdk->tgrd",
            weights.astype(jnp.bfloat16),
            block_values,
            preferred_element_type=jnp.float32,
        )
        return (accum * rescale[..., None] + mixed, top_new, sum_new)

    return lax.fori_loop(0, key_count // block, step, state)


def exchange(block, axis, count, pairing):
    pieces = [block]
    for k in range(1, count):
        route = [(src, pairing(src, k)) for src in range(count)]
        route = [(dst, src) for src, dst in route]
        pieces.append(lax.ppermute(block, axis, [(pairing(d, k), d) for d in range(count)]))
    return jnp.stack(pieces)


def in_member_order(stacked, me, pairing, along):
    count = stacked.shape[0]
    parts = [stacked[pairing(me, q)] for q in range(count)]
    return jnp.concatenate(parts, axis=along)


def shift_pair(me, k):
    return (me - k) % 4


def xor_pair(me, k):
    return me ^ k


def shards(
    tokens_in,
    norm_gain,
    query_weight,
    key_weight,
    value_weight,
    out_weight,
    cache_keys,
    cache_values,
    cached_len,
    append_slot,
    shard_owner,
):
    n_narrow = lax.psum(1, "narrow")
    me_narrow = lax.axis_index("narrow")
    position = lax.axis_index(WIDE)
    request = position // GROUP
    place = position % GROUP

    def narrow_pair(me, k):
        return (me - k) % n_narrow

    def narrow_src(me, q):
        return (me - q) % n_narrow


    def group_pair(d, k):
        return d ^ k

    def group_route_pieces(block):
        pieces = [block]
        for k in range(1, GROUP):
            route = [(src, src ^ k) for src in range(lax.psum(1, WIDE))]
            pieces.append(lax.ppermute(block, WIDE, route))
        return jnp.stack(pieces)


    sizes = (query_weight.shape[1], key_weight.shape[1], value_weight.shape[1], out_weight.shape[1])
    joined = jnp.concatenate([query_weight, key_weight, value_weight, out_weight], axis=1)
    block_rows, joined_width = joined.shape
    dims = (lax.psum(1, "z"), lax.psum(1, "x"), lax.psum(1, "c"))
    gathered, cache_blocks, tok_pieces = gather_wide(
        joined.reshape(-1, 128), jnp.concatenate([cache_keys, cache_values], axis=0), tokens_in,
        *dims, n_narrow)
    whole = jnp.concatenate([tok_pieces[q] for q in range(n_narrow)], axis=1)
    all_weights = gathered.reshape(-1, joined_width)
    qkv = all_weights[:, : sum(sizes[:3])]
    out_rows = all_weights[:, sum(sizes[:3]) :]

    normed = rms_normed(whole, norm_gain)
    tok_rows = whole.shape[0]
    query_width = query_weight.shape[1]
    kv_width = key_weight.shape[1]
    local_heads = query_width // HEAD_DIM
    local_groups = kv_width // HEAD_DIM
    repeats = local_heads // local_groups
    qkv_sum = jnp.dot(normed, qkv, preferred_element_type=jnp.float32)
    query_sum = qkv_sum[:, :query_width]
    key_sum = qkv_sum[:, query_width : query_width + kv_width]
    value_sum = qkv_sum[:, query_width + kv_width :]
    length = cached_len[request]
    offset = append_slot[request]
    owner = shard_owner[request]
    query_pos = length + place * tok_rows + jnp.arange(tok_rows, dtype=jnp.int32)
    queries = rotate(query_sum.reshape(tok_rows, local_heads, HEAD_DIM), query_pos).astype(
        jnp.bfloat16
    )
    queries = queries.reshape(tok_rows, local_groups, repeats, HEAD_DIM)
    new_keys = (
        rotate(key_sum.reshape(tok_rows, local_groups, HEAD_DIM), query_pos)
        .astype(jnp.bfloat16)
        .reshape(tok_rows, kv_width)
    )
    new_values = value_sum.astype(jnp.bfloat16)
    shard_rows = cache_keys.shape[1]

    old_both = jnp.concatenate([cache_blocks[q] for q in range(GROUP)], axis=1)
    old_keys = old_both[:kv_width]
    old_values = old_both[kv_width:]
    new_both = jnp.concatenate([new_keys, new_values], axis=1)
    new_both = in_member_order(group_route_pieces(new_both), place, lambda me, q: me ^ q, 0)
    new_keys = new_both[:, :kv_width]
    new_values = new_both[:, kv_width:]

    slot_index = jnp.arange(old_keys.shape[1], dtype=jnp.int32)
    cycle = (slot_index // shard_rows - owner) % GROUP * shard_rows + slot_index % shard_rows
    cached_pos = (cycle - offset + length) % WIN
    state = fold_keys(
        empty_state(tok_rows, local_groups, repeats),
        queries,
        query_pos,
        old_keys,
        old_values,
        cached_pos,
        cached_pos < length,
        512,
    )
    key_cols = new_keys.T
    value_cols = new_values.T
    new_count = key_cols.shape[1]
    new_pos = length + jnp.arange(new_count, dtype=jnp.int32)
    state = fold_keys(
        state,
        queries,
        query_pos,
        key_cols,
        value_cols,
        new_pos,
        jnp.ones((new_count,), dtype=bool),
        512,
    )
    accum, top_score, total = state
    attended = (accum / total[..., None]).astype(jnp.bfloat16).reshape(tok_rows, query_width)
    head_pieces = exchange(attended, "narrow", n_narrow, lambda d, k: (d - k) % n_narrow)
    all_heads = in_member_order(head_pieces, me_narrow, lambda me, q: (me - q) % n_narrow, 1)
    update = jnp.dot(all_heads, out_rows, preferred_element_type=jnp.float32).astype(jnp.bfloat16)

    first = ((place - owner) % GROUP * shard_rows - offset) % WIN
    keys_ext = jnp.concatenate(
        [key_cols, jnp.zeros((kv_width, WIN - new_count), key_cols.dtype), key_cols,
         jnp.zeros((kv_width, shard_rows - new_count), key_cols.dtype)], axis=1)
    values_ext = jnp.concatenate(
        [value_cols, jnp.zeros((kv_width, WIN - new_count), value_cols.dtype), value_cols,
         jnp.zeros((kv_width, shard_rows - new_count), value_cols.dtype)], axis=1)
    spot = (first + jnp.arange(shard_rows, dtype=jnp.int32)) % WIN
    written = spot < new_count
    put_keys = jnp.where(written[None, :], lax.dynamic_slice_in_dim(keys_ext, first, shard_rows, 1), cache_keys)
    put_values = jnp.where(written[None, :], lax.dynamic_slice_in_dim(values_ext, first, shard_rows, 1), cache_values)
    return (update, put_keys, put_values)


def solution(mesh):
    devices = mesh.devices
    wide_devices = devices[:, 0]
    xs = sorted({d.coords[0] for d in wide_devices})
    cores = sorted({getattr(d, "core_on_chip", 0) for d in wide_devices})
    n_x, n_c = len(xs), len(cores)
    n_z = devices.shape[0] // (n_x * n_c)
    fine = Mesh(devices.reshape(n_z, n_x, n_c, devices.shape[1]), ("z", "x", "c", "narrow"))
    rows = P(WIDE, "narrow")
    cols = P("narrow", WIDE)
    in_specs = (rows, P(), rows, rows, rows, rows, cols, cols, P(), P(), P())
    out_specs = (rows, cols, cols)
    return jax.shard_map(shards, mesh=fine, in_specs=in_specs, out_specs=out_specs, check_vma=False)
```

```python
import functools
import math

import numpy as np
import jax
import jax.numpy as jnp
from jax import lax
from jax.experimental import pallas as pl
from jax.experimental.pallas import tpu as pltpu
from jax.sharding import Mesh, PartitionSpec as P

MESH_ID = pl.DeviceIdType.MESH

HEAD_DIM = 80
WIN = 4096
GROUP_BITS = 2
GROUP = 4


EPSILON = 1e-05
ROPE_BASE = 10000.0
LOWEST = -1e30


def from_partner(block, axis, bit):
    count = lax.psum(1, axis)
    route = []
    for low in range(count):
        high = low | 1 << bit
        if high != low and high < count:
            route += [(low, high), (high, low)]
    return lax.ppermute(block, axis, route)


WIDE = ("z", "x", "c")
RING_SUBS = 8


def gather_kernel(nz, nx, nc, nn, blk_ref, cache_ref, tok_ref, out_ref, cache_out, tok_out,
                  plane_send, plane_recv, ring_send, ring_recv, die_send, die_recv, local_sem,
                  cache_send, cache_recv, tok_send, tok_recv):
    z = lax.axis_index("z")
    x = lax.axis_index("x")
    c = lax.axis_index("c")
    n = lax.axis_index("narrow")
    per_plane = nx * nc
    me_xc = x * nc + c
    me = z * per_plane + me_xc
    place = lax.rem(x, 2) * nc + c
    x_base = x - lax.rem(x, 2)
    half = nz // 2
    step_dir = 1 - 2 * c
    dst_z = lax.rem(z + step_dir + nz, nz)
    src_z = lax.rem(z - step_dir + nz, nz)
    partner = (z, x, 1 - c, n)

    def plane_slot(pz):
        return out_ref.at[pl.ds(pl.multiple_of(pz * per_plane, per_plane), per_plane)]

    def group_dev(p):
        return (z, x_base + p // nc, lax.rem(p, nc), n)

    barrier = pltpu.get_barrier_semaphore()
    for k in range(1, per_plane):
        peer = lax.rem(me_xc + k, per_plane)
        pl.semaphore_signal(barrier, inc=1, device_id=(z, peer // nc, lax.rem(peer, nc), n), device_id_type=MESH_ID)
    for zz in (dst_z, src_z):
        pl.semaphore_signal(barrier, inc=1, device_id=(zz, x, c, n), device_id_type=MESH_ID)
    for k in range(1, nn):
        pl.semaphore_signal(barrier, inc=1, device_id=(z, x, c, lax.rem(n + k, nn)), device_id_type=MESH_ID)
    pl.semaphore_wait(barrier, per_plane + 1 + nn - 1)

    sends = []
    locals_ = []
    for src, dst in ((blk_ref, out_ref.at[me]), (cache_ref, cache_out.at[place]), (tok_ref, tok_out.at[n])):
        cp = pltpu.make_async_copy(src, dst, local_sem.at[len(locals_)])
        cp.start()
        locals_.append(cp)
    for k in range(1, per_plane):
        peer = lax.rem(me_xc + k, per_plane)
        cp = pltpu.make_async_remote_copy(
            src_ref=blk_ref, dst_ref=out_ref.at[me],
            send_sem=plane_send.at[k], recv_sem=plane_recv.at[k],
            device_id=(z, peer // nc, lax.rem(peer, nc), n), device_id_type=MESH_ID)
        cp.start()
        sends.append(cp)
    for k in range(1, per_plane):
        sender = lax.rem(me_xc - k + per_plane, per_plane)
        pltpu.make_async_remote_copy(
            src_ref=blk_ref, dst_ref=out_ref.at[z * per_plane + sender],
            send_sem=plane_send.at[k], recv_sem=plane_recv.at[k],
            device_id=(z, x, c, n), device_id_type=MESH_ID).wait_recv()
    locals_[0].wait()
    for k in range(1, 2 * nc):
        cp = pltpu.make_async_remote_copy(
            src_ref=cache_ref, dst_ref=cache_out.at[place],
            send_sem=cache_send.at[k], recv_sem=cache_recv.at[k],
            device_id=group_dev(place ^ k), device_id_type=MESH_ID)
        cp.start()
        sends.append(cp)
    for k in range(1, nn):
        cp = pltpu.make_async_remote_copy(
            src_ref=tok_ref, dst_ref=tok_out.at[n],
            send_sem=tok_send.at[k], recv_sem=tok_recv.at[k],
            device_id=(z, x, c, lax.rem(n + k, nn)), device_id_type=MESH_ID)
        cp.start()
        sends.append(cp)

    subs = RING_SUBS
    sub_len = per_plane // subs

    def sub_slot(pz, j):
        return out_ref.at[pl.ds(pl.multiple_of(pz * per_plane + j * sub_len, sub_len), sub_len)]

    def ring_copy(s, j, pz, device):
        return pltpu.make_async_remote_copy(
            src_ref=sub_slot(pz, j), dst_ref=sub_slot(pz, j),
            send_sem=ring_send.at[s - 1, j], recv_sem=ring_recv.at[s - 1, j],
            device_id=device, device_id_type=MESH_ID)

    def die_copy(s, j, pz):
        return pltpu.make_async_remote_copy(
            src_ref=sub_slot(pz, j), dst_ref=sub_slot(pz, j),
            send_sem=die_send.at[s - 1, j], recv_sem=die_recv.at[s - 1, j],
            device_id=partner, device_id_type=MESH_ID)

    for s in range(1, half + 1):
        send_z = lax.rem(z - step_dir * (s - 1) + 2 * nz, nz)
        for j in range(subs):
            if s > 1:
                ring_copy(s - 1, j, send_z, (src_z, x, c, n)).wait_recv()
                if s - 1 < half:
                    dp = die_copy(s - 1, j, send_z)
                    dp.start()
                    sends.append(dp)
            cp = ring_copy(s, j, send_z, (dst_z, x, c, n))
            cp.start()
            sends.append(cp)
    last_z = lax.rem(z - step_dir * half + 2 * nz, nz)
    for j in range(subs):
        ring_copy(half, j, last_z, (src_z, x, c, n)).wait_recv()
    for s in range(1, half):
        other_z = lax.rem(z + step_dir * s + 2 * nz, nz)
        for j in range(subs):
            die_copy(s, j, other_z).wait_recv()
    for k in range(1, 2 * nc):
        pltpu.make_async_remote_copy(
            src_ref=cache_ref, dst_ref=cache_out.at[place ^ k],
            send_sem=cache_send.at[k], recv_sem=cache_recv.at[k],
            device_id=(z, x, c, n), device_id_type=MESH_ID).wait_recv()
    for k in range(1, nn):
        pltpu.make_async_remote_copy(
            src_ref=tok_ref, dst_ref=tok_out.at[lax.rem(n - k + nn, nn)],
            send_sem=tok_send.at[k], recv_sem=tok_recv.at[k],
            device_id=(z, x, c, n), device_id_type=MESH_ID).wait_recv()
    for cp in locals_[1:]:
        cp.wait()
    for cp in sends:
        cp.wait_send()


def gather_wide(block, cache, tokens, nz, nx, nc, nn):
    count = nz * nx * nc
    half = nz // 2
    per_plane = nx * nc
    group = 2 * nc
    nbytes = block.size * block.dtype.itemsize
    return pl.pallas_call(
        functools.partial(gather_kernel, nz, nx, nc, nn),
        out_shape=(
            jax.ShapeDtypeStruct((count,) + block.shape, block.dtype),
            jax.ShapeDtypeStruct((group,) + cache.shape, cache.dtype),
            jax.ShapeDtypeStruct((nn,) + tokens.shape, tokens.dtype),
        ),
        in_specs=[pl.BlockSpec(memory_space=pl.ANY)] * 3,
        out_specs=[pl.BlockSpec(memory_space=pl.ANY)] * 3,
        scratch_shapes=[
            pltpu.SemaphoreType.DMA((per_plane,)),
            pltpu.SemaphoreType.DMA((per_plane,)),
            pltpu.SemaphoreType.DMA((half, RING_SUBS)),
            pltpu.SemaphoreType.DMA((half, RING_SUBS)),
            pltpu.SemaphoreType.DMA((half, RING_SUBS)),
            pltpu.SemaphoreType.DMA((half, RING_SUBS)),
            pltpu.SemaphoreType.DMA((3,)),
            pltpu.SemaphoreType.DMA((group,)),
            pltpu.SemaphoreType.DMA((group,)),
            pltpu.SemaphoreType.DMA((nn,)),
            pltpu.SemaphoreType.DMA((nn,)),
        ],
        compiler_params=pltpu.CompilerParams(collective_id=0, has_side_effects=True),
        cost_estimate=pl.CostEstimate(flops=0, transcendentals=0, bytes_accessed=2 * count * nbytes),
    )(block, cache, tokens)


def gather_rows(block):
    rows = block.shape[0]
    plane = lax.all_gather(block, ("z", "x"), axis=0, tiled=False)
    both = lax.all_gather(plane, "c", axis=0, tiled=False)
    both = jnp.transpose(both, (1, 0, 2, 3))
    return both.reshape(-1, block.shape[1])


def rms_normed(rows_in, gain):
    values = rows_in.astype(jnp.float32)
    scaling = lax.rsqrt(jnp.mean(values * values, axis=-1, keepdims=True) + EPSILON)
    return (values * scaling * gain.astype(jnp.float32)).astype(jnp.bfloat16)


def rotate(values, positions):
    half_dim = values.shape[-1] // 2
    inverse = ROPE_BASE ** (-(jnp.arange(half_dim, dtype=jnp.float32) * (2.0 / values.shape[-1])))
    angles = positions.astype(jnp.float32)[:, None] * inverse[None, :]
    cos_part = jnp.cos(angles)[:, None, :]
    sin_part = jnp.sin(angles)[:, None, :]
    lower = values[..., :half_dim]
    higher = values[..., half_dim:]
    return jnp.concatenate(
        [lower * cos_part - higher * sin_part, higher * cos_part + lower * sin_part], axis=-1
    )


def ordered(mine, other, upper, along):
    first_half = jnp.where(upper, other, mine)
    second_half = jnp.where(upper, mine, other)
    return jnp.concatenate([first_half, second_half], axis=along)


def empty_state(row_count, groups, repeats):
    return (
        jnp.zeros((row_count, groups, repeats, HEAD_DIM), jnp.float32),
        jnp.full((row_count, groups, repeats), LOWEST, jnp.float32),
        jnp.zeros((row_count, groups, repeats), jnp.float32),
    )


def fold_keys(state, queries, query_pos, keys, values, key_pos, key_ok, widest):
    key_count = keys.shape[1]
    groups = queries.shape[1]
    block = math.gcd(key_count, widest)
    keys_split = keys.reshape(groups, HEAD_DIM, key_count)
    values_split = values.reshape(groups, HEAD_DIM, key_count)
    scale = HEAD_DIM ** (-0.5)

    def step(index, carry):
        accum, top_old, sum_old = carry
        start = index * block
        block_keys = lax.dynamic_slice_in_dim(keys_split, start, block, 2)
        block_values = lax.dynamic_slice_in_dim(values_split, start, block, 2)
        block_pos = lax.dynamic_slice_in_dim(key_pos, start, block, 0)
        block_ok = lax.dynamic_slice_in_dim(key_ok, start, block, 0)
        scores = (
            jnp.einsum("tgrd,gdk->tgrk", queries, block_keys, preferred_element_type=jnp.float32)
            * scale
        )
        allowed = (
            block_ok[None, :]
            & (block_pos[None, :] <= query_pos[:, None])
            & (query_pos[:, None] - block_pos[None, :] < WIN)
        )
        allowed = allowed[:, None, None, :]
        top_new = jnp.maximum(top_old, jnp.max(jnp.where(allowed, scores, LOWEST), axis=-1))
        weights = jnp.where(allowed, jnp.exp(scores - top_new[..., None]), 0.0)
        rescale = jnp.exp(top_old - top_new)
        sum_new = sum_old * rescale + jnp.sum(weights, axis=-1)
        mixed = jnp.einsum(
            "tgrk,gdk->tgrd",
            weights.astype(jnp.bfloat16),
            block_values,
            preferred_element_type=jnp.float32,
        )
        return (accum * rescale[..., None] + mixed, top_new, sum_new)

    return lax.fori_loop(0, key_count // block, step, state)


def exchange(block, axis, count, pairing):
    pieces = [block]
    for k in range(1, count):
        route = [(src, pairing(src, k)) for src in range(count)]
        route = [(dst, src) for src, dst in route]
        pieces.append(lax.ppermute(block, axis, [(pairing(d, k), d) for d in range(count)]))
    return jnp.stack(pieces)


def in_member_order(stacked, me, pairing, along):
    count = stacked.shape[0]
    parts = [stacked[pairing(me, q)] for q in range(count)]
    return jnp.concatenate(parts, axis=along)


def shift_pair(me, k):
    return (me - k) % 4


def xor_pair(me, k):
    return me ^ k


def shards(
    tokens_in,
    norm_gain,
    query_weight,
    key_weight,
    value_weight,
    out_weight,
    cache_keys,
    cache_values,
    cached_len,
    append_slot,
    shard_owner,
):
    n_narrow = lax.psum(1, "narrow")
    me_narrow = lax.axis_index("narrow")
    position = lax.axis_index(WIDE)
    request = position // GROUP
    place = position % GROUP

    def narrow_pair(me, k):
        return (me - k) % n_narrow

    def narrow_src(me, q):
        return (me - q) % n_narrow


    def group_pair(d, k):
        return d ^ k

    def group_route_pieces(block):
        pieces = [block]
        for k in range(1, GROUP):
            route = [(src, src ^ k) for src in range(lax.psum(1, WIDE))]
            pieces.append(lax.ppermute(block, WIDE, route))
        return jnp.stack(pieces)


    sizes = (query_weight.shape[1], key_weight.shape[1], value_weight.shape[1], out_weight.shape[1])
    joined = jnp.concatenate([query_weight, key_weight, value_weight, out_weight], axis=1)
    block_rows, joined_width = joined.shape
    dims = (lax.psum(1, "z"), lax.psum(1, "x"), lax.psum(1, "c"))
    gathered, cache_blocks, tok_pieces = gather_wide(
        joined.reshape(-1, 128), jnp.concatenate([cache_keys, cache_values], axis=0), tokens_in,
        *dims, n_narrow)
    whole = jnp.concatenate([tok_pieces[q] for q in range(n_narrow)], axis=1)
    all_weights = gathered.reshape(-1, joined_width)
    qkv = all_weights[:, : sum(sizes[:3])]
    out_rows = all_weights[:, sum(sizes[:3]) :]

    normed = rms_normed(whole, norm_gain)
    tok_rows = whole.shape[0]
    query_width = query_weight.shape[1]
    kv_width = key_weight.shape[1]
    local_heads = query_width // HEAD_DIM
    local_groups = kv_width // HEAD_DIM
    repeats = local_heads // local_groups
    qkv_sum = jnp.dot(normed, qkv, preferred_element_type=jnp.float32)
    query_sum = qkv_sum[:, :query_width]
    key_sum = qkv_sum[:, query_width : query_width + kv_width]
    value_sum = qkv_sum[:, query_width + kv_width :]
    length = cached_len[request]
    offset = append_slot[request]
    owner = shard_owner[request]
    query_pos = length + place * tok_rows + jnp.arange(tok_rows, dtype=jnp.int32)
    queries = rotate(query_sum.reshape(tok_rows, local_heads, HEAD_DIM), query_pos).astype(
        jnp.bfloat16
    )
    queries = queries.reshape(tok_rows, local_groups, repeats, HEAD_DIM)
    new_keys = (
        rotate(key_sum.reshape(tok_rows, local_groups, HEAD_DIM), query_pos)
        .astype(jnp.bfloat16)
        .reshape(tok_rows, kv_width)
    )
    new_values = value_sum.astype(jnp.bfloat16)
    shard_rows = cache_keys.shape[1]

    old_both = jnp.concatenate([cache_blocks[q] for q in range(GROUP)], axis=1)
    old_keys = old_both[:kv_width]
    old_values = old_both[kv_width:]
    new_both = jnp.concatenate([new_keys, new_values], axis=1)
    new_both = in_member_order(group_route_pieces(new_both), place, lambda me, q: me ^ q, 0)
    new_keys = new_both[:, :kv_width]
    new_values = new_both[:, kv_width:]

    slot_index = jnp.arange(old_keys.shape[1], dtype=jnp.int32)
    cycle = (slot_index // shard_rows - owner) % GROUP * shard_rows + slot_index % shard_rows
    cached_pos = (cycle - offset + length) % WIN
    state = fold_keys(
        empty_state(tok_rows, local_groups, repeats),
        queries,
        query_pos,
        old_keys,
        old_values,
        cached_pos,
        cached_pos < length,
        1024,
    )
    key_cols = new_keys.T
    value_cols = new_values.T
    new_count = key_cols.shape[1]
    new_pos = length + jnp.arange(new_count, dtype=jnp.int32)
    state = fold_keys(
        state,
        queries,
        query_pos,
        key_cols,
        value_cols,
        new_pos,
        jnp.ones((new_count,), dtype=bool),
        1024,
    )
    accum, top_score, total = state
    attended = (accum / total[..., None]).astype(jnp.bfloat16).reshape(tok_rows, query_width)
    head_pieces = exchange(attended, "narrow", n_narrow, lambda d, k: (d - k) % n_narrow)
    all_heads = in_member_order(head_pieces, me_narrow, lambda me, q: (me - q) % n_narrow, 1)
    update = jnp.dot(all_heads, out_rows, preferred_element_type=jnp.float32).astype(jnp.bfloat16)

    first = ((place - owner) % GROUP * shard_rows - offset) % WIN
    keys_ext = jnp.concatenate(
        [key_cols, jnp.zeros((kv_width, WIN - new_count), key_cols.dtype), key_cols,
         jnp.zeros((kv_width, shard_rows - new_count), key_cols.dtype)], axis=1)
    values_ext = jnp.concatenate(
        [value_cols, jnp.zeros((kv_width, WIN - new_count), value_cols.dtype), value_cols,
         jnp.zeros((kv_width, shard_rows - new_count), value_cols.dtype)], axis=1)
    spot = (first + jnp.arange(shard_rows, dtype=jnp.int32)) % WIN
    written = spot < new_count
    put_keys = jnp.where(written[None, :], lax.dynamic_slice_in_dim(keys_ext, first, shard_rows, 1), cache_keys)
    put_values = jnp.where(written[None, :], lax.dynamic_slice_in_dim(values_ext, first, shard_rows, 1), cache_values)
    return (update, put_keys, put_values)


def solution(mesh):
    devices = mesh.devices
    wide_devices = devices[:, 0]
    xs = sorted({d.coords[0] for d in wide_devices})
    cores = sorted({getattr(d, "core_on_chip", 0) for d in wide_devices})
    n_x, n_c = len(xs), len(cores)
    n_z = devices.shape[0] // (n_x * n_c)
    fine = Mesh(devices.reshape(n_z, n_x, n_c, devices.shape[1]), ("z", "x", "c", "narrow"))
    rows = P(WIDE, "narrow")
    cols = P("narrow", WIDE)
    in_specs = (rows, P(), rows, rows, rows, rows, cols, cols, P(), P(), P())
    out_specs = (rows, cols, cols)
    return jax.shard_map(shards, mesh=fine, in_specs=in_specs, out_specs=out_specs, check_vma=False)
```

```python
import functools
import math

import numpy as np
import jax
import jax.numpy as jnp
from jax import lax
from jax.experimental import pallas as pl
from jax.experimental.pallas import tpu as pltpu
from jax.sharding import Mesh, PartitionSpec as P

MESH_ID = pl.DeviceIdType.MESH

HEAD_DIM = 80
WIN = 4096
GROUP_BITS = 2
GROUP = 4


EPSILON = 1e-05
ROPE_BASE = 10000.0
LOWEST = -1e30


def from_partner(block, axis, bit):
    count = lax.psum(1, axis)
    route = []
    for low in range(count):
        high = low | 1 << bit
        if high != low and high < count:
            route += [(low, high), (high, low)]
    return lax.ppermute(block, axis, route)


WIDE = ("z", "x", "c")
RING_SUBS = 4


def gather_kernel(nz, nx, nc, nn, blk_a, blk_b, cache_ref, tok_ref, out_a, out_b, cache_out, tok_out,
                  plane_send, plane_recv, ring_send, ring_recv, die_send, die_recv, local_sem,
                  cache_send, cache_recv, tok_send, tok_recv):
    z = lax.axis_index("z")
    x = lax.axis_index("x")
    c = lax.axis_index("c")
    n = lax.axis_index("narrow")
    per_plane = nx * nc
    me_xc = x * nc + c
    me = z * per_plane + me_xc
    place = lax.rem(x, 2) * nc + c
    x_base = x - lax.rem(x, 2)
    half = nz // 2
    step_dir = 1 - 2 * c
    dst_z = lax.rem(z + step_dir + nz, nz)
    src_z = lax.rem(z - step_dir + nz, nz)
    partner = (z, x, 1 - c, n)
    weights = ((blk_a, out_a), (blk_b, out_b))

    def group_dev(p):
        return (z, x_base + p // nc, lax.rem(p, nc), n)

    barrier = pltpu.get_barrier_semaphore()
    for k in range(1, per_plane):
        peer = lax.rem(me_xc + k, per_plane)
        pl.semaphore_signal(barrier, inc=1, device_id=(z, peer // nc, lax.rem(peer, nc), n), device_id_type=MESH_ID)
    for zz in (dst_z, src_z):
        pl.semaphore_signal(barrier, inc=1, device_id=(zz, x, c, n), device_id_type=MESH_ID)
    for k in range(1, nn):
        pl.semaphore_signal(barrier, inc=1, device_id=(z, x, c, lax.rem(n + k, nn)), device_id_type=MESH_ID)
    pl.semaphore_wait(barrier, per_plane + 1 + nn - 1)

    sends = []
    locals_ = []
    pairs = ((blk_a, out_a.at[me]), (blk_b, out_b.at[me]), (cache_ref, cache_out.at[place]), (tok_ref, tok_out.at[n]))
    for src, dst in pairs:
        cp = pltpu.make_async_copy(src, dst, local_sem.at[len(locals_)])
        cp.start()
        locals_.append(cp)
    for k in range(1, per_plane):
        peer = lax.rem(me_xc + k, per_plane)
        for a, (blk, out) in enumerate(weights):
            cp = pltpu.make_async_remote_copy(
                src_ref=blk, dst_ref=out.at[me],
                send_sem=plane_send.at[a, k], recv_sem=plane_recv.at[a, k],
                device_id=(z, peer // nc, lax.rem(peer, nc), n), device_id_type=MESH_ID)
            cp.start()
            sends.append(cp)
    for k in range(1, per_plane):
        sender = lax.rem(me_xc - k + per_plane, per_plane)
        for a, (blk, out) in enumerate(weights):
            pltpu.make_async_remote_copy(
                src_ref=blk, dst_ref=out.at[z * per_plane + sender],
                send_sem=plane_send.at[a, k], recv_sem=plane_recv.at[a, k],
                device_id=(z, x, c, n), device_id_type=MESH_ID).wait_recv()
    locals_[0].wait()
    locals_[1].wait()
    for k in range(1, 2 * nc):
        cp = pltpu.make_async_remote_copy(
            src_ref=cache_ref, dst_ref=cache_out.at[place],
            send_sem=cache_send.at[k], recv_sem=cache_recv.at[k],
            device_id=group_dev(place ^ k), device_id_type=MESH_ID)
        cp.start()
        sends.append(cp)
    for k in range(1, nn):
        cp = pltpu.make_async_remote_copy(
            src_ref=tok_ref, dst_ref=tok_out.at[n],
            send_sem=tok_send.at[k], recv_sem=tok_recv.at[k],
            device_id=(z, x, c, lax.rem(n + k, nn)), device_id_type=MESH_ID)
        cp.start()
        sends.append(cp)

    subs = RING_SUBS
    sub_len = per_plane // subs

    def sub_slot(out, pz, j):
        return out.at[pl.ds(pl.multiple_of(pz * per_plane + j * sub_len, sub_len), sub_len)]

    def ring_copy(a, s, j, pz, device):
        out = weights[a][1]
        return pltpu.make_async_remote_copy(
            src_ref=sub_slot(out, pz, j), dst_ref=sub_slot(out, pz, j),
            send_sem=ring_send.at[a, s - 1, j], recv_sem=ring_recv.at[a, s - 1, j],
            device_id=device, device_id_type=MESH_ID)

    def die_copy(a, s, j, pz):
        out = weights[a][1]
        return pltpu.make_async_remote_copy(
            src_ref=sub_slot(out, pz, j), dst_ref=sub_slot(out, pz, j),
            send_sem=die_send.at[a, s - 1, j], recv_sem=die_recv.at[a, s - 1, j],
            device_id=partner, device_id_type=MESH_ID)

    for s in range(1, half + 1):
        send_z = lax.rem(z - step_dir * (s - 1) + 2 * nz, nz)
        for j in range(subs):
            for a in range(len(weights)):
                if s > 1:
                    ring_copy(a, s - 1, j, send_z, (src_z, x, c, n)).wait_recv()
                    dp = die_copy(a, s - 1, j, send_z)
                    dp.start()
                    sends.append(dp)
                cp = ring_copy(a, s, j, send_z, (dst_z, x, c, n))
                cp.start()
                sends.append(cp)
    last_z = lax.rem(z - step_dir * half + 2 * nz, nz)
    for j in range(subs):
        for a in range(len(weights)):
            ring_copy(a, half, j, last_z, (src_z, x, c, n)).wait_recv()
    for s in range(1, half):
        other_z = lax.rem(z + step_dir * s + 2 * nz, nz)
        for j in range(subs):
            for a in range(len(weights)):
                die_copy(a, s, j, other_z).wait_recv()
    for k in range(1, 2 * nc):
        pltpu.make_async_remote_copy(
            src_ref=cache_ref, dst_ref=cache_out.at[place ^ k],
            send_sem=cache_send.at[k], recv_sem=cache_recv.at[k],
            device_id=(z, x, c, n), device_id_type=MESH_ID).wait_recv()
    for k in range(1, nn):
        pltpu.make_async_remote_copy(
            src_ref=tok_ref, dst_ref=tok_out.at[lax.rem(n - k + nn, nn)],
            send_sem=tok_send.at[k], recv_sem=tok_recv.at[k],
            device_id=(z, x, c, n), device_id_type=MESH_ID).wait_recv()
    for cp in locals_[2:]:
        cp.wait()
    for cp in sends:
        cp.wait_send()


def gather_wide(block_a, block_b, cache, tokens, nz, nx, nc, nn):
    count = nz * nx * nc
    half = nz // 2
    per_plane = nx * nc
    group = 2 * nc
    nbytes = block_a.size * 2 + block_b.size * 2
    return pl.pallas_call(
        functools.partial(gather_kernel, nz, nx, nc, nn),
        out_shape=(
            jax.ShapeDtypeStruct((count,) + block_a.shape, block_a.dtype),
            jax.ShapeDtypeStruct((count,) + block_b.shape, block_b.dtype),
            jax.ShapeDtypeStruct((group,) + cache.shape, cache.dtype),
            jax.ShapeDtypeStruct((nn,) + tokens.shape, tokens.dtype),
        ),
        in_specs=[pl.BlockSpec(memory_space=pl.ANY)] * 4,
        out_specs=[pl.BlockSpec(memory_space=pl.ANY)] * 4,
        scratch_shapes=[
            pltpu.SemaphoreType.DMA((2, per_plane)),
            pltpu.SemaphoreType.DMA((2, per_plane)),
            pltpu.SemaphoreType.DMA((2, half, RING_SUBS)),
            pltpu.SemaphoreType.DMA((2, half, RING_SUBS)),
            pltpu.SemaphoreType.DMA((2, half, RING_SUBS)),
            pltpu.SemaphoreType.DMA((2, half, RING_SUBS)),
            pltpu.SemaphoreType.DMA((4,)),
            pltpu.SemaphoreType.DMA((group,)),
            pltpu.SemaphoreType.DMA((group,)),
            pltpu.SemaphoreType.DMA((nn,)),
            pltpu.SemaphoreType.DMA((nn,)),
        ],
        compiler_params=pltpu.CompilerParams(collective_id=0, has_side_effects=True),
        cost_estimate=pl.CostEstimate(flops=0, transcendentals=0, bytes_accessed=2 * count * nbytes),
    )(block_a, block_b, cache, tokens)


def gather_rows(block):
    rows = block.shape[0]
    plane = lax.all_gather(block, ("z", "x"), axis=0, tiled=False)
    both = lax.all_gather(plane, "c", axis=0, tiled=False)
    both = jnp.transpose(both, (1, 0, 2, 3))
    return both.reshape(-1, block.shape[1])


def rms_normed(rows_in, gain):
    values = rows_in.astype(jnp.float32)
    scaling = lax.rsqrt(jnp.mean(values * values, axis=-1, keepdims=True) + EPSILON)
    return (values * scaling * gain.astype(jnp.float32)).astype(jnp.bfloat16)


def rotate(values, positions):
    half_dim = values.shape[-1] // 2
    inverse = ROPE_BASE ** (-(jnp.arange(half_dim, dtype=jnp.float32) * (2.0 / values.shape[-1])))
    angles = positions.astype(jnp.float32)[:, None] * inverse[None, :]
    cos_part = jnp.cos(angles)[:, None, :]
    sin_part = jnp.sin(angles)[:, None, :]
    lower = values[..., :half_dim]
    higher = values[..., half_dim:]
    return jnp.concatenate(
        [lower * cos_part - higher * sin_part, higher * cos_part + lower * sin_part], axis=-1
    )


def ordered(mine, other, upper, along):
    first_half = jnp.where(upper, other, mine)
    second_half = jnp.where(upper, mine, other)
    return jnp.concatenate([first_half, second_half], axis=along)


def empty_state(row_count, groups, repeats):
    return (
        jnp.zeros((row_count, groups, repeats, HEAD_DIM), jnp.float32),
        jnp.full((row_count, groups, repeats), LOWEST, jnp.float32),
        jnp.zeros((row_count, groups, repeats), jnp.float32),
    )


def fold_keys(state, queries, query_pos, keys, values, key_pos, key_ok, widest):
    key_count = keys.shape[1]
    groups = queries.shape[1]
    block = math.gcd(key_count, widest)
    keys_split = keys.reshape(groups, HEAD_DIM, key_count)
    values_split = values.reshape(groups, HEAD_DIM, key_count)
    scale = HEAD_DIM ** (-0.5)

    def step(index, carry):
        accum, top_old, sum_old = carry
        start = index * block
        block_keys = lax.dynamic_slice_in_dim(keys_split, start, block, 2)
        block_values = lax.dynamic_slice_in_dim(values_split, start, block, 2)
        block_pos = lax.dynamic_slice_in_dim(key_pos, start, block, 0)
        block_ok = lax.dynamic_slice_in_dim(key_ok, start, block, 0)
        scores = (
            jnp.einsum("tgrd,gdk->tgrk", queries, block_keys, preferred_element_type=jnp.float32)
            * scale
        )
        allowed = (
            block_ok[None, :]
            & (block_pos[None, :] <= query_pos[:, None])
            & (query_pos[:, None] - block_pos[None, :] < WIN)
        )
        allowed = allowed[:, None, None, :]
        top_new = jnp.maximum(top_old, jnp.max(jnp.where(allowed, scores, LOWEST), axis=-1))
        weights = jnp.where(allowed, jnp.exp(scores - top_new[..., None]), 0.0)
        rescale = jnp.exp(top_old - top_new)
        sum_new = sum_old * rescale + jnp.sum(weights, axis=-1)
        mixed = jnp.einsum(
            "tgrk,gdk->tgrd",
            weights.astype(jnp.bfloat16),
            block_values,
            preferred_element_type=jnp.float32,
        )
        return (accum * rescale[..., None] + mixed, top_new, sum_new)

    return lax.fori_loop(0, key_count // block, step, state)


def exchange(block, axis, count, pairing):
    pieces = [block]
    for k in range(1, count):
        route = [(src, pairing(src, k)) for src in range(count)]
        route = [(dst, src) for src, dst in route]
        pieces.append(lax.ppermute(block, axis, [(pairing(d, k), d) for d in range(count)]))
    return jnp.stack(pieces)


def in_member_order(stacked, me, pairing, along):
    count = stacked.shape[0]
    parts = [stacked[pairing(me, q)] for q in range(count)]
    return jnp.concatenate(parts, axis=along)


def shift_pair(me, k):
    return (me - k) % 4


def xor_pair(me, k):
    return me ^ k


def shards(
    tokens_in,
    norm_gain,
    query_weight,
    key_weight,
    value_weight,
    out_weight,
    cache_keys,
    cache_values,
    cached_len,
    append_slot,
    shard_owner,
):
    n_narrow = lax.psum(1, "narrow")
    me_narrow = lax.axis_index("narrow")
    position = lax.axis_index(WIDE)
    request = position // GROUP
    place = position % GROUP

    def narrow_pair(me, k):
        return (me - k) % n_narrow

    def narrow_src(me, q):
        return (me - q) % n_narrow


    def group_pair(d, k):
        return d ^ k

    def group_route_pieces(block):
        pieces = [block]
        for k in range(1, GROUP):
            route = [(src, src ^ k) for src in range(lax.psum(1, WIDE))]
            pieces.append(lax.ppermute(block, WIDE, route))
        return jnp.stack(pieces)


    q_cols, kv_cols = query_weight.shape[1], key_weight.shape[1]
    joined = jnp.concatenate([query_weight, out_weight, key_weight, value_weight], axis=1)
    block_rows, joined_width = joined.shape
    tiled_rows = block_rows // 16 * 16
    dims = (lax.psum(1, "z"), lax.psum(1, "x"), lax.psum(1, "c"))
    part_a, part_b, cache_blocks, tok_pieces = gather_wide(
        joined[:tiled_rows], joined[tiled_rows:].reshape(-1, 128),
        jnp.concatenate([cache_keys, cache_values], axis=0), tokens_in, *dims, n_narrow)
    whole = jnp.concatenate([tok_pieces[q] for q in range(n_narrow)], axis=1)
    weights_a = part_a.reshape(-1, joined_width)
    weights_b = part_b.reshape(-1, block_rows - tiled_rows, joined_width).reshape(-1, joined_width)

    def split_rows(act):
        grouped = act.reshape(act.shape[0], -1, block_rows)
        return (grouped[:, :, :tiled_rows].reshape(act.shape[0], -1),
                grouped[:, :, tiled_rows:].reshape(act.shape[0], -1))

    def project(act, lo, hi):
        act_a, act_b = split_rows(act)
        return (jnp.dot(act_a, weights_a[:, lo:hi], preferred_element_type=jnp.float32)
                + jnp.dot(act_b, weights_b[:, lo:hi], preferred_element_type=jnp.float32))

    normed = rms_normed(whole, norm_gain)
    tok_rows = whole.shape[0]
    query_width = query_weight.shape[1]
    kv_width = key_weight.shape[1]
    local_heads = query_width // HEAD_DIM
    local_groups = kv_width // HEAD_DIM
    repeats = local_heads // local_groups
    query_sum = project(normed, 0, q_cols)
    kv_sum = project(normed, 2 * q_cols, 2 * q_cols + 2 * kv_cols)
    key_sum = kv_sum[:, :kv_width]
    value_sum = kv_sum[:, kv_width:]
    length = cached_len[request]
    offset = append_slot[request]
    owner = shard_owner[request]
    query_pos = length + place * tok_rows + jnp.arange(tok_rows, dtype=jnp.int32)
    queries = rotate(query_sum.reshape(tok_rows, local_heads, HEAD_DIM), query_pos).astype(
        jnp.bfloat16
    )
    queries = queries.reshape(tok_rows, local_groups, repeats, HEAD_DIM)
    new_keys = (
        rotate(key_sum.reshape(tok_rows, local_groups, HEAD_DIM), query_pos)
        .astype(jnp.bfloat16)
        .reshape(tok_rows, kv_width)
    )
    new_values = value_sum.astype(jnp.bfloat16)
    shard_rows = cache_keys.shape[1]

    old_both = jnp.concatenate([cache_blocks[q] for q in range(GROUP)], axis=1)
    old_keys = old_both[:kv_width]
    old_values = old_both[kv_width:]
    new_both = jnp.concatenate([new_keys, new_values], axis=1)
    new_both = in_member_order(group_route_pieces(new_both), place, lambda me, q: me ^ q, 0)
    new_keys = new_both[:, :kv_width]
    new_values = new_both[:, kv_width:]

    slot_index = jnp.arange(old_keys.shape[1], dtype=jnp.int32)
    cycle = (slot_index // shard_rows - owner) % GROUP * shard_rows + slot_index % shard_rows
    cached_pos = (cycle - offset + length) % WIN
    state = fold_keys(
        empty_state(tok_rows, local_groups, repeats),
        queries,
        query_pos,
        old_keys,
        old_values,
        cached_pos,
        cached_pos < length,
        512,
    )
    key_cols = new_keys.T
    value_cols = new_values.T
    new_count = key_cols.shape[1]
    new_pos = length + jnp.arange(new_count, dtype=jnp.int32)
    state = fold_keys(
        state,
        queries,
        query_pos,
        key_cols,
        value_cols,
        new_pos,
        jnp.ones((new_count,), dtype=bool),
        512,
    )
    accum, top_score, total = state
    attended = (accum / total[..., None]).astype(jnp.bfloat16).reshape(tok_rows, query_width)
    head_pieces = exchange(attended, "narrow", n_narrow, lambda d, k: (d - k) % n_narrow)
    all_heads = in_member_order(head_pieces, me_narrow, lambda me, q: (me - q) % n_narrow, 1)
    update = project(all_heads, q_cols, 2 * q_cols).astype(jnp.bfloat16)

    first = ((place - owner) % GROUP * shard_rows - offset) % WIN
    keys_ext = jnp.concatenate(
        [key_cols, jnp.zeros((kv_width, WIN - new_count), key_cols.dtype), key_cols,
         jnp.zeros((kv_width, shard_rows - new_count), key_cols.dtype)], axis=1)
    values_ext = jnp.concatenate(
        [value_cols, jnp.zeros((kv_width, WIN - new_count), value_cols.dtype), value_cols,
         jnp.zeros((kv_width, shard_rows - new_count), value_cols.dtype)], axis=1)
    spot = (first + jnp.arange(shard_rows, dtype=jnp.int32)) % WIN
    written = spot < new_count
    put_keys = jnp.where(written[None, :], lax.dynamic_slice_in_dim(keys_ext, first, shard_rows, 1), cache_keys)
    put_values = jnp.where(written[None, :], lax.dynamic_slice_in_dim(values_ext, first, shard_rows, 1), cache_values)
    return (update, put_keys, put_values)


def solution(mesh):
    devices = mesh.devices
    wide_devices = devices[:, 0]
    xs = sorted({d.coords[0] for d in wide_devices})
    cores = sorted({getattr(d, "core_on_chip", 0) for d in wide_devices})
    n_x, n_c = len(xs), len(cores)
    n_z = devices.shape[0] // (n_x * n_c)
    fine = Mesh(devices.reshape(n_z, n_x, n_c, devices.shape[1]), ("z", "x", "c", "narrow"))
    rows = P(WIDE, "narrow")
    cols = P("narrow", WIDE)
    in_specs = (rows, P(), rows, rows, rows, rows, cols, cols, P(), P(), P())
    out_specs = (rows, cols, cols)
    return jax.shard_map(shards, mesh=fine, in_specs=in_specs, out_specs=out_specs, check_vma=False)
```

```python
import functools
import math

import numpy as np
import jax
import jax.numpy as jnp
from jax import lax
from jax.experimental import pallas as pl
from jax.experimental.pallas import tpu as pltpu
from jax.sharding import Mesh, PartitionSpec as P

MESH_ID = pl.DeviceIdType.MESH

HEAD_DIM = 80
WIN = 4096
GROUP_BITS = 2
GROUP = 4


EPSILON = 1e-05
ROPE_BASE = 10000.0
LOWEST = -1e30


def from_partner(block, axis, bit):
    count = lax.psum(1, axis)
    route = []
    for low in range(count):
        high = low | 1 << bit
        if high != low and high < count:
            route += [(low, high), (high, low)]
    return lax.ppermute(block, axis, route)


WIDE = ("z", "x", "c")
RING_SUBS = 4


def gather_kernel(nz, nx, nc, nn, blk_ref, cache_ref, tok_ref, out_ref, cache_out, tok_out,
                  plane_send, plane_recv, ring_send, ring_recv, die_send, die_recv, local_sem,
                  cache_send, cache_recv, tok_send, tok_recv):
    z = lax.axis_index("z")
    x = lax.axis_index("x")
    c = lax.axis_index("c")
    n = lax.axis_index("narrow")
    per_plane = nx * nc
    me_xc = x * nc + c
    me = z * per_plane + me_xc
    place = lax.rem(x, 2) * nc + c
    x_base = x - lax.rem(x, 2)
    half = nz // 2
    step_dir = 1 - 2 * c
    dst_z = lax.rem(z + step_dir + nz, nz)
    src_z = lax.rem(z - step_dir + nz, nz)
    partner = (z, x, 1 - c, n)

    def plane_slot(pz):
        return out_ref.at[pl.ds(pl.multiple_of(pz * per_plane, per_plane), per_plane)]

    def group_dev(p):
        return (z, x_base + p // nc, lax.rem(p, nc), n)

    barrier = pltpu.get_barrier_semaphore()
    for k in range(1, per_plane):
        peer = lax.rem(me_xc + k, per_plane)
        pl.semaphore_signal(barrier, inc=1, device_id=(z, peer // nc, lax.rem(peer, nc), n), device_id_type=MESH_ID)
    for zz in (dst_z, src_z):
        pl.semaphore_signal(barrier, inc=1, device_id=(zz, x, c, n), device_id_type=MESH_ID)
    for k in range(1, nn):
        pl.semaphore_signal(barrier, inc=1, device_id=(z, x, c, lax.rem(n + k, nn)), device_id_type=MESH_ID)
    pl.semaphore_wait(barrier, per_plane + 1 + nn - 1)

    sends = []
    locals_ = []
    for src, dst in ((blk_ref, out_ref.at[me]), (cache_ref, cache_out.at[place]), (tok_ref, tok_out.at[n])):
        cp = pltpu.make_async_copy(src, dst, local_sem.at[len(locals_)])
        cp.start()
        locals_.append(cp)
    for k in range(1, per_plane):
        peer = lax.rem(me_xc + k, per_plane)
        cp = pltpu.make_async_remote_copy(
            src_ref=blk_ref, dst_ref=out_ref.at[me],
            send_sem=plane_send.at[k], recv_sem=plane_recv.at[k],
            device_id=(z, peer // nc, lax.rem(peer, nc), n), device_id_type=MESH_ID)
        cp.start()
        sends.append(cp)
    for k in range(1, per_plane):
        sender = lax.rem(me_xc - k + per_plane, per_plane)
        pltpu.make_async_remote_copy(
            src_ref=blk_ref, dst_ref=out_ref.at[z * per_plane + sender],
            send_sem=plane_send.at[k], recv_sem=plane_recv.at[k],
            device_id=(z, x, c, n), device_id_type=MESH_ID).wait_recv()
    locals_[0].wait()
    for k in range(1, 2 * nc):
        cp = pltpu.make_async_remote_copy(
            src_ref=cache_ref, dst_ref=cache_out.at[place],
            send_sem=cache_send.at[k], recv_sem=cache_recv.at[k],
            device_id=group_dev(place ^ k), device_id_type=MESH_ID)
        cp.start()
        sends.append(cp)
    for k in range(1, nn):
        cp = pltpu.make_async_remote_copy(
            src_ref=tok_ref, dst_ref=tok_out.at[n],
            send_sem=tok_send.at[k], recv_sem=tok_recv.at[k],
            device_id=(z, x, c, lax.rem(n + k, nn)), device_id_type=MESH_ID)
        cp.start()
        sends.append(cp)

    subs = RING_SUBS
    sub_len = per_plane // subs

    def sub_slot(pz, j):
        return out_ref.at[pl.ds(pl.multiple_of(pz * per_plane + j * sub_len, sub_len), sub_len)]

    def ring_copy(s, j, pz, device):
        return pltpu.make_async_remote_copy(
            src_ref=sub_slot(pz, j), dst_ref=sub_slot(pz, j),
            send_sem=ring_send.at[s - 1, j], recv_sem=ring_recv.at[s - 1, j],
            device_id=device, device_id_type=MESH_ID)

    def die_copy(s, j, pz):
        return pltpu.make_async_remote_copy(
            src_ref=sub_slot(pz, j), dst_ref=sub_slot(pz, j),
            send_sem=die_send.at[s - 1, j], recv_sem=die_recv.at[s - 1, j],
            device_id=partner, device_id_type=MESH_ID)

    for s in range(1, half + 1):
        send_z = lax.rem(z - step_dir * (s - 1) + 2 * nz, nz)
        for j in range(subs):
            if s > 1:
                ring_copy(s - 1, j, send_z, (src_z, x, c, n)).wait_recv()
                if s - 1 < half:
                    dp = die_copy(s - 1, j, send_z)
                    dp.start()
                    sends.append(dp)
            cp = ring_copy(s, j, send_z, (dst_z, x, c, n))
            cp.start()
            sends.append(cp)
    last_z = lax.rem(z - step_dir * half + 2 * nz, nz)
    for j in range(subs):
        ring_copy(half, j, last_z, (src_z, x, c, n)).wait_recv()
    for s in range(1, half):
        other_z = lax.rem(z + step_dir * s + 2 * nz, nz)
        for j in range(subs):
            die_copy(s, j, other_z).wait_recv()
    for k in range(1, 2 * nc):
        pltpu.make_async_remote_copy(
            src_ref=cache_ref, dst_ref=cache_out.at[place ^ k],
            send_sem=cache_send.at[k], recv_sem=cache_recv.at[k],
            device_id=(z, x, c, n), device_id_type=MESH_ID).wait_recv()
    for k in range(1, nn):
        pltpu.make_async_remote_copy(
            src_ref=tok_ref, dst_ref=tok_out.at[lax.rem(n - k + nn, nn)],
            send_sem=tok_send.at[k], recv_sem=tok_recv.at[k],
            device_id=(z, x, c, n), device_id_type=MESH_ID).wait_recv()
    for cp in locals_[1:]:
        cp.wait()
    for cp in sends:
        cp.wait_send()


def gather_wide(block, cache, tokens, nz, nx, nc, nn):
    count = nz * nx * nc
    half = nz // 2
    per_plane = nx * nc
    group = 2 * nc
    nbytes = block.size * block.dtype.itemsize
    return pl.pallas_call(
        functools.partial(gather_kernel, nz, nx, nc, nn),
        out_shape=(
            jax.ShapeDtypeStruct((count,) + block.shape, block.dtype),
            jax.ShapeDtypeStruct((group,) + cache.shape, cache.dtype),
            jax.ShapeDtypeStruct((nn,) + tokens.shape, tokens.dtype),
        ),
        in_specs=[pl.BlockSpec(memory_space=pl.ANY)] * 3,
        out_specs=[pl.BlockSpec(memory_space=pl.ANY)] * 3,
        scratch_shapes=[
            pltpu.SemaphoreType.DMA((per_plane,)),
            pltpu.SemaphoreType.DMA((per_plane,)),
            pltpu.SemaphoreType.DMA((half, RING_SUBS)),
            pltpu.SemaphoreType.DMA((half, RING_SUBS)),
            pltpu.SemaphoreType.DMA((half, RING_SUBS)),
            pltpu.SemaphoreType.DMA((half, RING_SUBS)),
            pltpu.SemaphoreType.DMA((3,)),
            pltpu.SemaphoreType.DMA((group,)),
            pltpu.SemaphoreType.DMA((group,)),
            pltpu.SemaphoreType.DMA((nn,)),
            pltpu.SemaphoreType.DMA((nn,)),
        ],
        compiler_params=pltpu.CompilerParams(collective_id=0, has_side_effects=True),
        cost_estimate=pl.CostEstimate(flops=0, transcendentals=0, bytes_accessed=2 * count * nbytes),
    )(block, cache, tokens)


def gather_rows(block):
    rows = block.shape[0]
    plane = lax.all_gather(block, ("z", "x"), axis=0, tiled=False)
    both = lax.all_gather(plane, "c", axis=0, tiled=False)
    both = jnp.transpose(both, (1, 0, 2, 3))
    return both.reshape(-1, block.shape[1])


def rms_normed(rows_in, gain):
    values = rows_in.astype(jnp.float32)
    scaling = lax.rsqrt(jnp.mean(values * values, axis=-1, keepdims=True) + EPSILON)
    return (values * scaling * gain.astype(jnp.float32)).astype(jnp.bfloat16)


def rotate(values, positions):
    half_dim = values.shape[-1] // 2
    inverse = ROPE_BASE ** (-(jnp.arange(half_dim, dtype=jnp.float32) * (2.0 / values.shape[-1])))
    angles = positions.astype(jnp.float32)[:, None] * inverse[None, :]
    cos_part = jnp.cos(angles)[:, None, :]
    sin_part = jnp.sin(angles)[:, None, :]
    lower = values[..., :half_dim]
    higher = values[..., half_dim:]
    return jnp.concatenate(
        [lower * cos_part - higher * sin_part, higher * cos_part + lower * sin_part], axis=-1
    )


def ordered(mine, other, upper, along):
    first_half = jnp.where(upper, other, mine)
    second_half = jnp.where(upper, mine, other)
    return jnp.concatenate([first_half, second_half], axis=along)


def empty_state(row_count, groups, repeats):
    return (
        jnp.zeros((row_count, groups, repeats, HEAD_DIM), jnp.float32),
        jnp.full((row_count, groups, repeats), LOWEST, jnp.float32),
        jnp.zeros((row_count, groups, repeats), jnp.float32),
    )


def fold_keys(state, queries, query_pos, keys, values, key_pos, key_ok, widest):
    key_count = keys.shape[1]
    groups = queries.shape[1]
    block = math.gcd(key_count, widest)
    keys_split = keys.reshape(groups, HEAD_DIM, key_count)
    values_split = values.reshape(groups, HEAD_DIM, key_count)
    scale = HEAD_DIM ** (-0.5)

    def step(index, carry):
        accum, top_old, sum_old = carry
        start = index * block
        block_keys = lax.dynamic_slice_in_dim(keys_split, start, block, 2)
        block_values = lax.dynamic_slice_in_dim(values_split, start, block, 2)
        block_pos = lax.dynamic_slice_in_dim(key_pos, start, block, 0)
        block_ok = lax.dynamic_slice_in_dim(key_ok, start, block, 0)
        scores = (
            jnp.einsum("tgrd,gdk->tgrk", queries, block_keys, preferred_element_type=jnp.float32)
            * scale
        )
        allowed = (
            block_ok[None, :]
            & (block_pos[None, :] <= query_pos[:, None])
            & (query_pos[:, None] - block_pos[None, :] < WIN)
        )
        allowed = allowed[:, None, None, :]
        top_new = jnp.maximum(top_old, jnp.max(jnp.where(allowed, scores, LOWEST), axis=-1))
        weights = jnp.where(allowed, jnp.exp(scores - top_new[..., None]), 0.0)
        rescale = jnp.exp(top_old - top_new)
        sum_new = sum_old * rescale + jnp.sum(weights, axis=-1)
        mixed = jnp.einsum(
            "tgrk,gdk->tgrd",
            weights.astype(jnp.bfloat16),
            block_values,
            preferred_element_type=jnp.float32,
        )
        return (accum * rescale[..., None] + mixed, top_new, sum_new)

    return lax.fori_loop(0, key_count // block, step, state)


def exchange(block, axis, count, pairing):
    pieces = [block]
    for k in range(1, count):
        route = [(src, pairing(src, k)) for src in range(count)]
        route = [(dst, src) for src, dst in route]
        pieces.append(lax.ppermute(block, axis, [(pairing(d, k), d) for d in range(count)]))
    return jnp.stack(pieces)


def in_member_order(stacked, me, pairing, along):
    count = stacked.shape[0]
    parts = [stacked[pairing(me, q)] for q in range(count)]
    return jnp.concatenate(parts, axis=along)


def shift_pair(me, k):
    return (me - k) % 4


def xor_pair(me, k):
    return me ^ k


def shards(
    tokens_in,
    norm_gain,
    query_weight,
    key_weight,
    value_weight,
    out_weight,
    cache_keys,
    cache_values,
    cached_len,
    append_slot,
    shard_owner,
):
    n_narrow = lax.psum(1, "narrow")
    me_narrow = lax.axis_index("narrow")
    position = lax.axis_index(WIDE)
    request = position // GROUP
    place = position % GROUP

    def narrow_pair(me, k):
        return (me - k) % n_narrow

    def narrow_src(me, q):
        return (me - q) % n_narrow


    def group_pair(d, k):
        return d ^ k

    def group_route_pieces(block):
        pieces = [block]
        for k in range(1, GROUP):
            route = [(src, src ^ k) for src in range(lax.psum(1, WIDE))]
            pieces.append(lax.ppermute(block, WIDE, route))
        return jnp.stack(pieces)


    sizes = (query_weight.shape[1], key_weight.shape[1], value_weight.shape[1], out_weight.shape[1])
    joined = jnp.concatenate([query_weight, key_weight, value_weight, out_weight], axis=1)
    block_rows, joined_width = joined.shape
    dims = (lax.psum(1, "z"), lax.psum(1, "x"), lax.psum(1, "c"))
    gathered, cache_blocks, tok_pieces = gather_wide(
        joined.reshape(-1, 128), jnp.concatenate([cache_keys, cache_values], axis=0), tokens_in,
        *dims, n_narrow)
    whole = jnp.concatenate([tok_pieces[q] for q in range(n_narrow)], axis=1)
    all_weights = gathered.reshape(-1, joined_width)
    qkv = all_weights[:, : sum(sizes[:3])]
    out_rows = all_weights[:, sum(sizes[:3]) :]

    normed = rms_normed(whole, norm_gain)
    tok_rows = whole.shape[0]
    query_width = query_weight.shape[1]
    kv_width = key_weight.shape[1]
    local_heads = query_width // HEAD_DIM
    local_groups = kv_width // HEAD_DIM
    repeats = local_heads // local_groups
    qkv_sum = jnp.dot(normed, qkv, preferred_element_type=jnp.float32)
    query_sum = qkv_sum[:, :query_width]
    key_sum = qkv_sum[:, query_width : query_width + kv_width]
    value_sum = qkv_sum[:, query_width + kv_width :]
    length = cached_len[request]
    offset = append_slot[request]
    owner = shard_owner[request]
    query_pos = length + place * tok_rows + jnp.arange(tok_rows, dtype=jnp.int32)
    queries = rotate(query_sum.reshape(tok_rows, local_heads, HEAD_DIM), query_pos).astype(
        jnp.bfloat16
    )
    queries = queries.reshape(tok_rows, local_groups, repeats, HEAD_DIM)
    new_keys = (
        rotate(key_sum.reshape(tok_rows, local_groups, HEAD_DIM), query_pos)
        .astype(jnp.bfloat16)
        .reshape(tok_rows, kv_width)
    )
    new_values = value_sum.astype(jnp.bfloat16)
    shard_rows = cache_keys.shape[1]

    old_both = jnp.concatenate([cache_blocks[q] for q in range(GROUP)], axis=1)
    old_keys = old_both[:kv_width]
    old_values = old_both[kv_width:]
    new_both = jnp.concatenate([new_keys, new_values], axis=1)
    new_both = in_member_order(group_route_pieces(new_both), place, lambda me, q: me ^ q, 0)
    new_keys = new_both[:, :kv_width]
    new_values = new_both[:, kv_width:]

    slot_index = jnp.arange(old_keys.shape[1], dtype=jnp.int32)
    cycle = (slot_index // shard_rows - owner) % GROUP * shard_rows + slot_index % shard_rows
    cached_pos = (cycle - offset + length) % WIN
    state = fold_keys(
        empty_state(tok_rows, local_groups, repeats),
        queries,
        query_pos,
        old_keys,
        old_values,
        cached_pos,
        cached_pos < length,
        256,
    )
    key_cols = new_keys.T
    value_cols = new_values.T
    new_count = key_cols.shape[1]
    new_pos = length + jnp.arange(new_count, dtype=jnp.int32)
    state = fold_keys(
        state,
        queries,
        query_pos,
        key_cols,
        value_cols,
        new_pos,
        jnp.ones((new_count,), dtype=bool),
        256,
    )
    accum, top_score, total = state
    attended = (accum / total[..., None]).astype(jnp.bfloat16).reshape(tok_rows, query_width)
    head_pieces = exchange(attended, "narrow", n_narrow, lambda d, k: (d - k) % n_narrow)
    all_heads = in_member_order(head_pieces, me_narrow, lambda me, q: (me - q) % n_narrow, 1)
    update = jnp.dot(all_heads, out_rows, preferred_element_type=jnp.float32).astype(jnp.bfloat16)

    first = ((place - owner) % GROUP * shard_rows - offset) % WIN
    keys_ext = jnp.concatenate(
        [key_cols, jnp.zeros((kv_width, WIN - new_count), key_cols.dtype), key_cols,
         jnp.zeros((kv_width, shard_rows - new_count), key_cols.dtype)], axis=1)
    values_ext = jnp.concatenate(
        [value_cols, jnp.zeros((kv_width, WIN - new_count), value_cols.dtype), value_cols,
         jnp.zeros((kv_width, shard_rows - new_count), value_cols.dtype)], axis=1)
    spot = (first + jnp.arange(shard_rows, dtype=jnp.int32)) % WIN
    written = spot < new_count
    put_keys = jnp.where(written[None, :], lax.dynamic_slice_in_dim(keys_ext, first, shard_rows, 1), cache_keys)
    put_values = jnp.where(written[None, :], lax.dynamic_slice_in_dim(values_ext, first, shard_rows, 1), cache_values)
    return (update, put_keys, put_values)


def solution(mesh):
    devices = mesh.devices
    wide_devices = devices[:, 0]
    xs = sorted({d.coords[0] for d in wide_devices})
    cores = sorted({getattr(d, "core_on_chip", 0) for d in wide_devices})
    n_x, n_c = len(xs), len(cores)
    n_z = devices.shape[0] // (n_x * n_c)
    fine = Mesh(devices.reshape(n_z, n_x, n_c, devices.shape[1]), ("z", "x", "c", "narrow"))
    rows = P(WIDE, "narrow")
    cols = P("narrow", WIDE)
    in_specs = (rows, P(), rows, rows, rows, rows, cols, cols, P(), P(), P())
    out_specs = (rows, cols, cols)
    return jax.shard_map(shards, mesh=fine, in_specs=in_specs, out_specs=out_specs, check_vma=False)
```

```python
import functools
import math

import numpy as np
import jax
import jax.numpy as jnp
from jax import lax
from jax.experimental import pallas as pl
from jax.experimental.pallas import tpu as pltpu
from jax.sharding import Mesh, PartitionSpec as P

MESH_ID = pl.DeviceIdType.MESH

HEAD_DIM = 80
WIN = 4096
GROUP_BITS = 2
GROUP = 4


EPSILON = 1e-05
ROPE_BASE = 10000.0
LOWEST = -1e30


def from_partner(block, axis, bit):
    count = lax.psum(1, axis)
    route = []
    for low in range(count):
        high = low | 1 << bit
        if high != low and high < count:
            route += [(low, high), (high, low)]
    return lax.ppermute(block, axis, route)


WIDE = ("z", "x", "c")
RING_SUBS = 4


def gather_kernel(nz, nx, nc, nn, blk_a, blk_b, cache_ref, tok_ref, out_a, out_b, cache_out, tok_out,
                  plane_send, plane_recv, ring_send, ring_recv, die_send, die_recv, local_sem,
                  cache_send, cache_recv, tok_send, tok_recv):
    z = lax.axis_index("z")
    x = lax.axis_index("x")
    c = lax.axis_index("c")
    n = lax.axis_index("narrow")
    per_plane = nx * nc
    me_xc = x * nc + c
    me = z * per_plane + me_xc
    place = lax.rem(x, 2) * nc + c
    x_base = x - lax.rem(x, 2)
    half = nz // 2
    step_dir = 1 - 2 * c
    dst_z = lax.rem(z + step_dir + nz, nz)
    src_z = lax.rem(z - step_dir + nz, nz)
    partner = (z, x, 1 - c, n)
    weights = ((blk_a, out_a), (blk_b, out_b))

    def group_dev(p):
        return (z, x_base + p // nc, lax.rem(p, nc), n)

    barrier = pltpu.get_barrier_semaphore()
    for k in range(1, per_plane):
        peer = lax.rem(me_xc + k, per_plane)
        pl.semaphore_signal(barrier, inc=1, device_id=(z, peer // nc, lax.rem(peer, nc), n), device_id_type=MESH_ID)
    for zz in (dst_z, src_z):
        pl.semaphore_signal(barrier, inc=1, device_id=(zz, x, c, n), device_id_type=MESH_ID)
    for k in range(1, nn):
        pl.semaphore_signal(barrier, inc=1, device_id=(z, x, c, lax.rem(n + k, nn)), device_id_type=MESH_ID)
    pl.semaphore_wait(barrier, per_plane + 1 + nn - 1)

    sends = []
    locals_ = []
    pairs = ((blk_a, out_a.at[me]), (blk_b, out_b.at[me]), (cache_ref, cache_out.at[place]), (tok_ref, tok_out.at[n]))
    for src, dst in pairs:
        cp = pltpu.make_async_copy(src, dst, local_sem.at[len(locals_)])
        cp.start()
        locals_.append(cp)
    for k in range(1, per_plane):
        peer = lax.rem(me_xc + k, per_plane)
        for a, (blk, out) in enumerate(weights):
            cp = pltpu.make_async_remote_copy(
                src_ref=blk, dst_ref=out.at[me],
                send_sem=plane_send.at[a, k], recv_sem=plane_recv.at[a, k],
                device_id=(z, peer // nc, lax.rem(peer, nc), n), device_id_type=MESH_ID)
            cp.start()
            sends.append(cp)
    for k in range(1, per_plane):
        sender = lax.rem(me_xc - k + per_plane, per_plane)
        for a, (blk, out) in enumerate(weights):
            pltpu.make_async_remote_copy(
                src_ref=blk, dst_ref=out.at[z * per_plane + sender],
                send_sem=plane_send.at[a, k], recv_sem=plane_recv.at[a, k],
                device_id=(z, x, c, n), device_id_type=MESH_ID).wait_recv()
    locals_[0].wait()
    locals_[1].wait()
    for k in range(1, 2 * nc):
        cp = pltpu.make_async_remote_copy(
            src_ref=cache_ref, dst_ref=cache_out.at[place],
            send_sem=cache_send.at[k], recv_sem=cache_recv.at[k],
            device_id=group_dev(place ^ k), device_id_type=MESH_ID)
        cp.start()
        sends.append(cp)
    for k in range(1, nn):
        cp = pltpu.make_async_remote_copy(
            src_ref=tok_ref, dst_ref=tok_out.at[n],
            send_sem=tok_send.at[k], recv_sem=tok_recv.at[k],
            device_id=(z, x, c, lax.rem(n + k, nn)), device_id_type=MESH_ID)
        cp.start()
        sends.append(cp)

    subs = RING_SUBS
    sub_len = per_plane // subs

    def sub_slot(out, pz, j):
        return out.at[pl.ds(pl.multiple_of(pz * per_plane + j * sub_len, sub_len), sub_len)]

    def ring_copy(a, s, j, pz, device):
        out = weights[a][1]
        return pltpu.make_async_remote_copy(
            src_ref=sub_slot(out, pz, j), dst_ref=sub_slot(out, pz, j),
            send_sem=ring_send.at[a, s - 1, j], recv_sem=ring_recv.at[a, s - 1, j],
            device_id=device, device_id_type=MESH_ID)

    def die_copy(a, s, j, pz):
        out = weights[a][1]
        return pltpu.make_async_remote_copy(
            src_ref=sub_slot(out, pz, j), dst_ref=sub_slot(out, pz, j),
            send_sem=die_send.at[a, s - 1, j], recv_sem=die_recv.at[a, s - 1, j],
            device_id=partner, device_id_type=MESH_ID)

    for s in range(1, half + 1):
        send_z = lax.rem(z - step_dir * (s - 1) + 2 * nz, nz)
        for j in range(subs):
            for a in range(len(weights)):
                if s > 1:
                    ring_copy(a, s - 1, j, send_z, (src_z, x, c, n)).wait_recv()
                    dp = die_copy(a, s - 1, j, send_z)
                    dp.start()
                    sends.append(dp)
                cp = ring_copy(a, s, j, send_z, (dst_z, x, c, n))
                cp.start()
                sends.append(cp)
    last_z = lax.rem(z - step_dir * half + 2 * nz, nz)
    for j in range(subs):
        for a in range(len(weights)):
            ring_copy(a, half, j, last_z, (src_z, x, c, n)).wait_recv()
    for s in range(1, half):
        other_z = lax.rem(z + step_dir * s + 2 * nz, nz)
        for j in range(subs):
            for a in range(len(weights)):
                die_copy(a, s, j, other_z).wait_recv()
    for k in range(1, 2 * nc):
        pltpu.make_async_remote_copy(
            src_ref=cache_ref, dst_ref=cache_out.at[place ^ k],
            send_sem=cache_send.at[k], recv_sem=cache_recv.at[k],
            device_id=(z, x, c, n), device_id_type=MESH_ID).wait_recv()
    for k in range(1, nn):
        pltpu.make_async_remote_copy(
            src_ref=tok_ref, dst_ref=tok_out.at[lax.rem(n - k + nn, nn)],
            send_sem=tok_send.at[k], recv_sem=tok_recv.at[k],
            device_id=(z, x, c, n), device_id_type=MESH_ID).wait_recv()
    for cp in locals_[2:]:
        cp.wait()
    for cp in sends:
        cp.wait_send()


def gather_wide(block_a, block_b, cache, tokens, nz, nx, nc, nn):
    count = nz * nx * nc
    half = nz // 2
    per_plane = nx * nc
    group = 2 * nc
    nbytes = block_a.size * 2 + block_b.size * 2
    return pl.pallas_call(
        functools.partial(gather_kernel, nz, nx, nc, nn),
        out_shape=(
            jax.ShapeDtypeStruct((count,) + block_a.shape, block_a.dtype),
            jax.ShapeDtypeStruct((count,) + block_b.shape, block_b.dtype),
            jax.ShapeDtypeStruct((group,) + cache.shape, cache.dtype),
            jax.ShapeDtypeStruct((nn,) + tokens.shape, tokens.dtype),
        ),
        in_specs=[pl.BlockSpec(memory_space=pl.ANY)] * 4,
        out_specs=[pl.BlockSpec(memory_space=pl.ANY)] * 4,
        scratch_shapes=[
            pltpu.SemaphoreType.DMA((2, per_plane)),
            pltpu.SemaphoreType.DMA((2, per_plane)),
            pltpu.SemaphoreType.DMA((2, half, RING_SUBS)),
            pltpu.SemaphoreType.DMA((2, half, RING_SUBS)),
            pltpu.SemaphoreType.DMA((2, half, RING_SUBS)),
            pltpu.SemaphoreType.DMA((2, half, RING_SUBS)),
            pltpu.SemaphoreType.DMA((4,)),
            pltpu.SemaphoreType.DMA((group,)),
            pltpu.SemaphoreType.DMA((group,)),
            pltpu.SemaphoreType.DMA((nn,)),
            pltpu.SemaphoreType.DMA((nn,)),
        ],
        compiler_params=pltpu.CompilerParams(collective_id=0, has_side_effects=True),
        cost_estimate=pl.CostEstimate(flops=0, transcendentals=0, bytes_accessed=2 * count * nbytes),
    )(block_a, block_b, cache, tokens)


def gather_rows(block):
    rows = block.shape[0]
    plane = lax.all_gather(block, ("z", "x"), axis=0, tiled=False)
    both = lax.all_gather(plane, "c", axis=0, tiled=False)
    both = jnp.transpose(both, (1, 0, 2, 3))
    return both.reshape(-1, block.shape[1])


def rms_normed(rows_in, gain):
    values = rows_in.astype(jnp.float32)
    scaling = lax.rsqrt(jnp.mean(values * values, axis=-1, keepdims=True) + EPSILON)
    return (values * scaling * gain.astype(jnp.float32)).astype(jnp.bfloat16)


def rotate(values, positions):
    half_dim = values.shape[-1] // 2
    inverse = ROPE_BASE ** (-(jnp.arange(half_dim, dtype=jnp.float32) * (2.0 / values.shape[-1])))
    angles = positions.astype(jnp.float32)[:, None] * inverse[None, :]
    cos_part = jnp.cos(angles)[:, None, :]
    sin_part = jnp.sin(angles)[:, None, :]
    lower = values[..., :half_dim]
    higher = values[..., half_dim:]
    return jnp.concatenate(
        [lower * cos_part - higher * sin_part, higher * cos_part + lower * sin_part], axis=-1
    )


def ordered(mine, other, upper, along):
    first_half = jnp.where(upper, other, mine)
    second_half = jnp.where(upper, mine, other)
    return jnp.concatenate([first_half, second_half], axis=along)


def empty_state(row_count, groups, repeats):
    return (
        jnp.zeros((row_count, groups, repeats, HEAD_DIM), jnp.float32),
        jnp.full((row_count, groups, repeats), LOWEST, jnp.float32),
        jnp.zeros((row_count, groups, repeats), jnp.float32),
    )


def fold_keys(state, queries, query_pos, keys, values, key_pos, key_ok, widest):
    key_count = keys.shape[1]
    groups = queries.shape[1]
    block = math.gcd(key_count, widest)
    keys_split = keys.reshape(groups, HEAD_DIM, key_count)
    values_split = values.reshape(groups, HEAD_DIM, key_count)
    scale = HEAD_DIM ** (-0.5)

    def step(index, carry):
        accum, top_old, sum_old = carry
        start = index * block
        block_keys = lax.dynamic_slice_in_dim(keys_split, start, block, 2)
        block_values = lax.dynamic_slice_in_dim(values_split, start, block, 2)
        block_pos = lax.dynamic_slice_in_dim(key_pos, start, block, 0)
        block_ok = lax.dynamic_slice_in_dim(key_ok, start, block, 0)
        scores = (
            jnp.einsum("tgrd,gdk->tgrk", queries, block_keys, preferred_element_type=jnp.float32)
            * scale
        )
        allowed = (
            block_ok[None, :]
            & (block_pos[None, :] <= query_pos[:, None])
            & (query_pos[:, None] - block_pos[None, :] < WIN)
        )
        allowed = allowed[:, None, None, :]
        top_new = jnp.maximum(top_old, jnp.max(jnp.where(allowed, scores, LOWEST), axis=-1))
        weights = jnp.where(allowed, jnp.exp(scores - top_new[..., None]), 0.0)
        rescale = jnp.exp(top_old - top_new)
        sum_new = sum_old * rescale + jnp.sum(weights, axis=-1)
        mixed = jnp.einsum(
            "tgrk,gdk->tgrd",
            weights.astype(jnp.bfloat16),
            block_values,
            preferred_element_type=jnp.float32,
        )
        return (accum * rescale[..., None] + mixed, top_new, sum_new)

    return lax.fori_loop(0, key_count // block, step, state)


def exchange(block, axis, count, pairing):
    pieces = [block]
    for k in range(1, count):
        route = [(src, pairing(src, k)) for src in range(count)]
        route = [(dst, src) for src, dst in route]
        pieces.append(lax.ppermute(block, axis, [(pairing(d, k), d) for d in range(count)]))
    return jnp.stack(pieces)


def in_member_order(stacked, me, pairing, along):
    count = stacked.shape[0]
    parts = [stacked[pairing(me, q)] for q in range(count)]
    return jnp.concatenate(parts, axis=along)


def shift_pair(me, k):
    return (me - k) % 4


def xor_pair(me, k):
    return me ^ k


def shards(
    tokens_in,
    norm_gain,
    query_weight,
    key_weight,
    value_weight,
    out_weight,
    cache_keys,
    cache_values,
    cached_len,
    append_slot,
    shard_owner,
):
    n_narrow = lax.psum(1, "narrow")
    me_narrow = lax.axis_index("narrow")
    position = lax.axis_index(WIDE)
    request = position // GROUP
    place = position % GROUP

    def narrow_pair(me, k):
        return (me - k) % n_narrow

    def narrow_src(me, q):
        return (me - q) % n_narrow


    def group_pair(d, k):
        return d ^ k

    def group_route_pieces(block):
        pieces = [block]
        for k in range(1, GROUP):
            route = [(src, src ^ k) for src in range(lax.psum(1, WIDE))]
            pieces.append(lax.ppermute(block, WIDE, route))
        return jnp.stack(pieces)


    sizes = (query_weight.shape[1], key_weight.shape[1], value_weight.shape[1], out_weight.shape[1])
    joined = jnp.concatenate([query_weight, key_weight, value_weight, out_weight], axis=1)
    block_rows, joined_width = joined.shape
    dims = (lax.psum(1, "z"), lax.psum(1, "x"), lax.psum(1, "c"))
    tiled_rows = block_rows // 16 * 16
    part_a, part_b, cache_blocks, tok_pieces = gather_wide(
        joined[:tiled_rows], joined[tiled_rows:].reshape(-1, 128),
        jnp.concatenate([cache_keys, cache_values], axis=0), tokens_in, *dims, n_narrow)
    whole = jnp.concatenate([tok_pieces[q] for q in range(n_narrow)], axis=1)
    part_b = part_b.reshape(-1, block_rows - tiled_rows, joined_width).reshape(-1, joined_width)
    all_weights = jnp.concatenate([part_a.reshape(-1, joined_width), part_b], axis=0)

    def rows_order(act):
        grouped = act.reshape(act.shape[0], -1, block_rows)
        return jnp.concatenate(
            [grouped[:, :, :tiled_rows].reshape(act.shape[0], -1),
             grouped[:, :, tiled_rows:].reshape(act.shape[0], -1)], axis=1)

    qkv = all_weights[:, : sum(sizes[:3])]
    out_rows = all_weights[:, sum(sizes[:3]) :]

    normed = rms_normed(whole, norm_gain)
    tok_rows = whole.shape[0]
    query_width = query_weight.shape[1]
    kv_width = key_weight.shape[1]
    local_heads = query_width // HEAD_DIM
    local_groups = kv_width // HEAD_DIM
    repeats = local_heads // local_groups
    qkv_sum = jnp.dot(rows_order(normed), qkv, preferred_element_type=jnp.float32)
    query_sum = qkv_sum[:, :query_width]
    key_sum = qkv_sum[:, query_width : query_width + kv_width]
    value_sum = qkv_sum[:, query_width + kv_width :]
    length = cached_len[request]
    offset = append_slot[request]
    owner = shard_owner[request]
    query_pos = length + place * tok_rows + jnp.arange(tok_rows, dtype=jnp.int32)
    queries = rotate(query_sum.reshape(tok_rows, local_heads, HEAD_DIM), query_pos).astype(
        jnp.bfloat16
    )
    queries = queries.reshape(tok_rows, local_groups, repeats, HEAD_DIM)
    new_keys = (
        rotate(key_sum.reshape(tok_rows, local_groups, HEAD_DIM), query_pos)
        .astype(jnp.bfloat16)
        .reshape(tok_rows, kv_width)
    )
    new_values = value_sum.astype(jnp.bfloat16)
    shard_rows = cache_keys.shape[1]

    old_both = jnp.concatenate([cache_blocks[q] for q in range(GROUP)], axis=1)
    old_keys = old_both[:kv_width]
    old_values = old_both[kv_width:]
    new_both = jnp.concatenate([new_keys, new_values], axis=1)
    new_both = in_member_order(group_route_pieces(new_both), place, lambda me, q: me ^ q, 0)
    new_keys = new_both[:, :kv_width]
    new_values = new_both[:, kv_width:]

    slot_index = jnp.arange(old_keys.shape[1], dtype=jnp.int32)
    cycle = (slot_index // shard_rows - owner) % GROUP * shard_rows + slot_index % shard_rows
    cached_pos = (cycle - offset + length) % WIN
    state = fold_keys(
        empty_state(tok_rows, local_groups, repeats),
        queries,
        query_pos,
        old_keys,
        old_values,
        cached_pos,
        cached_pos < length,
        512,
    )
    key_cols = new_keys.T
    value_cols = new_values.T
    new_count = key_cols.shape[1]
    new_pos = length + jnp.arange(new_count, dtype=jnp.int32)
    state = fold_keys(
        state,
        queries,
        query_pos,
        key_cols,
        value_cols,
        new_pos,
        jnp.ones((new_count,), dtype=bool),
        512,
    )
    accum, top_score, total = state
    attended = (accum / total[..., None]).astype(jnp.bfloat16).reshape(tok_rows, query_width)
    head_pieces = exchange(attended, "narrow", n_narrow, lambda d, k: (d - k) % n_narrow)
    all_heads = in_member_order(head_pieces, me_narrow, lambda me, q: (me - q) % n_narrow, 1)
    update = jnp.dot(rows_order(all_heads), out_rows, preferred_element_type=jnp.float32).astype(jnp.bfloat16)

    first = ((place - owner) % GROUP * shard_rows - offset) % WIN
    keys_ext = jnp.concatenate(
        [key_cols, jnp.zeros((kv_width, WIN - new_count), key_cols.dtype), key_cols,
         jnp.zeros((kv_width, shard_rows - new_count), key_cols.dtype)], axis=1)
    values_ext = jnp.concatenate(
        [value_cols, jnp.zeros((kv_width, WIN - new_count), value_cols.dtype), value_cols,
         jnp.zeros((kv_width, shard_rows - new_count), value_cols.dtype)], axis=1)
    spot = (first + jnp.arange(shard_rows, dtype=jnp.int32)) % WIN
    written = spot < new_count
    put_keys = jnp.where(written[None, :], lax.dynamic_slice_in_dim(keys_ext, first, shard_rows, 1), cache_keys)
    put_values = jnp.where(written[None, :], lax.dynamic_slice_in_dim(values_ext, first, shard_rows, 1), cache_values)
    return (update, put_keys, put_values)


def solution(mesh):
    devices = mesh.devices
    wide_devices = devices[:, 0]
    xs = sorted({d.coords[0] for d in wide_devices})
    cores = sorted({getattr(d, "core_on_chip", 0) for d in wide_devices})
    n_x, n_c = len(xs), len(cores)
    n_z = devices.shape[0] // (n_x * n_c)
    fine = Mesh(devices.reshape(n_z, n_x, n_c, devices.shape[1]), ("z", "x", "c", "narrow"))
    rows = P(WIDE, "narrow")
    cols = P("narrow", WIDE)
    in_specs = (rows, P(), rows, rows, rows, rows, cols, cols, P(), P(), P())
    out_specs = (rows, cols, cols)
    return jax.shard_map(shards, mesh=fine, in_specs=in_specs, out_specs=out_specs, check_vma=False)
```

```python
import functools
import math

import numpy as np
import jax
import jax.numpy as jnp
from jax import lax
from jax.experimental import pallas as pl
from jax.experimental.pallas import tpu as pltpu
from jax.sharding import Mesh, PartitionSpec as P

MESH_ID = pl.DeviceIdType.MESH

HEAD_DIM = 80
WIN = 4096
GROUP_BITS = 2
GROUP = 4


EPSILON = 1e-05
ROPE_BASE = 10000.0
LOWEST = -1e30


def from_partner(block, axis, bit):
    count = lax.psum(1, axis)
    route = []
    for low in range(count):
        high = low | 1 << bit
        if high != low and high < count:
            route += [(low, high), (high, low)]
    return lax.ppermute(block, axis, route)


WIDE = ("z", "x", "c")
RING_SUBS = 4


def gather_kernel(nz, nx, nc, nn, blk_ref, cache_ref, tok_ref, out_ref, cache_out, tok_out,
                  plane_send, plane_recv, ring_send, ring_recv, die_send, die_recv, local_sem,
                  cache_send, cache_recv, tok_send, tok_recv):
    z = lax.axis_index("z")
    x = lax.axis_index("x")
    c = lax.axis_index("c")
    n = lax.axis_index("narrow")
    per_plane = nx * nc
    me_xc = x * nc + c
    me = z * per_plane + me_xc
    place = lax.rem(x, 2) * nc + c
    x_base = x - lax.rem(x, 2)
    half = nz // 2
    step_dir = 1 - 2 * c
    dst_z = lax.rem(z + step_dir + nz, nz)
    src_z = lax.rem(z - step_dir + nz, nz)
    partner = (z, x, 1 - c, n)

    def plane_slot(pz):
        return out_ref.at[pl.ds(pl.multiple_of(pz * per_plane, per_plane), per_plane)]

    def group_dev(p):
        return (z, x_base + p // nc, lax.rem(p, nc), n)

    barrier = pltpu.get_barrier_semaphore()
    for k in range(1, per_plane):
        peer = lax.rem(me_xc + k, per_plane)
        pl.semaphore_signal(barrier, inc=1, device_id=(z, peer // nc, lax.rem(peer, nc), n), device_id_type=MESH_ID)
    for zz in (dst_z, src_z):
        pl.semaphore_signal(barrier, inc=1, device_id=(zz, x, c, n), device_id_type=MESH_ID)
    for k in range(1, nn):
        pl.semaphore_signal(barrier, inc=1, device_id=(z, x, c, lax.rem(n + k, nn)), device_id_type=MESH_ID)
    pl.semaphore_wait(barrier, per_plane + 1 + nn - 1)

    sends = []
    locals_ = []
    for src, dst in ((blk_ref, out_ref.at[me]), (cache_ref, cache_out.at[place]), (tok_ref, tok_out.at[n])):
        cp = pltpu.make_async_copy(src, dst, local_sem.at[len(locals_)])
        cp.start()
        locals_.append(cp)
    for k in range(1, per_plane):
        peer = lax.rem(me_xc + k, per_plane)
        cp = pltpu.make_async_remote_copy(
            src_ref=blk_ref, dst_ref=out_ref.at[me],
            send_sem=plane_send.at[k], recv_sem=plane_recv.at[k],
            device_id=(z, peer // nc, lax.rem(peer, nc), n), device_id_type=MESH_ID)
        cp.start()
        sends.append(cp)
    for k in range(1, per_plane):
        sender = lax.rem(me_xc - k + per_plane, per_plane)
        pltpu.make_async_remote_copy(
            src_ref=blk_ref, dst_ref=out_ref.at[z * per_plane + sender],
            send_sem=plane_send.at[k], recv_sem=plane_recv.at[k],
            device_id=(z, x, c, n), device_id_type=MESH_ID).wait_recv()
    locals_[0].wait()
    for k in range(1, 2 * nc):
        cp = pltpu.make_async_remote_copy(
            src_ref=cache_ref, dst_ref=cache_out.at[place],
            send_sem=cache_send.at[k], recv_sem=cache_recv.at[k],
            device_id=group_dev(place ^ k), device_id_type=MESH_ID)
        cp.start()
        sends.append(cp)
    for k in range(1, nn):
        cp = pltpu.make_async_remote_copy(
            src_ref=tok_ref, dst_ref=tok_out.at[n],
            send_sem=tok_send.at[k], recv_sem=tok_recv.at[k],
            device_id=(z, x, c, lax.rem(n + k, nn)), device_id_type=MESH_ID)
        cp.start()
        sends.append(cp)

    subs = RING_SUBS
    sub_len = per_plane // subs

    def sub_slot(pz, j):
        return out_ref.at[pl.ds(pl.multiple_of(pz * per_plane + j * sub_len, sub_len), sub_len)]

    def ring_copy(s, j, pz, device):
        return pltpu.make_async_remote_copy(
            src_ref=sub_slot(pz, j), dst_ref=sub_slot(pz, j),
            send_sem=ring_send.at[s - 1, j], recv_sem=ring_recv.at[s - 1, j],
            device_id=device, device_id_type=MESH_ID)

    def die_copy(s, j, pz):
        return pltpu.make_async_remote_copy(
            src_ref=sub_slot(pz, j), dst_ref=sub_slot(pz, j),
            send_sem=die_send.at[s - 1, j], recv_sem=die_recv.at[s - 1, j],
            device_id=partner, device_id_type=MESH_ID)

    for s in range(1, half + 1):
        send_z = lax.rem(z - step_dir * (s - 1) + 2 * nz, nz)
        for j in range(subs):
            if s > 1:
                ring_copy(s - 1, j, send_z, (src_z, x, c, n)).wait_recv()
                if s - 1 < half:
                    dp = die_copy(s - 1, j, send_z)
                    dp.start()
                    sends.append(dp)
            cp = ring_copy(s, j, send_z, (dst_z, x, c, n))
            cp.start()
            sends.append(cp)
    last_z = lax.rem(z - step_dir * half + 2 * nz, nz)
    for j in range(subs):
        ring_copy(half, j, last_z, (src_z, x, c, n)).wait_recv()
    for s in range(1, half):
        other_z = lax.rem(z + step_dir * s + 2 * nz, nz)
        for j in range(subs):
            die_copy(s, j, other_z).wait_recv()
    for k in range(1, 2 * nc):
        pltpu.make_async_remote_copy(
            src_ref=cache_ref, dst_ref=cache_out.at[place ^ k],
            send_sem=cache_send.at[k], recv_sem=cache_recv.at[k],
            device_id=(z, x, c, n), device_id_type=MESH_ID).wait_recv()
    for k in range(1, nn):
        pltpu.make_async_remote_copy(
            src_ref=tok_ref, dst_ref=tok_out.at[lax.rem(n - k + nn, nn)],
            send_sem=tok_send.at[k], recv_sem=tok_recv.at[k],
            device_id=(z, x, c, n), device_id_type=MESH_ID).wait_recv()
    for cp in locals_[1:]:
        cp.wait()
    for cp in sends:
        cp.wait_send()


def gather_wide(block, cache, tokens, nz, nx, nc, nn):
    count = nz * nx * nc
    half = nz // 2
    per_plane = nx * nc
    group = 2 * nc
    nbytes = block.size * block.dtype.itemsize
    return pl.pallas_call(
        functools.partial(gather_kernel, nz, nx, nc, nn),
        out_shape=(
            jax.ShapeDtypeStruct((count,) + block.shape, block.dtype),
            jax.ShapeDtypeStruct((group,) + cache.shape, cache.dtype),
            jax.ShapeDtypeStruct((nn,) + tokens.shape, tokens.dtype),
        ),
        in_specs=[pl.BlockSpec(memory_space=pl.ANY)] * 3,
        out_specs=[pl.BlockSpec(memory_space=pl.ANY)] * 3,
        scratch_shapes=[
            pltpu.SemaphoreType.DMA((per_plane,)),
            pltpu.SemaphoreType.DMA((per_plane,)),
            pltpu.SemaphoreType.DMA((half, RING_SUBS)),
            pltpu.SemaphoreType.DMA((half, RING_SUBS)),
            pltpu.SemaphoreType.DMA((half, RING_SUBS)),
            pltpu.SemaphoreType.DMA((half, RING_SUBS)),
            pltpu.SemaphoreType.DMA((3,)),
            pltpu.SemaphoreType.DMA((group,)),
            pltpu.SemaphoreType.DMA((group,)),
            pltpu.SemaphoreType.DMA((nn,)),
            pltpu.SemaphoreType.DMA((nn,)),
        ],
        compiler_params=pltpu.CompilerParams(collective_id=0, has_side_effects=True),
        cost_estimate=pl.CostEstimate(flops=0, transcendentals=0, bytes_accessed=2 * count * nbytes),
    )(block, cache, tokens)


def gather_rows(block):
    rows = block.shape[0]
    plane = lax.all_gather(block, ("z", "x"), axis=0, tiled=False)
    both = lax.all_gather(plane, "c", axis=0, tiled=False)
    both = jnp.transpose(both, (1, 0, 2, 3))
    return both.reshape(-1, block.shape[1])


def rms_normed(rows_in, gain):
    values = rows_in.astype(jnp.float32)
    scaling = lax.rsqrt(jnp.mean(values * values, axis=-1, keepdims=True) + EPSILON)
    return (values * scaling * gain.astype(jnp.float32)).astype(jnp.bfloat16)


def rotate(values, positions):
    half_dim = values.shape[-1] // 2
    inverse = ROPE_BASE ** (-(jnp.arange(half_dim, dtype=jnp.float32) * (2.0 / values.shape[-1])))
    angles = positions.astype(jnp.float32)[:, None] * inverse[None, :]
    cos_part = jnp.cos(angles)[:, None, :]
    sin_part = jnp.sin(angles)[:, None, :]
    lower = values[..., :half_dim]
    higher = values[..., half_dim:]
    return jnp.concatenate(
        [lower * cos_part - higher * sin_part, higher * cos_part + lower * sin_part], axis=-1
    )


def ordered(mine, other, upper, along):
    first_half = jnp.where(upper, other, mine)
    second_half = jnp.where(upper, mine, other)
    return jnp.concatenate([first_half, second_half], axis=along)


def empty_state(row_count, groups, repeats):
    return (
        jnp.zeros((row_count, groups, repeats, HEAD_DIM), jnp.float32),
        jnp.full((row_count, groups, repeats), LOWEST, jnp.float32),
        jnp.zeros((row_count, groups, repeats), jnp.float32),
    )


def fold_keys(state, queries, query_pos, keys, values, key_pos, key_ok, widest):
    key_count = keys.shape[1]
    groups = queries.shape[1]
    block = math.gcd(key_count, widest)
    keys_split = keys.reshape(groups, HEAD_DIM, key_count)
    values_split = values.reshape(groups, HEAD_DIM, key_count)
    scale = HEAD_DIM ** (-0.5)

    def step(index, carry):
        accum, top_old, sum_old = carry
        start = index * block
        block_keys = lax.dynamic_slice_in_dim(keys_split, start, block, 2)
        block_values = lax.dynamic_slice_in_dim(values_split, start, block, 2)
        block_pos = lax.dynamic_slice_in_dim(key_pos, start, block, 0)
        block_ok = lax.dynamic_slice_in_dim(key_ok, start, block, 0)
        scores = (
            jnp.einsum("tgrd,gdk->tgrk", queries, block_keys, preferred_element_type=jnp.float32)
            * scale
        )
        allowed = (
            block_ok[None, :]
            & (block_pos[None, :] <= query_pos[:, None])
            & (query_pos[:, None] - block_pos[None, :] < WIN)
        )
        allowed = allowed[:, None, None, :]
        top_new = jnp.maximum(top_old, jnp.max(jnp.where(allowed, scores, LOWEST), axis=-1))
        weights = jnp.where(allowed, jnp.exp(scores - top_new[..., None]), 0.0)
        rescale = jnp.exp(top_old - top_new)
        sum_new = sum_old * rescale + jnp.sum(weights, axis=-1)
        mixed = jnp.einsum(
            "tgrk,gdk->tgrd",
            weights.astype(jnp.bfloat16),
            block_values,
            preferred_element_type=jnp.float32,
        )
        return (accum * rescale[..., None] + mixed, top_new, sum_new)

    return lax.fori_loop(0, key_count // block, step, state)


def exchange(block, axis, count, pairing):
    pieces = [block]
    for k in range(1, count):
        route = [(src, pairing(src, k)) for src in range(count)]
        route = [(dst, src) for src, dst in route]
        pieces.append(lax.ppermute(block, axis, [(pairing(d, k), d) for d in range(count)]))
    return jnp.stack(pieces)


def in_member_order(stacked, me, pairing, along):
    count = stacked.shape[0]
    parts = [stacked[pairing(me, q)] for q in range(count)]
    return jnp.concatenate(parts, axis=along)


def shift_pair(me, k):
    return (me - k) % 4


def xor_pair(me, k):
    return me ^ k


def shards(
    tokens_in,
    norm_gain,
    query_weight,
    key_weight,
    value_weight,
    out_weight,
    cache_keys,
    cache_values,
    cached_len,
    append_slot,
    shard_owner,
):
    n_narrow = lax.psum(1, "narrow")
    me_narrow = lax.axis_index("narrow")
    position = lax.axis_index(WIDE)
    request = position // GROUP
    place = position % GROUP

    def narrow_pair(me, k):
        return (me - k) % n_narrow

    def narrow_src(me, q):
        return (me - q) % n_narrow


    def group_pair(d, k):
        return d ^ k

    def group_route_pieces(block):
        pieces = [block]
        for k in range(1, GROUP):
            route = [(src, src ^ k) for src in range(lax.psum(1, WIDE))]
            pieces.append(lax.ppermute(block, WIDE, route))
        return jnp.stack(pieces)


    sizes = (query_weight.shape[1], key_weight.shape[1], value_weight.shape[1], out_weight.shape[1])
    joined = jnp.concatenate([query_weight, key_weight, value_weight, out_weight], axis=1)
    block_rows, joined_width = joined.shape
    dims = (lax.psum(1, "z"), lax.psum(1, "x"), lax.psum(1, "c"))
    gathered, cache_blocks, tok_pieces = gather_wide(
        joined.reshape(-1, 128), jnp.concatenate([cache_keys, cache_values], axis=0), tokens_in,
        *dims, n_narrow)
    whole = jnp.concatenate([tok_pieces[q] for q in range(n_narrow)], axis=1)
    all_weights = gathered.reshape(-1, joined_width)
    qkv = all_weights[:, : sum(sizes[:3])]
    out_rows = all_weights[:, sum(sizes[:3]) :]

    normed = rms_normed(whole, norm_gain)
    tok_rows = whole.shape[0]
    query_width = query_weight.shape[1]
    kv_width = key_weight.shape[1]
    local_heads = query_width // HEAD_DIM
    local_groups = kv_width // HEAD_DIM
    repeats = local_heads // local_groups
    qkv_sum = jnp.dot(normed, qkv, preferred_element_type=jnp.float32)
    query_sum = qkv_sum[:, :query_width]
    key_sum = qkv_sum[:, query_width : query_width + kv_width]
    value_sum = qkv_sum[:, query_width + kv_width :]
    length = cached_len[request]
    offset = append_slot[request]
    owner = shard_owner[request]
    query_pos = length + place * tok_rows + jnp.arange(tok_rows, dtype=jnp.int32)
    queries = rotate(query_sum.reshape(tok_rows, local_heads, HEAD_DIM), query_pos).astype(
        jnp.bfloat16
    )
    queries = queries.reshape(tok_rows, local_groups, repeats, HEAD_DIM)
    new_keys = (
        rotate(key_sum.reshape(tok_rows, local_groups, HEAD_DIM), query_pos)
        .astype(jnp.bfloat16)
        .reshape(tok_rows, kv_width)
    )
    new_values = value_sum.astype(jnp.bfloat16)
    shard_rows = cache_keys.shape[1]

    old_both = jnp.concatenate([cache_blocks[q] for q in range(GROUP)], axis=1)
    old_keys = old_both[:kv_width]
    old_values = old_both[kv_width:]
    new_both = jnp.concatenate([new_keys, new_values], axis=1)
    new_both = in_member_order(group_route_pieces(new_both), place, lambda me, q: me ^ q, 0)
    new_keys = new_both[:, :kv_width]
    new_values = new_both[:, kv_width:]

    slot_index = jnp.arange(old_keys.shape[1], dtype=jnp.int32)
    cycle = (slot_index // shard_rows - owner) % GROUP * shard_rows + slot_index % shard_rows
    cached_pos = (cycle - offset + length) % WIN
    state = fold_keys(
        empty_state(tok_rows, local_groups, repeats),
        queries,
        query_pos,
        old_keys,
        old_values,
        cached_pos,
        cached_pos < length,
        512,
    )
    key_cols = new_keys.T
    value_cols = new_values.T
    new_count = key_cols.shape[1]
    new_pos = length + jnp.arange(new_count, dtype=jnp.int32)
    state = fold_keys(
        state,
        queries,
        query_pos,
        key_cols,
        value_cols,
        new_pos,
        jnp.ones((new_count,), dtype=bool),
        512,
    )
    accum, top_score, total = state
    attended = (accum / total[..., None]).astype(jnp.bfloat16).reshape(tok_rows, query_width)
    all_heads = lax.all_gather(attended, "narrow", axis=1, tiled=True)
    update = jnp.dot(all_heads, out_rows, preferred_element_type=jnp.float32).astype(jnp.bfloat16)

    first = ((place - owner) % GROUP * shard_rows - offset) % WIN
    keys_ext = jnp.concatenate(
        [key_cols, jnp.zeros((kv_width, WIN - new_count), key_cols.dtype), key_cols,
         jnp.zeros((kv_width, shard_rows - new_count), key_cols.dtype)], axis=1)
    values_ext = jnp.concatenate(
        [value_cols, jnp.zeros((kv_width, WIN - new_count), value_cols.dtype), value_cols,
         jnp.zeros((kv_width, shard_rows - new_count), value_cols.dtype)], axis=1)
    spot = (first + jnp.arange(shard_rows, dtype=jnp.int32)) % WIN
    written = spot < new_count
    put_keys = jnp.where(written[None, :], lax.dynamic_slice_in_dim(keys_ext, first, shard_rows, 1), cache_keys)
    put_values = jnp.where(written[None, :], lax.dynamic_slice_in_dim(values_ext, first, shard_rows, 1), cache_values)
    return (update, put_keys, put_values)


def solution(mesh):
    devices = mesh.devices
    wide_devices = devices[:, 0]
    xs = sorted({d.coords[0] for d in wide_devices})
    cores = sorted({getattr(d, "core_on_chip", 0) for d in wide_devices})
    n_x, n_c = len(xs), len(cores)
    n_z = devices.shape[0] // (n_x * n_c)
    fine = Mesh(devices.reshape(n_z, n_x, n_c, devices.shape[1]), ("z", "x", "c", "narrow"))
    rows = P(WIDE, "narrow")
    cols = P("narrow", WIDE)
    in_specs = (rows, P(), rows, rows, rows, rows, cols, cols, P(), P(), P())
    out_specs = (rows, cols, cols)
    return jax.shard_map(shards, mesh=fine, in_specs=in_specs, out_specs=out_specs, check_vma=False)
```

```python
import functools
import math

import numpy as np
import jax
import jax.numpy as jnp
from jax import lax
from jax.experimental import pallas as pl
from jax.experimental.pallas import tpu as pltpu
from jax.sharding import Mesh, PartitionSpec as P

MESH_ID = pl.DeviceIdType.MESH

HEAD_DIM = 80
WIN = 4096
GROUP_BITS = 2
GROUP = 4


EPSILON = 1e-05
ROPE_BASE = 10000.0
LOWEST = -1e30


def from_partner(block, axis, bit):
    count = lax.psum(1, axis)
    route = []
    for low in range(count):
        high = low | 1 << bit
        if high != low and high < count:
            route += [(low, high), (high, low)]
    return lax.ppermute(block, axis, route)


WIDE = ("z", "x", "c")
RING_SUBS = 4


def gather_kernel(nz, nx, nc, nn, blk_ref, cache_ref, tok_ref, out_ref, cache_out, tok_out,
                  plane_send, plane_recv, ring_send, ring_recv, die_send, die_recv, local_sem,
                  cache_send, cache_recv, tok_send, tok_recv):
    z = lax.axis_index("z")
    x = lax.axis_index("x")
    c = lax.axis_index("c")
    n = lax.axis_index("narrow")
    per_plane = nx * nc
    me_xc = x * nc + c
    me = z * per_plane + me_xc
    place = lax.rem(x, 2) * nc + c
    x_base = x - lax.rem(x, 2)
    half = nz // 2
    step_dir = 1 - 2 * c
    dst_z = lax.rem(z + step_dir + nz, nz)
    src_z = lax.rem(z - step_dir + nz, nz)
    partner = (z, x, 1 - c, n)

    def plane_slot(pz):
        return out_ref.at[pl.ds(pl.multiple_of(pz * per_plane, per_plane), per_plane)]

    def group_dev(p):
        return (z, x_base + p // nc, lax.rem(p, nc), n)

    barrier = pltpu.get_barrier_semaphore()
    for k in range(1, per_plane):
        peer = lax.rem(me_xc + k, per_plane)
        pl.semaphore_signal(barrier, inc=1, device_id=(z, peer // nc, lax.rem(peer, nc), n), device_id_type=MESH_ID)
    for zz in (dst_z, src_z):
        pl.semaphore_signal(barrier, inc=1, device_id=(zz, x, c, n), device_id_type=MESH_ID)
    for k in range(1, nn):
        pl.semaphore_signal(barrier, inc=1, device_id=(z, x, c, lax.rem(n + k, nn)), device_id_type=MESH_ID)
    pl.semaphore_wait(barrier, per_plane + 1 + nn - 1)

    sends = []
    locals_ = []
    for src, dst in ((blk_ref, out_ref.at[me]), (cache_ref, cache_out.at[place]), (tok_ref, tok_out.at[n])):
        cp = pltpu.make_async_copy(src, dst, local_sem.at[len(locals_)])
        cp.start()
        locals_.append(cp)
    for k in range(1, per_plane):
        peer = lax.rem(me_xc + k, per_plane)
        cp = pltpu.make_async_remote_copy(
            src_ref=blk_ref, dst_ref=out_ref.at[me],
            send_sem=plane_send.at[k], recv_sem=plane_recv.at[k],
            device_id=(z, peer // nc, lax.rem(peer, nc), n), device_id_type=MESH_ID)
        cp.start()
        sends.append(cp)
    for k in range(1, per_plane):
        sender = lax.rem(me_xc - k + per_plane, per_plane)
        pltpu.make_async_remote_copy(
            src_ref=blk_ref, dst_ref=out_ref.at[z * per_plane + sender],
            send_sem=plane_send.at[k], recv_sem=plane_recv.at[k],
            device_id=(z, x, c, n), device_id_type=MESH_ID).wait_recv()
    locals_[0].wait()
    for k in range(1, 2 * nc):
        cp = pltpu.make_async_remote_copy(
            src_ref=cache_ref, dst_ref=cache_out.at[place],
            send_sem=cache_send.at[k], recv_sem=cache_recv.at[k],
            device_id=group_dev(place ^ k), device_id_type=MESH_ID)
        cp.start()
        sends.append(cp)
    for k in range(1, nn):
        cp = pltpu.make_async_remote_copy(
            src_ref=tok_ref, dst_ref=tok_out.at[n],
            send_sem=tok_send.at[k], recv_sem=tok_recv.at[k],
            device_id=(z, x, c, lax.rem(n + k, nn)), device_id_type=MESH_ID)
        cp.start()
        sends.append(cp)

    subs = RING_SUBS
    sub_len = per_plane // subs

    def sub_slot(pz, j):
        return out_ref.at[pl.ds(pl.multiple_of(pz * per_plane + j * sub_len, sub_len), sub_len)]

    def ring_copy(s, j, pz, device):
        return pltpu.make_async_remote_copy(
            src_ref=sub_slot(pz, j), dst_ref=sub_slot(pz, j),
            send_sem=ring_send.at[s - 1, j], recv_sem=ring_recv.at[s - 1, j],
            device_id=device, device_id_type=MESH_ID)

    def die_copy(s, j, pz):
        return pltpu.make_async_remote_copy(
            src_ref=sub_slot(pz, j), dst_ref=sub_slot(pz, j),
            send_sem=die_send.at[s - 1, j], recv_sem=die_recv.at[s - 1, j],
            device_id=partner, device_id_type=MESH_ID)

    for s in range(1, half + 1):
        send_z = lax.rem(z - step_dir * (s - 1) + 2 * nz, nz)
        for j in range(subs):
            if s > 1:
                ring_copy(s - 1, j, send_z, (src_z, x, c, n)).wait_recv()
                if s - 1 < half:
                    dp = die_copy(s - 1, j, send_z)
                    dp.start()
                    sends.append(dp)
            cp = ring_copy(s, j, send_z, (dst_z, x, c, n))
            cp.start()
            sends.append(cp)
    last_z = lax.rem(z - step_dir * half + 2 * nz, nz)
    for j in range(subs):
        ring_copy(half, j, last_z, (src_z, x, c, n)).wait_recv()
    for s in range(1, half):
        other_z = lax.rem(z + step_dir * s + 2 * nz, nz)
        for j in range(subs):
            die_copy(s, j, other_z).wait_recv()
    for k in range(1, 2 * nc):
        pltpu.make_async_remote_copy(
            src_ref=cache_ref, dst_ref=cache_out.at[place ^ k],
            send_sem=cache_send.at[k], recv_sem=cache_recv.at[k],
            device_id=(z, x, c, n), device_id_type=MESH_ID).wait_recv()
    for k in range(1, nn):
        pltpu.make_async_remote_copy(
            src_ref=tok_ref, dst_ref=tok_out.at[lax.rem(n - k + nn, nn)],
            send_sem=tok_send.at[k], recv_sem=tok_recv.at[k],
            device_id=(z, x, c, n), device_id_type=MESH_ID).wait_recv()
    for cp in locals_[1:]:
        cp.wait()
    for cp in sends:
        cp.wait_send()


def gather_wide(block, cache, tokens, nz, nx, nc, nn):
    count = nz * nx * nc
    half = nz // 2
    per_plane = nx * nc
    group = 2 * nc
    nbytes = block.size * block.dtype.itemsize
    return pl.pallas_call(
        functools.partial(gather_kernel, nz, nx, nc, nn),
        out_shape=(
            jax.ShapeDtypeStruct((count,) + block.shape, block.dtype),
            jax.ShapeDtypeStruct((group,) + cache.shape, cache.dtype),
            jax.ShapeDtypeStruct((nn,) + tokens.shape, tokens.dtype),
        ),
        in_specs=[pl.BlockSpec(memory_space=pl.ANY)] * 3,
        out_specs=[pl.BlockSpec(memory_space=pl.ANY)] * 3,
        scratch_shapes=[
            pltpu.SemaphoreType.DMA((per_plane,)),
            pltpu.SemaphoreType.DMA((per_plane,)),
            pltpu.SemaphoreType.DMA((half, RING_SUBS)),
            pltpu.SemaphoreType.DMA((half, RING_SUBS)),
            pltpu.SemaphoreType.DMA((half, RING_SUBS)),
            pltpu.SemaphoreType.DMA((half, RING_SUBS)),
            pltpu.SemaphoreType.DMA((3,)),
            pltpu.SemaphoreType.DMA((group,)),
            pltpu.SemaphoreType.DMA((group,)),
            pltpu.SemaphoreType.DMA((nn,)),
            pltpu.SemaphoreType.DMA((nn,)),
        ],
        compiler_params=pltpu.CompilerParams(collective_id=0, has_side_effects=True),
        cost_estimate=pl.CostEstimate(flops=0, transcendentals=0, bytes_accessed=2 * count * nbytes),
    )(block, cache, tokens)


def gather_rows(block):
    rows = block.shape[0]
    plane = lax.all_gather(block, ("z", "x"), axis=0, tiled=False)
    both = lax.all_gather(plane, "c", axis=0, tiled=False)
    both = jnp.transpose(both, (1, 0, 2, 3))
    return both.reshape(-1, block.shape[1])


def rms_normed(rows_in, gain):
    values = rows_in.astype(jnp.float32)
    scaling = lax.rsqrt(jnp.mean(values * values, axis=-1, keepdims=True) + EPSILON)
    return (values * scaling * gain.astype(jnp.float32)).astype(jnp.bfloat16)


def rotate(values, positions):
    half_dim = values.shape[-1] // 2
    inverse = ROPE_BASE ** (-(jnp.arange(half_dim, dtype=jnp.float32) * (2.0 / values.shape[-1])))
    angles = positions.astype(jnp.float32)[:, None] * inverse[None, :]
    cos_part = jnp.cos(angles)[:, None, :]
    sin_part = jnp.sin(angles)[:, None, :]
    lower = values[..., :half_dim]
    higher = values[..., half_dim:]
    return jnp.concatenate(
        [lower * cos_part - higher * sin_part, higher * cos_part + lower * sin_part], axis=-1
    )


def ordered(mine, other, upper, along):
    first_half = jnp.where(upper, other, mine)
    second_half = jnp.where(upper, mine, other)
    return jnp.concatenate([first_half, second_half], axis=along)


def empty_state(row_count, groups, repeats):
    return (
        jnp.zeros((row_count, groups, repeats, HEAD_DIM), jnp.float32),
        jnp.full((row_count, groups, repeats), LOWEST, jnp.float32),
        jnp.zeros((row_count, groups, repeats), jnp.float32),
    )


def fold_keys(state, queries, query_pos, keys, values, key_pos, key_ok, widest):
    key_count = keys.shape[1]
    groups = queries.shape[1]
    block = math.gcd(key_count, widest)
    keys_split = keys.reshape(groups, HEAD_DIM, key_count)
    values_split = values.reshape(groups, HEAD_DIM, key_count)
    scale = HEAD_DIM ** (-0.5)

    def step(index, carry):
        accum, top_old, sum_old = carry
        start = index * block
        block_keys = lax.dynamic_slice_in_dim(keys_split, start, block, 2)
        block_values = lax.dynamic_slice_in_dim(values_split, start, block, 2)
        block_pos = lax.dynamic_slice_in_dim(key_pos, start, block, 0)
        block_ok = lax.dynamic_slice_in_dim(key_ok, start, block, 0)
        scores = (
            jnp.einsum("tgrd,gdk->tgrk", queries, block_keys, preferred_element_type=jnp.float32)
            * scale
        )
        allowed = (
            block_ok[None, :]
            & (block_pos[None, :] <= query_pos[:, None])
            & (query_pos[:, None] - block_pos[None, :] < WIN)
        )
        allowed = allowed[:, None, None, :]
        top_new = jnp.maximum(top_old, jnp.max(jnp.where(allowed, scores, LOWEST), axis=-1))
        weights = jnp.where(allowed, jnp.exp(scores - top_new[..., None]), 0.0)
        rescale = jnp.exp(top_old - top_new)
        sum_new = sum_old * rescale + jnp.sum(weights, axis=-1)
        mixed = jnp.einsum(
            "tgrk,gdk->tgrd",
            weights.astype(jnp.bfloat16),
            block_values,
            preferred_element_type=jnp.float32,
        )
        return (accum * rescale[..., None] + mixed, top_new, sum_new)

    return lax.fori_loop(0, key_count // block, step, state)


def exchange(block, axis, count, pairing):
    pieces = [block]
    for k in range(1, count):
        route = [(src, pairing(src, k)) for src in range(count)]
        route = [(dst, src) for src, dst in route]
        pieces.append(lax.ppermute(block, axis, [(pairing(d, k), d) for d in range(count)]))
    return jnp.stack(pieces)


def in_member_order(stacked, me, pairing, along):
    count = stacked.shape[0]
    parts = [stacked[pairing(me, q)] for q in range(count)]
    return jnp.concatenate(parts, axis=along)


def shift_pair(me, k):
    return (me - k) % 4


def xor_pair(me, k):
    return me ^ k


def shards(
    tokens_in,
    norm_gain,
    query_weight,
    key_weight,
    value_weight,
    out_weight,
    cache_keys,
    cache_values,
    cached_len,
    append_slot,
    shard_owner,
):
    n_narrow = lax.psum(1, "narrow")
    me_narrow = lax.axis_index("narrow")
    position = lax.axis_index(WIDE)
    request = position // GROUP
    place = position % GROUP

    def narrow_pair(me, k):
        return (me - k) % n_narrow

    def narrow_src(me, q):
        return (me - q) % n_narrow


    def group_pair(d, k):
        return d ^ k

    def group_route_pieces(block):
        pieces = [block]
        for k in range(1, GROUP):
            route = [(src, src ^ k) for src in range(lax.psum(1, WIDE))]
            pieces.append(lax.ppermute(block, WIDE, route))
        return jnp.stack(pieces)


    sizes = (query_weight.shape[1], key_weight.shape[1], value_weight.shape[1], out_weight.shape[1])
    pad_cols = -sum(sizes) % 128
    joined = jnp.concatenate(
        [query_weight, key_weight, value_weight, out_weight,
         jnp.zeros((query_weight.shape[0], pad_cols), query_weight.dtype)], axis=1)
    block_rows, joined_width = joined.shape
    dims = (lax.psum(1, "z"), lax.psum(1, "x"), lax.psum(1, "c"))
    gathered, cache_blocks, tok_pieces = gather_wide(
        joined.reshape(-1, 128), jnp.concatenate([cache_keys, cache_values], axis=0), tokens_in,
        *dims, n_narrow)
    whole = jnp.concatenate([tok_pieces[q] for q in range(n_narrow)], axis=1)
    all_weights = gathered.reshape(-1, joined_width)
    qkv = all_weights[:, : sum(sizes[:3])]
    out_rows = all_weights[:, sum(sizes[:3]) : sum(sizes)]

    normed = rms_normed(whole, norm_gain)
    tok_rows = whole.shape[0]
    query_width = query_weight.shape[1]
    kv_width = key_weight.shape[1]
    local_heads = query_width // HEAD_DIM
    local_groups = kv_width // HEAD_DIM
    repeats = local_heads // local_groups
    qkv_sum = jnp.dot(normed, qkv, preferred_element_type=jnp.float32)
    query_sum = qkv_sum[:, :query_width]
    key_sum = qkv_sum[:, query_width : query_width + kv_width]
    value_sum = qkv_sum[:, query_width + kv_width :]
    length = cached_len[request]
    offset = append_slot[request]
    owner = shard_owner[request]
    query_pos = length + place * tok_rows + jnp.arange(tok_rows, dtype=jnp.int32)
    queries = rotate(query_sum.reshape(tok_rows, local_heads, HEAD_DIM), query_pos).astype(
        jnp.bfloat16
    )
    queries = queries.reshape(tok_rows, local_groups, repeats, HEAD_DIM)
    new_keys = (
        rotate(key_sum.reshape(tok_rows, local_groups, HEAD_DIM), query_pos)
        .astype(jnp.bfloat16)
        .reshape(tok_rows, kv_width)
    )
    new_values = value_sum.astype(jnp.bfloat16)
    shard_rows = cache_keys.shape[1]

    old_both = jnp.concatenate([cache_blocks[q] for q in range(GROUP)], axis=1)
    old_keys = old_both[:kv_width]
    old_values = old_both[kv_width:]
    new_both = jnp.concatenate([new_keys, new_values], axis=1)
    new_both = in_member_order(group_route_pieces(new_both), place, lambda me, q: me ^ q, 0)
    new_keys = new_both[:, :kv_width]
    new_values = new_both[:, kv_width:]

    slot_index = jnp.arange(old_keys.shape[1], dtype=jnp.int32)
    cycle = (slot_index // shard_rows - owner) % GROUP * shard_rows + slot_index % shard_rows
    cached_pos = (cycle - offset + length) % WIN
    state = fold_keys(
        empty_state(tok_rows, local_groups, repeats),
        queries,
        query_pos,
        old_keys,
        old_values,
        cached_pos,
        cached_pos < length,
        512,
    )
    key_cols = new_keys.T
    value_cols = new_values.T
    new_count = key_cols.shape[1]
    new_pos = length + jnp.arange(new_count, dtype=jnp.int32)
    state = fold_keys(
        state,
        queries,
        query_pos,
        key_cols,
        value_cols,
        new_pos,
        jnp.ones((new_count,), dtype=bool),
        512,
    )
    accum, top_score, total = state
    attended = (accum / total[..., None]).astype(jnp.bfloat16).reshape(tok_rows, query_width)
    all_heads = lax.all_gather(attended, "narrow", axis=1, tiled=True)
    update = jnp.dot(all_heads, out_rows, preferred_element_type=jnp.float32).astype(jnp.bfloat16)

    first = ((place - owner) % GROUP * shard_rows - offset) % WIN
    keys_ext = jnp.concatenate(
        [key_cols, jnp.zeros((kv_width, WIN - new_count), key_cols.dtype), key_cols,
         jnp.zeros((kv_width, shard_rows - new_count), key_cols.dtype)], axis=1)
    values_ext = jnp.concatenate(
        [value_cols, jnp.zeros((kv_width, WIN - new_count), value_cols.dtype), value_cols,
         jnp.zeros((kv_width, shard_rows - new_count), value_cols.dtype)], axis=1)
    spot = (first + jnp.arange(shard_rows, dtype=jnp.int32)) % WIN
    written = spot < new_count
    put_keys = jnp.where(written[None, :], lax.dynamic_slice_in_dim(keys_ext, first, shard_rows, 1), cache_keys)
    put_values = jnp.where(written[None, :], lax.dynamic_slice_in_dim(values_ext, first, shard_rows, 1), cache_values)
    return (update, put_keys, put_values)


def solution(mesh):
    devices = mesh.devices
    wide_devices = devices[:, 0]
    xs = sorted({d.coords[0] for d in wide_devices})
    cores = sorted({getattr(d, "core_on_chip", 0) for d in wide_devices})
    n_x, n_c = len(xs), len(cores)
    n_z = devices.shape[0] // (n_x * n_c)
    fine = Mesh(devices.reshape(n_z, n_x, n_c, devices.shape[1]), ("z", "x", "c", "narrow"))
    rows = P(WIDE, "narrow")
    cols = P("narrow", WIDE)
    in_specs = (rows, P(), rows, rows, rows, rows, cols, cols, P(), P(), P())
    out_specs = (rows, cols, cols)
    return jax.shard_map(shards, mesh=fine, in_specs=in_specs, out_specs=out_specs, check_vma=False)
```

```python
import functools
import math

import numpy as np
import jax
import jax.numpy as jnp
from jax import lax
from jax.experimental import pallas as pl
from jax.experimental.pallas import tpu as pltpu
from jax.sharding import Mesh, PartitionSpec as P

MESH_ID = pl.DeviceIdType.MESH

HEAD_DIM = 80
WIN = 4096
GROUP_BITS = 2
GROUP = 4


EPSILON = 1e-05
ROPE_BASE = 10000.0
LOWEST = -1e30


def from_partner(block, axis, bit):
    count = lax.psum(1, axis)
    route = []
    for low in range(count):
        high = low | 1 << bit
        if high != low and high < count:
            route += [(low, high), (high, low)]
    return lax.ppermute(block, axis, route)


WIDE = ("z", "x", "c")
RING_SUBS = 4


def gather_kernel(nz, nx, nc, nn, blk_ref, cache_ref, tok_ref, out_ref, cache_out, tok_out,
                  plane_send, plane_recv, ring_send, ring_recv, die_send, die_recv, local_sem,
                  cache_send, cache_recv, tok_send, tok_recv):
    z = lax.axis_index("z")
    x = lax.axis_index("x")
    c = lax.axis_index("c")
    n = lax.axis_index("narrow")
    per_plane = nx * nc
    me_xc = x * nc + c
    me = z * per_plane + me_xc
    place = lax.rem(x, 2) * nc + c
    x_base = x - lax.rem(x, 2)
    half = nz // 2
    step_dir = 1 - 2 * c
    dst_z = lax.rem(z + step_dir + nz, nz)
    src_z = lax.rem(z - step_dir + nz, nz)
    partner = (z, x, 1 - c, n)

    def plane_slot(pz):
        return out_ref.at[pl.ds(pl.multiple_of(pz * per_plane, per_plane), per_plane)]

    def group_dev(p):
        return (z, x_base + p // nc, lax.rem(p, nc), n)

    barrier = pltpu.get_barrier_semaphore()
    for k in range(1, per_plane):
        peer = lax.rem(me_xc + k, per_plane)
        pl.semaphore_signal(barrier, inc=1, device_id=(z, peer // nc, lax.rem(peer, nc), n), device_id_type=MESH_ID)
    for zz in (dst_z, src_z):
        pl.semaphore_signal(barrier, inc=1, device_id=(zz, x, c, n), device_id_type=MESH_ID)
    for k in range(1, nn):
        pl.semaphore_signal(barrier, inc=1, device_id=(z, x, c, lax.rem(n + k, nn)), device_id_type=MESH_ID)
    pl.semaphore_wait(barrier, per_plane + 1 + nn - 1)

    sends = []
    locals_ = []
    for src, dst in ((blk_ref, out_ref.at[me]), (cache_ref, cache_out.at[place]), (tok_ref, tok_out.at[n])):
        cp = pltpu.make_async_copy(src, dst, local_sem.at[len(locals_)])
        cp.start()
        locals_.append(cp)
    for k in range(1, per_plane):
        peer = lax.rem(me_xc + k, per_plane)
        cp = pltpu.make_async_remote_copy(
            src_ref=blk_ref, dst_ref=out_ref.at[me],
            send_sem=plane_send.at[k], recv_sem=plane_recv.at[k],
            device_id=(z, peer // nc, lax.rem(peer, nc), n), device_id_type=MESH_ID)
        cp.start()
        sends.append(cp)
    locals_[0].wait()
    for k in range(1, 2 * nc):
        cp = pltpu.make_async_remote_copy(
            src_ref=cache_ref, dst_ref=cache_out.at[place],
            send_sem=cache_send.at[k], recv_sem=cache_recv.at[k],
            device_id=group_dev(place ^ k), device_id_type=MESH_ID)
        cp.start()
        sends.append(cp)
    for k in range(1, nn):
        cp = pltpu.make_async_remote_copy(
            src_ref=tok_ref, dst_ref=tok_out.at[n],
            send_sem=tok_send.at[k], recv_sem=tok_recv.at[k],
            device_id=(z, x, c, lax.rem(n + k, nn)), device_id_type=MESH_ID)
        cp.start()
        sends.append(cp)

    subs = RING_SUBS
    sub_len = per_plane // subs

    def sub_slot(pz, j):
        return out_ref.at[pl.ds(pl.multiple_of(pz * per_plane + j * sub_len, sub_len), sub_len)]

    def ring_copy(s, j, pz, device):
        return pltpu.make_async_remote_copy(
            src_ref=sub_slot(pz, j), dst_ref=sub_slot(pz, j),
            send_sem=ring_send.at[s - 1, j], recv_sem=ring_recv.at[s - 1, j],
            device_id=device, device_id_type=MESH_ID)

    def die_copy(s, j, pz):
        return pltpu.make_async_remote_copy(
            src_ref=sub_slot(pz, j), dst_ref=sub_slot(pz, j),
            send_sem=die_send.at[s - 1, j], recv_sem=die_recv.at[s - 1, j],
            device_id=partner, device_id_type=MESH_ID)

    for s in range(1, half + 1):
        send_z = lax.rem(z - step_dir * (s - 1) + 2 * nz, nz)
        for j in range(subs):
            if s == 1:
                for b in range(sub_len):
                    held = j * sub_len + b
                    k = lax.rem(me_xc - held + per_plane, per_plane)

                    @pl.when(k != 0)
                    def _():
                        pltpu.make_async_remote_copy(
                            src_ref=blk_ref, dst_ref=out_ref.at[z * per_plane + held],
                            send_sem=plane_send.at[k], recv_sem=plane_recv.at[k],
                            device_id=(z, x, c, n), device_id_type=MESH_ID).wait_recv()
            if s > 1:
                ring_copy(s - 1, j, send_z, (src_z, x, c, n)).wait_recv()
                if s - 1 < half:
                    dp = die_copy(s - 1, j, send_z)
                    dp.start()
                    sends.append(dp)
            cp = ring_copy(s, j, send_z, (dst_z, x, c, n))
            cp.start()
            sends.append(cp)
    last_z = lax.rem(z - step_dir * half + 2 * nz, nz)
    for j in range(subs):
        ring_copy(half, j, last_z, (src_z, x, c, n)).wait_recv()
    for s in range(1, half):
        other_z = lax.rem(z + step_dir * s + 2 * nz, nz)
        for j in range(subs):
            die_copy(s, j, other_z).wait_recv()
    for k in range(1, 2 * nc):
        pltpu.make_async_remote_copy(
            src_ref=cache_ref, dst_ref=cache_out.at[place ^ k],
            send_sem=cache_send.at[k], recv_sem=cache_recv.at[k],
            device_id=(z, x, c, n), device_id_type=MESH_ID).wait_recv()
    for k in range(1, nn):
        pltpu.make_async_remote_copy(
            src_ref=tok_ref, dst_ref=tok_out.at[lax.rem(n - k + nn, nn)],
            send_sem=tok_send.at[k], recv_sem=tok_recv.at[k],
            device_id=(z, x, c, n), device_id_type=MESH_ID).wait_recv()
    for cp in locals_[1:]:
        cp.wait()
    for cp in sends:
        cp.wait_send()


def gather_wide(block, cache, tokens, nz, nx, nc, nn):
    count = nz * nx * nc
    half = nz // 2
    per_plane = nx * nc
    group = 2 * nc
    nbytes = block.size * block.dtype.itemsize
    return pl.pallas_call(
        functools.partial(gather_kernel, nz, nx, nc, nn),
        out_shape=(
            jax.ShapeDtypeStruct((count,) + block.shape, block.dtype),
            jax.ShapeDtypeStruct((group,) + cache.shape, cache.dtype),
            jax.ShapeDtypeStruct((nn,) + tokens.shape, tokens.dtype),
        ),
        in_specs=[pl.BlockSpec(memory_space=pl.ANY)] * 3,
        out_specs=[pl.BlockSpec(memory_space=pl.ANY)] * 3,
        scratch_shapes=[
            pltpu.SemaphoreType.DMA((per_plane,)),
            pltpu.SemaphoreType.DMA((per_plane,)),
            pltpu.SemaphoreType.DMA((half, RING_SUBS)),
            pltpu.SemaphoreType.DMA((half, RING_SUBS)),
            pltpu.SemaphoreType.DMA((half, RING_SUBS)),
            pltpu.SemaphoreType.DMA((half, RING_SUBS)),
            pltpu.SemaphoreType.DMA((3,)),
            pltpu.SemaphoreType.DMA((group,)),
            pltpu.SemaphoreType.DMA((group,)),
            pltpu.SemaphoreType.DMA((nn,)),
            pltpu.SemaphoreType.DMA((nn,)),
        ],
        compiler_params=pltpu.CompilerParams(collective_id=0, has_side_effects=True),
        cost_estimate=pl.CostEstimate(flops=0, transcendentals=0, bytes_accessed=2 * count * nbytes),
    )(block, cache, tokens)


def gather_rows(block):
    rows = block.shape[0]
    plane = lax.all_gather(block, ("z", "x"), axis=0, tiled=False)
    both = lax.all_gather(plane, "c", axis=0, tiled=False)
    both = jnp.transpose(both, (1, 0, 2, 3))
    return both.reshape(-1, block.shape[1])


def rms_normed(rows_in, gain):
    values = rows_in.astype(jnp.float32)
    scaling = lax.rsqrt(jnp.mean(values * values, axis=-1, keepdims=True) + EPSILON)
    return (values * scaling * gain.astype(jnp.float32)).astype(jnp.bfloat16)


def rotate(values, positions):
    half_dim = values.shape[-1] // 2
    inverse = ROPE_BASE ** (-(jnp.arange(half_dim, dtype=jnp.float32) * (2.0 / values.shape[-1])))
    angles = positions.astype(jnp.float32)[:, None] * inverse[None, :]
    cos_part = jnp.cos(angles)[:, None, :]
    sin_part = jnp.sin(angles)[:, None, :]
    lower = values[..., :half_dim]
    higher = values[..., half_dim:]
    return jnp.concatenate(
        [lower * cos_part - higher * sin_part, higher * cos_part + lower * sin_part], axis=-1
    )


def ordered(mine, other, upper, along):
    first_half = jnp.where(upper, other, mine)
    second_half = jnp.where(upper, mine, other)
    return jnp.concatenate([first_half, second_half], axis=along)


def empty_state(row_count, groups, repeats):
    return (
        jnp.zeros((row_count, groups, repeats, HEAD_DIM), jnp.float32),
        jnp.full((row_count, groups, repeats), LOWEST, jnp.float32),
        jnp.zeros((row_count, groups, repeats), jnp.float32),
    )


def fold_keys(state, queries, query_pos, keys, values, key_pos, key_ok, widest):
    key_count = keys.shape[1]
    groups = queries.shape[1]
    block = math.gcd(key_count, widest)
    keys_split = keys.reshape(groups, HEAD_DIM, key_count)
    values_split = values.reshape(groups, HEAD_DIM, key_count)
    scale = HEAD_DIM ** (-0.5)

    def step(index, carry):
        accum, top_old, sum_old = carry
        start = index * block
        block_keys = lax.dynamic_slice_in_dim(keys_split, start, block, 2)
        block_values = lax.dynamic_slice_in_dim(values_split, start, block, 2)
        block_pos = lax.dynamic_slice_in_dim(key_pos, start, block, 0)
        block_ok = lax.dynamic_slice_in_dim(key_ok, start, block, 0)
        scores = (
            jnp.einsum("tgrd,gdk->tgrk", queries, block_keys, preferred_element_type=jnp.float32)
            * scale
        )
        allowed = (
            block_ok[None, :]
            & (block_pos[None, :] <= query_pos[:, None])
            & (query_pos[:, None] - block_pos[None, :] < WIN)
        )
        allowed = allowed[:, None, None, :]
        top_new = jnp.maximum(top_old, jnp.max(jnp.where(allowed, scores, LOWEST), axis=-1))
        weights = jnp.where(allowed, jnp.exp(scores - top_new[..., None]), 0.0)
        rescale = jnp.exp(top_old - top_new)
        sum_new = sum_old * rescale + jnp.sum(weights, axis=-1)
        mixed = jnp.einsum(
            "tgrk,gdk->tgrd",
            weights.astype(jnp.bfloat16),
            block_values,
            preferred_element_type=jnp.float32,
        )
        return (accum * rescale[..., None] + mixed, top_new, sum_new)

    return lax.fori_loop(0, key_count // block, step, state)


def exchange(block, axis, count, pairing):
    pieces = [block]
    for k in range(1, count):
        route = [(src, pairing(src, k)) for src in range(count)]
        route = [(dst, src) for src, dst in route]
        pieces.append(lax.ppermute(block, axis, [(pairing(d, k), d) for d in range(count)]))
    return jnp.stack(pieces)


def in_member_order(stacked, me, pairing, along):
    count = stacked.shape[0]
    parts = [stacked[pairing(me, q)] for q in range(count)]
    return jnp.concatenate(parts, axis=along)


def shift_pair(me, k):
    return (me - k) % 4


def xor_pair(me, k):
    return me ^ k


def shards(
    tokens_in,
    norm_gain,
    query_weight,
    key_weight,
    value_weight,
    out_weight,
    cache_keys,
    cache_values,
    cached_len,
    append_slot,
    shard_owner,
):
    n_narrow = lax.psum(1, "narrow")
    me_narrow = lax.axis_index("narrow")
    position = lax.axis_index(WIDE)
    request = position // GROUP
    place = position % GROUP

    def narrow_pair(me, k):
        return (me - k) % n_narrow

    def narrow_src(me, q):
        return (me - q) % n_narrow


    def group_pair(d, k):
        return d ^ k

    def group_route_pieces(block):
        pieces = [block]
        for k in range(1, GROUP):
            route = [(src, src ^ k) for src in range(lax.psum(1, WIDE))]
            pieces.append(lax.ppermute(block, WIDE, route))
        return jnp.stack(pieces)


    sizes = (query_weight.shape[1], key_weight.shape[1], value_weight.shape[1], out_weight.shape[1])
    joined = jnp.concatenate([query_weight, key_weight, value_weight, out_weight], axis=1)
    block_rows, joined_width = joined.shape
    dims = (lax.psum(1, "z"), lax.psum(1, "x"), lax.psum(1, "c"))
    gathered, cache_blocks, tok_pieces = gather_wide(
        joined.reshape(-1, 128), jnp.concatenate([cache_keys, cache_values], axis=0), tokens_in,
        *dims, n_narrow)
    whole = jnp.concatenate([tok_pieces[q] for q in range(n_narrow)], axis=1)
    all_weights = gathered.reshape(-1, joined_width)
    qkv = all_weights[:, : sum(sizes[:3])]
    out_rows = all_weights[:, sum(sizes[:3]) :]

    normed = rms_normed(whole, norm_gain)
    tok_rows = whole.shape[0]
    query_width = query_weight.shape[1]
    kv_width = key_weight.shape[1]
    local_heads = query_width // HEAD_DIM
    local_groups = kv_width // HEAD_DIM
    repeats = local_heads // local_groups
    qkv_sum = jnp.dot(normed, qkv, preferred_element_type=jnp.float32)
    query_sum = qkv_sum[:, :query_width]
    key_sum = qkv_sum[:, query_width : query_width + kv_width]
    value_sum = qkv_sum[:, query_width + kv_width :]
    length = cached_len[request]
    offset = append_slot[request]
    owner = shard_owner[request]
    query_pos = length + place * tok_rows + jnp.arange(tok_rows, dtype=jnp.int32)
    queries = rotate(query_sum.reshape(tok_rows, local_heads, HEAD_DIM), query_pos).astype(
        jnp.bfloat16
    )
    queries = queries.reshape(tok_rows, local_groups, repeats, HEAD_DIM)
    new_keys = (
        rotate(key_sum.reshape(tok_rows, local_groups, HEAD_DIM), query_pos)
        .astype(jnp.bfloat16)
        .reshape(tok_rows, kv_width)
    )
    new_values = value_sum.astype(jnp.bfloat16)
    shard_rows = cache_keys.shape[1]

    old_both = jnp.concatenate([cache_blocks[q] for q in range(GROUP)], axis=1)
    old_keys = old_both[:kv_width]
    old_values = old_both[kv_width:]
    new_both = jnp.concatenate([new_keys, new_values], axis=1)
    new_both = in_member_order(group_route_pieces(new_both), place, lambda me, q: me ^ q, 0)
    new_keys = new_both[:, :kv_width]
    new_values = new_both[:, kv_width:]

    slot_index = jnp.arange(old_keys.shape[1], dtype=jnp.int32)
    cycle = (slot_index // shard_rows - owner) % GROUP * shard_rows + slot_index % shard_rows
    cached_pos = (cycle - offset + length) % WIN
    state = fold_keys(
        empty_state(tok_rows, local_groups, repeats),
        queries,
        query_pos,
        old_keys,
        old_values,
        cached_pos,
        cached_pos < length,
        512,
    )
    key_cols = new_keys.T
    value_cols = new_values.T
    new_count = key_cols.shape[1]
    new_pos = length + jnp.arange(new_count, dtype=jnp.int32)
    state = fold_keys(
        state,
        queries,
        query_pos,
        key_cols,
        value_cols,
        new_pos,
        jnp.ones((new_count,), dtype=bool),
        512,
    )
    accum, top_score, total = state
    attended = (accum / total[..., None]).astype(jnp.bfloat16).reshape(tok_rows, query_width)
    all_heads = lax.all_gather(attended, "narrow", axis=1, tiled=True)
    update = jnp.dot(all_heads, out_rows, preferred_element_type=jnp.float32).astype(jnp.bfloat16)

    first = ((place - owner) % GROUP * shard_rows - offset) % WIN
    keys_ext = jnp.concatenate(
        [key_cols, jnp.zeros((kv_width, WIN - new_count), key_cols.dtype), key_cols,
         jnp.zeros((kv_width, shard_rows - new_count), key_cols.dtype)], axis=1)
    values_ext = jnp.concatenate(
        [value_cols, jnp.zeros((kv_width, WIN - new_count), value_cols.dtype), value_cols,
         jnp.zeros((kv_width, shard_rows - new_count), value_cols.dtype)], axis=1)
    spot = (first + jnp.arange(shard_rows, dtype=jnp.int32)) % WIN
    written = spot < new_count
    put_keys = jnp.where(written[None, :], lax.dynamic_slice_in_dim(keys_ext, first, shard_rows, 1), cache_keys)
    put_values = jnp.where(written[None, :], lax.dynamic_slice_in_dim(values_ext, first, shard_rows, 1), cache_values)
    return (update, put_keys, put_values)


def solution(mesh):
    devices = mesh.devices
    wide_devices = devices[:, 0]
    xs = sorted({d.coords[0] for d in wide_devices})
    cores = sorted({getattr(d, "core_on_chip", 0) for d in wide_devices})
    n_x, n_c = len(xs), len(cores)
    n_z = devices.shape[0] // (n_x * n_c)
    fine = Mesh(devices.reshape(n_z, n_x, n_c, devices.shape[1]), ("z", "x", "c", "narrow"))
    rows = P(WIDE, "narrow")
    cols = P("narrow", WIDE)
    in_specs = (rows, P(), rows, rows, rows, rows, cols, cols, P(), P(), P())
    out_specs = (rows, cols, cols)
    return jax.shard_map(shards, mesh=fine, in_specs=in_specs, out_specs=out_specs, check_vma=False)
```

```python
import functools
import math

import numpy as np
import jax
import jax.numpy as jnp
from jax import lax
from jax.experimental import pallas as pl
from jax.experimental.pallas import tpu as pltpu
from jax.sharding import Mesh, PartitionSpec as P

MESH_ID = pl.DeviceIdType.MESH

HEAD_DIM = 80
WIN = 4096
GROUP_BITS = 2
GROUP = 4


EPSILON = 1e-05
ROPE_BASE = 10000.0
LOWEST = -1e30


def from_partner(block, axis, bit):
    count = lax.psum(1, axis)
    route = []
    for low in range(count):
        high = low | 1 << bit
        if high != low and high < count:
            route += [(low, high), (high, low)]
    return lax.ppermute(block, axis, route)


WIDE = ("z", "x", "c")
RING_SUBS = 8


def gather_kernel(nz, nx, nc, nn, blk_ref, cache_ref, tok_ref, out_ref, cache_out, tok_out,
                  plane_send, plane_recv, ring_send, ring_recv, die_send, die_recv, local_sem,
                  cache_send, cache_recv, tok_send, tok_recv):
    z = lax.axis_index("z")
    x = lax.axis_index("x")
    c = lax.axis_index("c")
    n = lax.axis_index("narrow")
    per_plane = nx * nc
    me_xc = x * nc + c
    me = z * per_plane + me_xc
    place = lax.rem(x, 2) * nc + c
    x_base = x - lax.rem(x, 2)
    half = nz // 2
    step_dir = 1 - 2 * c
    dst_z = lax.rem(z + step_dir + nz, nz)
    src_z = lax.rem(z - step_dir + nz, nz)
    partner = (z, x, 1 - c, n)

    def plane_slot(pz):
        return out_ref.at[pl.ds(pl.multiple_of(pz * per_plane, per_plane), per_plane)]

    def group_dev(p):
        return (z, x_base + p // nc, lax.rem(p, nc), n)

    barrier = pltpu.get_barrier_semaphore()
    for k in range(1, per_plane):
        peer = lax.rem(me_xc + k, per_plane)
        pl.semaphore_signal(barrier, inc=1, device_id=(z, peer // nc, lax.rem(peer, nc), n), device_id_type=MESH_ID)
    for zz in (dst_z, src_z):
        pl.semaphore_signal(barrier, inc=1, device_id=(zz, x, c, n), device_id_type=MESH_ID)
    for k in range(1, nn):
        pl.semaphore_signal(barrier, inc=1, device_id=(z, x, c, lax.rem(n + k, nn)), device_id_type=MESH_ID)
    pl.semaphore_wait(barrier, per_plane + 1 + nn - 1)

    sends = []
    locals_ = []
    for src, dst in ((blk_ref, out_ref.at[me]), (cache_ref, cache_out.at[place]), (tok_ref, tok_out.at[n])):
        cp = pltpu.make_async_copy(src, dst, local_sem.at[len(locals_)])
        cp.start()
        locals_.append(cp)
    for k in range(1, per_plane):
        peer = lax.rem(me_xc + k, per_plane)
        cp = pltpu.make_async_remote_copy(
            src_ref=blk_ref, dst_ref=out_ref.at[me],
            send_sem=plane_send.at[k], recv_sem=plane_recv.at[k],
            device_id=(z, peer // nc, lax.rem(peer, nc), n), device_id_type=MESH_ID)
        cp.start()
        sends.append(cp)
    locals_[0].wait()
    for k in range(1, 2 * nc):
        cp = pltpu.make_async_remote_copy(
            src_ref=cache_ref, dst_ref=cache_out.at[place],
            send_sem=cache_send.at[k], recv_sem=cache_recv.at[k],
            device_id=group_dev(place ^ k), device_id_type=MESH_ID)
        cp.start()
        sends.append(cp)
    for k in range(1, nn):
        cp = pltpu.make_async_remote_copy(
            src_ref=tok_ref, dst_ref=tok_out.at[n],
            send_sem=tok_send.at[k], recv_sem=tok_recv.at[k],
            device_id=(z, x, c, lax.rem(n + k, nn)), device_id_type=MESH_ID)
        cp.start()
        sends.append(cp)

    subs = RING_SUBS
    sub_len = per_plane // subs

    def sub_slot(pz, j):
        return out_ref.at[pl.ds(pl.multiple_of(pz * per_plane + j * sub_len, sub_len), sub_len)]

    def ring_copy(s, j, pz, device):
        return pltpu.make_async_remote_copy(
            src_ref=sub_slot(pz, j), dst_ref=sub_slot(pz, j),
            send_sem=ring_send.at[s - 1, j], recv_sem=ring_recv.at[s - 1, j],
            device_id=device, device_id_type=MESH_ID)

    def die_copy(s, j, pz):
        return pltpu.make_async_remote_copy(
            src_ref=sub_slot(pz, j), dst_ref=sub_slot(pz, j),
            send_sem=die_send.at[s - 1, j], recv_sem=die_recv.at[s - 1, j],
            device_id=partner, device_id_type=MESH_ID)

    for s in range(1, half + 1):
        send_z = lax.rem(z - step_dir * (s - 1) + 2 * nz, nz)
        for j in range(subs):
            if s == 1:
                for b in range(sub_len):
                    held = j * sub_len + b
                    k = lax.rem(me_xc - held + per_plane, per_plane)

                    @pl.when(k != 0)
                    def _():
                        pltpu.make_async_remote_copy(
                            src_ref=blk_ref, dst_ref=out_ref.at[z * per_plane + held],
                            send_sem=plane_send.at[k], recv_sem=plane_recv.at[k],
                            device_id=(z, x, c, n), device_id_type=MESH_ID).wait_recv()
            if s > 1:
                ring_copy(s - 1, j, send_z, (src_z, x, c, n)).wait_recv()
                if s - 1 < half:
                    dp = die_copy(s - 1, j, send_z)
                    dp.start()
                    sends.append(dp)
            cp = ring_copy(s, j, send_z, (dst_z, x, c, n))
            cp.start()
            sends.append(cp)
    last_z = lax.rem(z - step_dir * half + 2 * nz, nz)
    for j in range(subs):
        ring_copy(half, j, last_z, (src_z, x, c, n)).wait_recv()
    for s in range(1, half):
        other_z = lax.rem(z + step_dir * s + 2 * nz, nz)
        for j in range(subs):
            die_copy(s, j, other_z).wait_recv()
    for k in range(1, 2 * nc):
        pltpu.make_async_remote_copy(
            src_ref=cache_ref, dst_ref=cache_out.at[place ^ k],
            send_sem=cache_send.at[k], recv_sem=cache_recv.at[k],
            device_id=(z, x, c, n), device_id_type=MESH_ID).wait_recv()
    for k in range(1, nn):
        pltpu.make_async_remote_copy(
            src_ref=tok_ref, dst_ref=tok_out.at[lax.rem(n - k + nn, nn)],
            send_sem=tok_send.at[k], recv_sem=tok_recv.at[k],
            device_id=(z, x, c, n), device_id_type=MESH_ID).wait_recv()
    for cp in locals_[1:]:
        cp.wait()
    for cp in sends:
        cp.wait_send()


def gather_wide(block, cache, tokens, nz, nx, nc, nn):
    count = nz * nx * nc
    half = nz // 2
    per_plane = nx * nc
    group = 2 * nc
    nbytes = block.size * block.dtype.itemsize
    return pl.pallas_call(
        functools.partial(gather_kernel, nz, nx, nc, nn),
        out_shape=(
            jax.ShapeDtypeStruct((count,) + block.shape, block.dtype),
            jax.ShapeDtypeStruct((group,) + cache.shape, cache.dtype),
            jax.ShapeDtypeStruct((nn,) + tokens.shape, tokens.dtype),
        ),
        in_specs=[pl.BlockSpec(memory_space=pl.ANY)] * 3,
        out_specs=[pl.BlockSpec(memory_space=pl.ANY)] * 3,
        scratch_shapes=[
            pltpu.SemaphoreType.DMA((per_plane,)),
            pltpu.SemaphoreType.DMA((per_plane,)),
            pltpu.SemaphoreType.DMA((half, RING_SUBS)),
            pltpu.SemaphoreType.DMA((half, RING_SUBS)),
            pltpu.SemaphoreType.DMA((half, RING_SUBS)),
            pltpu.SemaphoreType.DMA((half, RING_SUBS)),
            pltpu.SemaphoreType.DMA((3,)),
            pltpu.SemaphoreType.DMA((group,)),
            pltpu.SemaphoreType.DMA((group,)),
            pltpu.SemaphoreType.DMA((nn,)),
            pltpu.SemaphoreType.DMA((nn,)),
        ],
        compiler_params=pltpu.CompilerParams(collective_id=0, has_side_effects=True),
        cost_estimate=pl.CostEstimate(flops=0, transcendentals=0, bytes_accessed=2 * count * nbytes),
    )(block, cache, tokens)


def gather_rows(block):
    rows = block.shape[0]
    plane = lax.all_gather(block, ("z", "x"), axis=0, tiled=False)
    both = lax.all_gather(plane, "c", axis=0, tiled=False)
    both = jnp.transpose(both, (1, 0, 2, 3))
    return both.reshape(-1, block.shape[1])


def rms_normed(rows_in, gain):
    values = rows_in.astype(jnp.float32)
    scaling = lax.rsqrt(jnp.mean(values * values, axis=-1, keepdims=True) + EPSILON)
    return (values * scaling * gain.astype(jnp.float32)).astype(jnp.bfloat16)


def rotate(values, positions):
    half_dim = values.shape[-1] // 2
    inverse = ROPE_BASE ** (-(jnp.arange(half_dim, dtype=jnp.float32) * (2.0 / values.shape[-1])))
    angles = positions.astype(jnp.float32)[:, None] * inverse[None, :]
    cos_part = jnp.cos(angles)[:, None, :]
    sin_part = jnp.sin(angles)[:, None, :]
    lower = values[..., :half_dim]
    higher = values[..., half_dim:]
    return jnp.concatenate(
        [lower * cos_part - higher * sin_part, higher * cos_part + lower * sin_part], axis=-1
    )


def ordered(mine, other, upper, along):
    first_half = jnp.where(upper, other, mine)
    second_half = jnp.where(upper, mine, other)
    return jnp.concatenate([first_half, second_half], axis=along)


def empty_state(row_count, groups, repeats):
    return (
        jnp.zeros((row_count, groups, repeats, HEAD_DIM), jnp.float32),
        jnp.full((row_count, groups, repeats), LOWEST, jnp.float32),
        jnp.zeros((row_count, groups, repeats), jnp.float32),
    )


def fold_keys(state, queries, query_pos, keys, values, key_pos, key_ok, widest):
    key_count = keys.shape[1]
    groups = queries.shape[1]
    block = math.gcd(key_count, widest)
    keys_split = keys.reshape(groups, HEAD_DIM, key_count)
    values_split = values.reshape(groups, HEAD_DIM, key_count)
    scale = HEAD_DIM ** (-0.5)

    def step(index, carry):
        accum, top_old, sum_old = carry
        start = index * block
        block_keys = lax.dynamic_slice_in_dim(keys_split, start, block, 2)
        block_values = lax.dynamic_slice_in_dim(values_split, start, block, 2)
        block_pos = lax.dynamic_slice_in_dim(key_pos, start, block, 0)
        block_ok = lax.dynamic_slice_in_dim(key_ok, start, block, 0)
        scores = (
            jnp.einsum("tgrd,gdk->tgrk", queries, block_keys, preferred_element_type=jnp.float32)
            * scale
        )
        allowed = (
            block_ok[None, :]
            & (block_pos[None, :] <= query_pos[:, None])
            & (query_pos[:, None] - block_pos[None, :] < WIN)
        )
        allowed = allowed[:, None, None, :]
        top_new = jnp.maximum(top_old, jnp.max(jnp.where(allowed, scores, LOWEST), axis=-1))
        weights = jnp.where(allowed, jnp.exp(scores - top_new[..., None]), 0.0)
        rescale = jnp.exp(top_old - top_new)
        sum_new = sum_old * rescale + jnp.sum(weights, axis=-1)
        mixed = jnp.einsum(
            "tgrk,gdk->tgrd",
            weights.astype(jnp.bfloat16),
            block_values,
            preferred_element_type=jnp.float32,
        )
        return (accum * rescale[..., None] + mixed, top_new, sum_new)

    return lax.fori_loop(0, key_count // block, step, state)


def exchange(block, axis, count, pairing):
    pieces = [block]
    for k in range(1, count):
        route = [(src, pairing(src, k)) for src in range(count)]
        route = [(dst, src) for src, dst in route]
        pieces.append(lax.ppermute(block, axis, [(pairing(d, k), d) for d in range(count)]))
    return jnp.stack(pieces)


def in_member_order(stacked, me, pairing, along):
    count = stacked.shape[0]
    parts = [stacked[pairing(me, q)] for q in range(count)]
    return jnp.concatenate(parts, axis=along)


def shift_pair(me, k):
    return (me - k) % 4


def xor_pair(me, k):
    return me ^ k


def shards(
    tokens_in,
    norm_gain,
    query_weight,
    key_weight,
    value_weight,
    out_weight,
    cache_keys,
    cache_values,
    cached_len,
    append_slot,
    shard_owner,
):
    n_narrow = lax.psum(1, "narrow")
    me_narrow = lax.axis_index("narrow")
    position = lax.axis_index(WIDE)
    request = position // GROUP
    place = position % GROUP

    def narrow_pair(me, k):
        return (me - k) % n_narrow

    def narrow_src(me, q):
        return (me - q) % n_narrow


    def group_pair(d, k):
        return d ^ k

    def group_route_pieces(block):
        pieces = [block]
        for k in range(1, GROUP):
            route = [(src, src ^ k) for src in range(lax.psum(1, WIDE))]
            pieces.append(lax.ppermute(block, WIDE, route))
        return jnp.stack(pieces)


    sizes = (query_weight.shape[1], key_weight.shape[1], value_weight.shape[1], out_weight.shape[1])
    joined = jnp.concatenate([query_weight, key_weight, value_weight, out_weight], axis=1)
    block_rows, joined_width = joined.shape
    dims = (lax.psum(1, "z"), lax.psum(1, "x"), lax.psum(1, "c"))
    gathered, cache_blocks, tok_pieces = gather_wide(
        joined.reshape(-1, 128), jnp.concatenate([cache_keys, cache_values], axis=0), tokens_in,
        *dims, n_narrow)
    whole = jnp.concatenate([tok_pieces[q] for q in range(n_narrow)], axis=1)
    all_weights = gathered.reshape(-1, joined_width)
    qkv = all_weights[:, : sum(sizes[:3])]
    out_rows = all_weights[:, sum(sizes[:3]) :]

    normed = rms_normed(whole, norm_gain)
    tok_rows = whole.shape[0]
    query_width = query_weight.shape[1]
    kv_width = key_weight.shape[1]
    local_heads = query_width // HEAD_DIM
    local_groups = kv_width // HEAD_DIM
    repeats = local_heads // local_groups
    qkv_sum = jnp.dot(normed, qkv, preferred_element_type=jnp.float32)
    query_sum = qkv_sum[:, :query_width]
    key_sum = qkv_sum[:, query_width : query_width + kv_width]
    value_sum = qkv_sum[:, query_width + kv_width :]
    length = cached_len[request]
    offset = append_slot[request]
    owner = shard_owner[request]
    query_pos = length + place * tok_rows + jnp.arange(tok_rows, dtype=jnp.int32)
    queries = rotate(query_sum.reshape(tok_rows, local_heads, HEAD_DIM), query_pos).astype(
        jnp.bfloat16
    )
    queries = queries.reshape(tok_rows, local_groups, repeats, HEAD_DIM)
    new_keys = (
        rotate(key_sum.reshape(tok_rows, local_groups, HEAD_DIM), query_pos)
        .astype(jnp.bfloat16)
        .reshape(tok_rows, kv_width)
    )
    new_values = value_sum.astype(jnp.bfloat16)
    shard_rows = cache_keys.shape[1]

    old_both = jnp.concatenate([cache_blocks[q] for q in range(GROUP)], axis=1)
    old_keys = old_both[:kv_width]
    old_values = old_both[kv_width:]
    new_both = jnp.concatenate([new_keys, new_values], axis=1)
    new_both = in_member_order(group_route_pieces(new_both), place, lambda me, q: me ^ q, 0)
    new_keys = new_both[:, :kv_width]
    new_values = new_both[:, kv_width:]

    slot_index = jnp.arange(old_keys.shape[1], dtype=jnp.int32)
    cycle = (slot_index // shard_rows - owner) % GROUP * shard_rows + slot_index % shard_rows
    cached_pos = (cycle - offset + length) % WIN
    state = fold_keys(
        empty_state(tok_rows, local_groups, repeats),
        queries,
        query_pos,
        old_keys,
        old_values,
        cached_pos,
        cached_pos < length,
        512,
    )
    key_cols = new_keys.T
    value_cols = new_values.T
    new_count = key_cols.shape[1]
    new_pos = length + jnp.arange(new_count, dtype=jnp.int32)
    state = fold_keys(
        state,
        queries,
        query_pos,
        key_cols,
        value_cols,
        new_pos,
        jnp.ones((new_count,), dtype=bool),
        512,
    )
    accum, top_score, total = state
    attended = (accum / total[..., None]).astype(jnp.bfloat16).reshape(tok_rows, query_width)
    all_heads = lax.all_gather(attended, "narrow", axis=1, tiled=True)
    update = jnp.dot(all_heads, out_rows, preferred_element_type=jnp.float32).astype(jnp.bfloat16)

    first = ((place - owner) % GROUP * shard_rows - offset) % WIN
    keys_ext = jnp.concatenate(
        [key_cols, jnp.zeros((kv_width, WIN - new_count), key_cols.dtype), key_cols,
         jnp.zeros((kv_width, shard_rows - new_count), key_cols.dtype)], axis=1)
    values_ext = jnp.concatenate(
        [value_cols, jnp.zeros((kv_width, WIN - new_count), value_cols.dtype), value_cols,
         jnp.zeros((kv_width, shard_rows - new_count), value_cols.dtype)], axis=1)
    spot = (first + jnp.arange(shard_rows, dtype=jnp.int32)) % WIN
    written = spot < new_count
    put_keys = jnp.where(written[None, :], lax.dynamic_slice_in_dim(keys_ext, first, shard_rows, 1), cache_keys)
    put_values = jnp.where(written[None, :], lax.dynamic_slice_in_dim(values_ext, first, shard_rows, 1), cache_values)
    return (update, put_keys, put_values)


def solution(mesh):
    devices = mesh.devices
    wide_devices = devices[:, 0]
    xs = sorted({d.coords[0] for d in wide_devices})
    cores = sorted({getattr(d, "core_on_chip", 0) for d in wide_devices})
    n_x, n_c = len(xs), len(cores)
    n_z = devices.shape[0] // (n_x * n_c)
    fine = Mesh(devices.reshape(n_z, n_x, n_c, devices.shape[1]), ("z", "x", "c", "narrow"))
    rows = P(WIDE, "narrow")
    cols = P("narrow", WIDE)
    in_specs = (rows, P(), rows, rows, rows, rows, cols, cols, P(), P(), P())
    out_specs = (rows, cols, cols)
    return jax.shard_map(shards, mesh=fine, in_specs=in_specs, out_specs=out_specs, check_vma=False)
```

```python
import functools
import math

import numpy as np
import jax
import jax.numpy as jnp
from jax import lax
from jax.experimental import pallas as pl
from jax.experimental.pallas import tpu as pltpu
from jax.sharding import Mesh, PartitionSpec as P

MESH_ID = pl.DeviceIdType.MESH

HEAD_DIM = 80
WIN = 4096
GROUP_BITS = 2
GROUP = 4


EPSILON = 1e-05
ROPE_BASE = 10000.0
LOWEST = -1e30


def from_partner(block, axis, bit):
    count = lax.psum(1, axis)
    route = []
    for low in range(count):
        high = low | 1 << bit
        if high != low and high < count:
            route += [(low, high), (high, low)]
    return lax.ppermute(block, axis, route)


WIDE = ("z", "x", "c")
RING_SUBS = 4


def gather_kernel(nz, nx, nc, nn, blk_ref, cache_ref, tok_ref, out_ref, cache_out, tok_out,
                  plane_send, plane_recv, ring_send, ring_recv, die_send, die_recv, local_sem,
                  cache_send, cache_recv, tok_send, tok_recv):
    z = lax.axis_index("z")
    x = lax.axis_index("x")
    c = lax.axis_index("c")
    n = lax.axis_index("narrow")
    per_plane = nx * nc
    me_xc = x * nc + c
    me = z * per_plane + me_xc
    place = lax.rem(x, 2) * nc + c
    x_base = x - lax.rem(x, 2)
    half = nz // 2
    step_dir = 1 - 2 * c
    dst_z = lax.rem(z + step_dir + nz, nz)
    src_z = lax.rem(z - step_dir + nz, nz)
    partner = (z, x, 1 - c, n)

    def plane_slot(pz):
        return out_ref.at[pl.ds(pl.multiple_of(pz * per_plane, per_plane), per_plane)]

    def group_dev(p):
        return (z, x_base + p // nc, lax.rem(p, nc), n)

    barrier = pltpu.get_barrier_semaphore()
    for k in range(1, per_plane):
        peer = lax.rem(me_xc + k, per_plane)
        pl.semaphore_signal(barrier, inc=1, device_id=(z, peer // nc, lax.rem(peer, nc), n), device_id_type=MESH_ID)
    for zz in (dst_z, src_z):
        pl.semaphore_signal(barrier, inc=1, device_id=(zz, x, c, n), device_id_type=MESH_ID)
    for k in range(1, nn):
        pl.semaphore_signal(barrier, inc=1, device_id=(z, x, c, lax.rem(n + k, nn)), device_id_type=MESH_ID)
    pl.semaphore_wait(barrier, per_plane + 1 + nn - 1)

    sends = []
    locals_ = []
    for src, dst in ((blk_ref, out_ref.at[me]), (cache_ref, cache_out.at[place]), (tok_ref, tok_out.at[n])):
        cp = pltpu.make_async_copy(src, dst, local_sem.at[len(locals_)])
        cp.start()
        locals_.append(cp)
    for k in range(1, per_plane):
        peer = lax.rem(me_xc + k, per_plane)
        cp = pltpu.make_async_remote_copy(
            src_ref=blk_ref, dst_ref=out_ref.at[me],
            send_sem=plane_send.at[k], recv_sem=plane_recv.at[k],
            device_id=(z, peer // nc, lax.rem(peer, nc), n), device_id_type=MESH_ID)
        cp.start()
        sends.append(cp)
    locals_[0].wait()
    for k in range(1, 2 * nc):
        cp = pltpu.make_async_remote_copy(
            src_ref=cache_ref, dst_ref=cache_out.at[place],
            send_sem=cache_send.at[k], recv_sem=cache_recv.at[k],
            device_id=group_dev(place ^ k), device_id_type=MESH_ID)
        cp.start()
        sends.append(cp)
    for k in range(1, nn):
        cp = pltpu.make_async_remote_copy(
            src_ref=tok_ref, dst_ref=tok_out.at[n],
            send_sem=tok_send.at[k], recv_sem=tok_recv.at[k],
            device_id=(z, x, c, lax.rem(n + k, nn)), device_id_type=MESH_ID)
        cp.start()
        sends.append(cp)

    subs = RING_SUBS
    sub_len = per_plane // subs

    def sub_slot(pz, j):
        return out_ref.at[pl.ds(pl.multiple_of(pz * per_plane + j * sub_len, sub_len), sub_len)]

    def ring_copy(s, j, pz, device):
        return pltpu.make_async_remote_copy(
            src_ref=sub_slot(pz, j), dst_ref=sub_slot(pz, j),
            send_sem=ring_send.at[s - 1, j], recv_sem=ring_recv.at[s - 1, j],
            device_id=device, device_id_type=MESH_ID)

    def die_copy(s, j, pz):
        return pltpu.make_async_remote_copy(
            src_ref=sub_slot(pz, j), dst_ref=sub_slot(pz, j),
            send_sem=die_send.at[s - 1, j], recv_sem=die_recv.at[s - 1, j],
            device_id=partner, device_id_type=MESH_ID)

    for s in range(1, half + 1):
        send_z = lax.rem(z - step_dir * (s - 1) + 2 * nz, nz)
        for j in range(subs):
            if s == 1:
                for b in range(sub_len):
                    held = j * sub_len + b
                    k = lax.rem(me_xc - held + per_plane, per_plane)

                    @pl.when(k != 0)
                    def _():
                        pltpu.make_async_remote_copy(
                            src_ref=blk_ref, dst_ref=out_ref.at[z * per_plane + held],
                            send_sem=plane_send.at[k], recv_sem=plane_recv.at[k],
                            device_id=(z, x, c, n), device_id_type=MESH_ID).wait_recv()
            if s > 1:
                ring_copy(s - 1, j, send_z, (src_z, x, c, n)).wait_recv()
            cp = ring_copy(s, j, send_z, (dst_z, x, c, n))
            cp.start()
            sends.append(cp)
            if s > 1:
                dp = die_copy(s - 1, j, send_z)
                dp.start()
                sends.append(dp)
    last_z = lax.rem(z - step_dir * half + 2 * nz, nz)
    for j in range(subs):
        ring_copy(half, j, last_z, (src_z, x, c, n)).wait_recv()
    for s in range(1, half):
        other_z = lax.rem(z + step_dir * s + 2 * nz, nz)
        for j in range(subs):
            die_copy(s, j, other_z).wait_recv()
    for k in range(1, 2 * nc):
        pltpu.make_async_remote_copy(
            src_ref=cache_ref, dst_ref=cache_out.at[place ^ k],
            send_sem=cache_send.at[k], recv_sem=cache_recv.at[k],
            device_id=(z, x, c, n), device_id_type=MESH_ID).wait_recv()
    for k in range(1, nn):
        pltpu.make_async_remote_copy(
            src_ref=tok_ref, dst_ref=tok_out.at[lax.rem(n - k + nn, nn)],
            send_sem=tok_send.at[k], recv_sem=tok_recv.at[k],
            device_id=(z, x, c, n), device_id_type=MESH_ID).wait_recv()
    for cp in locals_[1:]:
        cp.wait()
    for cp in sends:
        cp.wait_send()


def gather_wide(block, cache, tokens, nz, nx, nc, nn):
    count = nz * nx * nc
    half = nz // 2
    per_plane = nx * nc
    group = 2 * nc
    nbytes = block.size * block.dtype.itemsize
    return pl.pallas_call(
        functools.partial(gather_kernel, nz, nx, nc, nn),
        out_shape=(
            jax.ShapeDtypeStruct((count,) + block.shape, block.dtype),
            jax.ShapeDtypeStruct((group,) + cache.shape, cache.dtype),
            jax.ShapeDtypeStruct((nn,) + tokens.shape, tokens.dtype),
        ),
        in_specs=[pl.BlockSpec(memory_space=pl.ANY)] * 3,
        out_specs=[pl.BlockSpec(memory_space=pl.ANY)] * 3,
        scratch_shapes=[
            pltpu.SemaphoreType.DMA((per_plane,)),
            pltpu.SemaphoreType.DMA((per_plane,)),
            pltpu.SemaphoreType.DMA((half, RING_SUBS)),
            pltpu.SemaphoreType.DMA((half, RING_SUBS)),
            pltpu.SemaphoreType.DMA((half, RING_SUBS)),
            pltpu.SemaphoreType.DMA((half, RING_SUBS)),
            pltpu.SemaphoreType.DMA((3,)),
            pltpu.SemaphoreType.DMA((group,)),
            pltpu.SemaphoreType.DMA((group,)),
            pltpu.SemaphoreType.DMA((nn,)),
            pltpu.SemaphoreType.DMA((nn,)),
        ],
        compiler_params=pltpu.CompilerParams(collective_id=0, has_side_effects=True),
        cost_estimate=pl.CostEstimate(flops=0, transcendentals=0, bytes_accessed=2 * count * nbytes),
    )(block, cache, tokens)


def gather_rows(block):
    rows = block.shape[0]
    plane = lax.all_gather(block, ("z", "x"), axis=0, tiled=False)
    both = lax.all_gather(plane, "c", axis=0, tiled=False)
    both = jnp.transpose(both, (1, 0, 2, 3))
    return both.reshape(-1, block.shape[1])


def rms_normed(rows_in, gain):
    values = rows_in.astype(jnp.float32)
    scaling = lax.rsqrt(jnp.mean(values * values, axis=-1, keepdims=True) + EPSILON)
    return (values * scaling * gain.astype(jnp.float32)).astype(jnp.bfloat16)


def rotate(values, positions):
    half_dim = values.shape[-1] // 2
    inverse = ROPE_BASE ** (-(jnp.arange(half_dim, dtype=jnp.float32) * (2.0 / values.shape[-1])))
    angles = positions.astype(jnp.float32)[:, None] * inverse[None, :]
    cos_part = jnp.cos(angles)[:, None, :]
    sin_part = jnp.sin(angles)[:, None, :]
    lower = values[..., :half_dim]
    higher = values[..., half_dim:]
    return jnp.concatenate(
        [lower * cos_part - higher * sin_part, higher * cos_part + lower * sin_part], axis=-1
    )


def ordered(mine, other, upper, along):
    first_half = jnp.where(upper, other, mine)
    second_half = jnp.where(upper, mine, other)
    return jnp.concatenate([first_half, second_half], axis=along)


def empty_state(row_count, groups, repeats):
    return (
        jnp.zeros((row_count, groups, repeats, HEAD_DIM), jnp.float32),
        jnp.full((row_count, groups, repeats), LOWEST, jnp.float32),
        jnp.zeros((row_count, groups, repeats), jnp.float32),
    )


def fold_keys(state, queries, query_pos, keys, values, key_pos, key_ok, widest):
    key_count = keys.shape[1]
    groups = queries.shape[1]
    block = math.gcd(key_count, widest)
    keys_split = keys.reshape(groups, HEAD_DIM, key_count)
    values_split = values.reshape(groups, HEAD_DIM, key_count)
    scale = HEAD_DIM ** (-0.5)

    def step(index, carry):
        accum, top_old, sum_old = carry
        start = index * block
        block_keys = lax.dynamic_slice_in_dim(keys_split, start, block, 2)
        block_values = lax.dynamic_slice_in_dim(values_split, start, block, 2)
        block_pos = lax.dynamic_slice_in_dim(key_pos, start, block, 0)
        block_ok = lax.dynamic_slice_in_dim(key_ok, start, block, 0)
        scores = (
            jnp.einsum("tgrd,gdk->tgrk", queries, block_keys, preferred_element_type=jnp.float32)
            * scale
        )
        allowed = (
            block_ok[None, :]
            & (block_pos[None, :] <= query_pos[:, None])
            & (query_pos[:, None] - block_pos[None, :] < WIN)
        )
        allowed = allowed[:, None, None, :]
        top_new = jnp.maximum(top_old, jnp.max(jnp.where(allowed, scores, LOWEST), axis=-1))
        weights = jnp.where(allowed, jnp.exp(scores - top_new[..., None]), 0.0)
        rescale = jnp.exp(top_old - top_new)
        sum_new = sum_old * rescale + jnp.sum(weights, axis=-1)
        mixed = jnp.einsum(
            "tgrk,gdk->tgrd",
            weights.astype(jnp.bfloat16),
            block_values,
            preferred_element_type=jnp.float32,
        )
        return (accum * rescale[..., None] + mixed, top_new, sum_new)

    return lax.fori_loop(0, key_count // block, step, state)


def exchange(block, axis, count, pairing):
    pieces = [block]
    for k in range(1, count):
        route = [(src, pairing(src, k)) for src in range(count)]
        route = [(dst, src) for src, dst in route]
        pieces.append(lax.ppermute(block, axis, [(pairing(d, k), d) for d in range(count)]))
    return jnp.stack(pieces)


def in_member_order(stacked, me, pairing, along):
    count = stacked.shape[0]
    parts = [stacked[pairing(me, q)] for q in range(count)]
    return jnp.concatenate(parts, axis=along)


def shift_pair(me, k):
    return (me - k) % 4


def xor_pair(me, k):
    return me ^ k


def shards(
    tokens_in,
    norm_gain,
    query_weight,
    key_weight,
    value_weight,
    out_weight,
    cache_keys,
    cache_values,
    cached_len,
    append_slot,
    shard_owner,
):
    n_narrow = lax.psum(1, "narrow")
    me_narrow = lax.axis_index("narrow")
    position = lax.axis_index(WIDE)
    request = position // GROUP
    place = position % GROUP

    def narrow_pair(me, k):
        return (me - k) % n_narrow

    def narrow_src(me, q):
        return (me - q) % n_narrow


    def group_pair(d, k):
        return d ^ k

    def group_route_pieces(block):
        pieces = [block]
        for k in range(1, GROUP):
            route = [(src, src ^ k) for src in range(lax.psum(1, WIDE))]
            pieces.append(lax.ppermute(block, WIDE, route))
        return jnp.stack(pieces)


    sizes = (query_weight.shape[1], key_weight.shape[1], value_weight.shape[1], out_weight.shape[1])
    joined = jnp.concatenate([query_weight, key_weight, value_weight, out_weight], axis=1)
    block_rows, joined_width = joined.shape
    dims = (lax.psum(1, "z"), lax.psum(1, "x"), lax.psum(1, "c"))
    gathered, cache_blocks, tok_pieces = gather_wide(
        joined.reshape(-1, 128), jnp.concatenate([cache_keys, cache_values], axis=0), tokens_in,
        *dims, n_narrow)
    whole = jnp.concatenate([tok_pieces[q] for q in range(n_narrow)], axis=1)
    all_weights = gathered.reshape(-1, joined_width)
    qkv = all_weights[:, : sum(sizes[:3])]
    out_rows = all_weights[:, sum(sizes[:3]) :]

    normed = rms_normed(whole, norm_gain)
    tok_rows = whole.shape[0]
    query_width = query_weight.shape[1]
    kv_width = key_weight.shape[1]
    local_heads = query_width // HEAD_DIM
    local_groups = kv_width // HEAD_DIM
    repeats = local_heads // local_groups
    qkv_sum = jnp.dot(normed, qkv, preferred_element_type=jnp.float32)
    query_sum = qkv_sum[:, :query_width]
    key_sum = qkv_sum[:, query_width : query_width + kv_width]
    value_sum = qkv_sum[:, query_width + kv_width :]
    length = cached_len[request]
    offset = append_slot[request]
    owner = shard_owner[request]
    query_pos = length + place * tok_rows + jnp.arange(tok_rows, dtype=jnp.int32)
    queries = rotate(query_sum.reshape(tok_rows, local_heads, HEAD_DIM), query_pos).astype(
        jnp.bfloat16
    )
    queries = queries.reshape(tok_rows, local_groups, repeats, HEAD_DIM)
    new_keys = (
        rotate(key_sum.reshape(tok_rows, local_groups, HEAD_DIM), query_pos)
        .astype(jnp.bfloat16)
        .reshape(tok_rows, kv_width)
    )
    new_values = value_sum.astype(jnp.bfloat16)
    shard_rows = cache_keys.shape[1]

    old_both = jnp.concatenate([cache_blocks[q] for q in range(GROUP)], axis=1)
    old_keys = old_both[:kv_width]
    old_values = old_both[kv_width:]
    new_both = jnp.concatenate([new_keys, new_values], axis=1)
    new_both = in_member_order(group_route_pieces(new_both), place, lambda me, q: me ^ q, 0)
    new_keys = new_both[:, :kv_width]
    new_values = new_both[:, kv_width:]

    slot_index = jnp.arange(old_keys.shape[1], dtype=jnp.int32)
    cycle = (slot_index // shard_rows - owner) % GROUP * shard_rows + slot_index % shard_rows
    cached_pos = (cycle - offset + length) % WIN
    state = fold_keys(
        empty_state(tok_rows, local_groups, repeats),
        queries,
        query_pos,
        old_keys,
        old_values,
        cached_pos,
        cached_pos < length,
        512,
    )
    key_cols = new_keys.T
    value_cols = new_values.T
    new_count = key_cols.shape[1]
    new_pos = length + jnp.arange(new_count, dtype=jnp.int32)
    state = fold_keys(
        state,
        queries,
        query_pos,
        key_cols,
        value_cols,
        new_pos,
        jnp.ones((new_count,), dtype=bool),
        512,
    )
    accum, top_score, total = state
    attended = (accum / total[..., None]).astype(jnp.bfloat16).reshape(tok_rows, query_width)
    all_heads = lax.all_gather(attended, "narrow", axis=1, tiled=True)
    update = jnp.dot(all_heads, out_rows, preferred_element_type=jnp.float32).astype(jnp.bfloat16)

    first = ((place - owner) % GROUP * shard_rows - offset) % WIN
    keys_ext = jnp.concatenate(
        [key_cols, jnp.zeros((kv_width, WIN - new_count), key_cols.dtype), key_cols,
         jnp.zeros((kv_width, shard_rows - new_count), key_cols.dtype)], axis=1)
    values_ext = jnp.concatenate(
        [value_cols, jnp.zeros((kv_width, WIN - new_count), value_cols.dtype), value_cols,
         jnp.zeros((kv_width, shard_rows - new_count), value_cols.dtype)], axis=1)
    spot = (first + jnp.arange(shard_rows, dtype=jnp.int32)) % WIN
    written = spot < new_count
    put_keys = jnp.where(written[None, :], lax.dynamic_slice_in_dim(keys_ext, first, shard_rows, 1), cache_keys)
    put_values = jnp.where(written[None, :], lax.dynamic_slice_in_dim(values_ext, first, shard_rows, 1), cache_values)
    return (update, put_keys, put_values)


def solution(mesh):
    devices = mesh.devices
    wide_devices = devices[:, 0]
    xs = sorted({d.coords[0] for d in wide_devices})
    cores = sorted({getattr(d, "core_on_chip", 0) for d in wide_devices})
    n_x, n_c = len(xs), len(cores)
    n_z = devices.shape[0] // (n_x * n_c)
    fine = Mesh(devices.reshape(n_z, n_x, n_c, devices.shape[1]), ("z", "x", "c", "narrow"))
    rows = P(WIDE, "narrow")
    cols = P("narrow", WIDE)
    in_specs = (rows, P(), rows, rows, rows, rows, cols, cols, P(), P(), P())
    out_specs = (rows, cols, cols)
    return jax.shard_map(shards, mesh=fine, in_specs=in_specs, out_specs=out_specs, check_vma=False)
```

```python
import functools
import math

import numpy as np
import jax
import jax.numpy as jnp
from jax import lax
from jax.experimental import pallas as pl
from jax.experimental.pallas import tpu as pltpu
from jax.sharding import Mesh, PartitionSpec as P

MESH_ID = pl.DeviceIdType.MESH

HEAD_DIM = 80
WIN = 4096
GROUP_BITS = 2
GROUP = 4


EPSILON = 1e-05
ROPE_BASE = 10000.0
LOWEST = -1e30


def from_partner(block, axis, bit):
    count = lax.psum(1, axis)
    route = []
    for low in range(count):
        high = low | 1 << bit
        if high != low and high < count:
            route += [(low, high), (high, low)]
    return lax.ppermute(block, axis, route)


WIDE = ("z", "x", "c")
RING_SUBS = 2


def gather_kernel(nz, nx, nc, nn, blk_ref, cache_ref, tok_ref, out_ref, cache_out, tok_out,
                  plane_send, plane_recv, ring_send, ring_recv, die_send, die_recv, local_sem,
                  cache_send, cache_recv, tok_send, tok_recv):
    z = lax.axis_index("z")
    x = lax.axis_index("x")
    c = lax.axis_index("c")
    n = lax.axis_index("narrow")
    per_plane = nx * nc
    me_xc = x * nc + c
    me = z * per_plane + me_xc
    place = lax.rem(x, 2) * nc + c
    x_base = x - lax.rem(x, 2)
    half = nz // 2
    step_dir = 1 - 2 * c
    dst_z = lax.rem(z + step_dir + nz, nz)
    src_z = lax.rem(z - step_dir + nz, nz)
    partner = (z, x, 1 - c, n)

    def plane_slot(pz):
        return out_ref.at[pl.ds(pl.multiple_of(pz * per_plane, per_plane), per_plane)]

    def group_dev(p):
        return (z, x_base + p // nc, lax.rem(p, nc), n)

    barrier = pltpu.get_barrier_semaphore()
    for k in range(1, per_plane):
        peer = lax.rem(me_xc + k, per_plane)
        pl.semaphore_signal(barrier, inc=1, device_id=(z, peer // nc, lax.rem(peer, nc), n), device_id_type=MESH_ID)
    for zz in (dst_z, src_z):
        pl.semaphore_signal(barrier, inc=1, device_id=(zz, x, c, n), device_id_type=MESH_ID)
    for k in range(1, nn):
        pl.semaphore_signal(barrier, inc=1, device_id=(z, x, c, lax.rem(n + k, nn)), device_id_type=MESH_ID)
    pl.semaphore_wait(barrier, per_plane + 1 + nn - 1)

    sends = []
    locals_ = []
    for src, dst in ((blk_ref, out_ref.at[me]), (cache_ref, cache_out.at[place]), (tok_ref, tok_out.at[n])):
        cp = pltpu.make_async_copy(src, dst, local_sem.at[len(locals_)])
        cp.start()
        locals_.append(cp)
    for k in range(1, per_plane):
        peer = lax.rem(me_xc + k, per_plane)
        cp = pltpu.make_async_remote_copy(
            src_ref=blk_ref, dst_ref=out_ref.at[me],
            send_sem=plane_send.at[k], recv_sem=plane_recv.at[k],
            device_id=(z, peer // nc, lax.rem(peer, nc), n), device_id_type=MESH_ID)
        cp.start()
        sends.append(cp)
    locals_[0].wait()
    for k in range(1, 2 * nc):
        cp = pltpu.make_async_remote_copy(
            src_ref=cache_ref, dst_ref=cache_out.at[place],
            send_sem=cache_send.at[k], recv_sem=cache_recv.at[k],
            device_id=group_dev(place ^ k), device_id_type=MESH_ID)
        cp.start()
        sends.append(cp)
    for k in range(1, nn):
        cp = pltpu.make_async_remote_copy(
            src_ref=tok_ref, dst_ref=tok_out.at[n],
            send_sem=tok_send.at[k], recv_sem=tok_recv.at[k],
            device_id=(z, x, c, lax.rem(n + k, nn)), device_id_type=MESH_ID)
        cp.start()
        sends.append(cp)

    subs = RING_SUBS
    sub_len = per_plane // subs

    def sub_slot(pz, j):
        return out_ref.at[pl.ds(pl.multiple_of(pz * per_plane + j * sub_len, sub_len), sub_len)]

    def ring_copy(s, j, pz, device):
        return pltpu.make_async_remote_copy(
            src_ref=sub_slot(pz, j), dst_ref=sub_slot(pz, j),
            send_sem=ring_send.at[s - 1, j], recv_sem=ring_recv.at[s - 1, j],
            device_id=device, device_id_type=MESH_ID)

    def die_copy(s, j, pz):
        return pltpu.make_async_remote_copy(
            src_ref=sub_slot(pz, j), dst_ref=sub_slot(pz, j),
            send_sem=die_send.at[s - 1, j], recv_sem=die_recv.at[s - 1, j],
            device_id=partner, device_id_type=MESH_ID)

    for s in range(1, half + 1):
        send_z = lax.rem(z - step_dir * (s - 1) + 2 * nz, nz)
        for j in range(subs):
            if s == 1:
                for b in range(sub_len):
                    held = j * sub_len + b
                    k = lax.rem(me_xc - held + per_plane, per_plane)

                    @pl.when(k != 0)
                    def _():
                        pltpu.make_async_remote_copy(
                            src_ref=blk_ref, dst_ref=out_ref.at[z * per_plane + held],
                            send_sem=plane_send.at[k], recv_sem=plane_recv.at[k],
                            device_id=(z, x, c, n), device_id_type=MESH_ID).wait_recv()
            if s > 1:
                ring_copy(s - 1, j, send_z, (src_z, x, c, n)).wait_recv()
                if s - 1 < half:
                    dp = die_copy(s - 1, j, send_z)
                    dp.start()
                    sends.append(dp)
            cp = ring_copy(s, j, send_z, (dst_z, x, c, n))
            cp.start()
            sends.append(cp)
    last_z = lax.rem(z - step_dir * half + 2 * nz, nz)
    for j in range(subs):
        ring_copy(half, j, last_z, (src_z, x, c, n)).wait_recv()
    for s in range(1, half):
        other_z = lax.rem(z + step_dir * s + 2 * nz, nz)
        for j in range(subs):
            die_copy(s, j, other_z).wait_recv()
    for k in range(1, 2 * nc):
        pltpu.make_async_remote_copy(
            src_ref=cache_ref, dst_ref=cache_out.at[place ^ k],
            send_sem=cache_send.at[k], recv_sem=cache_recv.at[k],
            device_id=(z, x, c, n), device_id_type=MESH_ID).wait_recv()
    for k in range(1, nn):
        pltpu.make_async_remote_copy(
            src_ref=tok_ref, dst_ref=tok_out.at[lax.rem(n - k + nn, nn)],
            send_sem=tok_send.at[k], recv_sem=tok_recv.at[k],
            device_id=(z, x, c, n), device_id_type=MESH_ID).wait_recv()
    for cp in locals_[1:]:
        cp.wait()
    for cp in sends:
        cp.wait_send()


def gather_wide(block, cache, tokens, nz, nx, nc, nn):
    count = nz * nx * nc
    half = nz // 2
    per_plane = nx * nc
    group = 2 * nc
    nbytes = block.size * block.dtype.itemsize
    return pl.pallas_call(
        functools.partial(gather_kernel, nz, nx, nc, nn),
        out_shape=(
            jax.ShapeDtypeStruct((count,) + block.shape, block.dtype),
            jax.ShapeDtypeStruct((group,) + cache.shape, cache.dtype),
            jax.ShapeDtypeStruct((nn,) + tokens.shape, tokens.dtype),
        ),
        in_specs=[pl.BlockSpec(memory_space=pl.ANY)] * 3,
        out_specs=[pl.BlockSpec(memory_space=pl.ANY)] * 3,
        scratch_shapes=[
            pltpu.SemaphoreType.DMA((per_plane,)),
            pltpu.SemaphoreType.DMA((per_plane,)),
            pltpu.SemaphoreType.DMA((half, RING_SUBS)),
            pltpu.SemaphoreType.DMA((half, RING_SUBS)),
            pltpu.SemaphoreType.DMA((half, RING_SUBS)),
            pltpu.SemaphoreType.DMA((half, RING_SUBS)),
            pltpu.SemaphoreType.DMA((3,)),
            pltpu.SemaphoreType.DMA((group,)),
            pltpu.SemaphoreType.DMA((group,)),
            pltpu.SemaphoreType.DMA((nn,)),
            pltpu.SemaphoreType.DMA((nn,)),
        ],
        compiler_params=pltpu.CompilerParams(collective_id=0, has_side_effects=True),
        cost_estimate=pl.CostEstimate(flops=0, transcendentals=0, bytes_accessed=2 * count * nbytes),
    )(block, cache, tokens)


def gather_rows(block):
    rows = block.shape[0]
    plane = lax.all_gather(block, ("z", "x"), axis=0, tiled=False)
    both = lax.all_gather(plane, "c", axis=0, tiled=False)
    both = jnp.transpose(both, (1, 0, 2, 3))
    return both.reshape(-1, block.shape[1])


def rms_normed(rows_in, gain):
    values = rows_in.astype(jnp.float32)
    scaling = lax.rsqrt(jnp.mean(values * values, axis=-1, keepdims=True) + EPSILON)
    return (values * scaling * gain.astype(jnp.float32)).astype(jnp.bfloat16)


def rotate(values, positions):
    half_dim = values.shape[-1] // 2
    inverse = ROPE_BASE ** (-(jnp.arange(half_dim, dtype=jnp.float32) * (2.0 / values.shape[-1])))
    angles = positions.astype(jnp.float32)[:, None] * inverse[None, :]
    cos_part = jnp.cos(angles)[:, None, :]
    sin_part = jnp.sin(angles)[:, None, :]
    lower = values[..., :half_dim]
    higher = values[..., half_dim:]
    return jnp.concatenate(
        [lower * cos_part - higher * sin_part, higher * cos_part + lower * sin_part], axis=-1
    )


def ordered(mine, other, upper, along):
    first_half = jnp.where(upper, other, mine)
    second_half = jnp.where(upper, mine, other)
    return jnp.concatenate([first_half, second_half], axis=along)


def empty_state(row_count, groups, repeats):
    return (
        jnp.zeros((row_count, groups, repeats, HEAD_DIM), jnp.float32),
        jnp.full((row_count, groups, repeats), LOWEST, jnp.float32),
        jnp.zeros((row_count, groups, repeats), jnp.float32),
    )


def fold_keys(state, queries, query_pos, keys, values, key_pos, key_ok, widest):
    key_count = keys.shape[1]
    groups = queries.shape[1]
    block = math.gcd(key_count, widest)
    keys_split = keys.reshape(groups, HEAD_DIM, key_count)
    values_split = values.reshape(groups, HEAD_DIM, key_count)
    scale = HEAD_DIM ** (-0.5)

    def step(index, carry):
        accum, top_old, sum_old = carry
        start = index * block
        block_keys = lax.dynamic_slice_in_dim(keys_split, start, block, 2)
        block_values = lax.dynamic_slice_in_dim(values_split, start, block, 2)
        block_pos = lax.dynamic_slice_in_dim(key_pos, start, block, 0)
        block_ok = lax.dynamic_slice_in_dim(key_ok, start, block, 0)
        scores = (
            jnp.einsum("tgrd,gdk->tgrk", queries, block_keys, preferred_element_type=jnp.float32)
            * scale
        )
        allowed = (
            block_ok[None, :]
            & (block_pos[None, :] <= query_pos[:, None])
            & (query_pos[:, None] - block_pos[None, :] < WIN)
        )
        allowed = allowed[:, None, None, :]
        top_new = jnp.maximum(top_old, jnp.max(jnp.where(allowed, scores, LOWEST), axis=-1))
        weights = jnp.where(allowed, jnp.exp(scores - top_new[..., None]), 0.0)
        rescale = jnp.exp(top_old - top_new)
        sum_new = sum_old * rescale + jnp.sum(weights, axis=-1)
        mixed = jnp.einsum(
            "tgrk,gdk->tgrd",
            weights.astype(jnp.bfloat16),
            block_values,
            preferred_element_type=jnp.float32,
        )
        return (accum * rescale[..., None] + mixed, top_new, sum_new)

    return lax.fori_loop(0, key_count // block, step, state)


def exchange(block, axis, count, pairing):
    pieces = [block]
    for k in range(1, count):
        route = [(src, pairing(src, k)) for src in range(count)]
        route = [(dst, src) for src, dst in route]
        pieces.append(lax.ppermute(block, axis, [(pairing(d, k), d) for d in range(count)]))
    return jnp.stack(pieces)


def in_member_order(stacked, me, pairing, along):
    count = stacked.shape[0]
    parts = [stacked[pairing(me, q)] for q in range(count)]
    return jnp.concatenate(parts, axis=along)


def shift_pair(me, k):
    return (me - k) % 4


def xor_pair(me, k):
    return me ^ k


def shards(
    tokens_in,
    norm_gain,
    query_weight,
    key_weight,
    value_weight,
    out_weight,
    cache_keys,
    cache_values,
    cached_len,
    append_slot,
    shard_owner,
):
    n_narrow = lax.psum(1, "narrow")
    me_narrow = lax.axis_index("narrow")
    position = lax.axis_index(WIDE)
    request = position // GROUP
    place = position % GROUP

    def narrow_pair(me, k):
        return (me - k) % n_narrow

    def narrow_src(me, q):
        return (me - q) % n_narrow


    def group_pair(d, k):
        return d ^ k

    def group_route_pieces(block):
        pieces = [block]
        for k in range(1, GROUP):
            route = [(src, src ^ k) for src in range(lax.psum(1, WIDE))]
            pieces.append(lax.ppermute(block, WIDE, route))
        return jnp.stack(pieces)


    sizes = (query_weight.shape[1], key_weight.shape[1], value_weight.shape[1], out_weight.shape[1])
    joined = jnp.concatenate([query_weight, key_weight, value_weight, out_weight], axis=1)
    block_rows, joined_width = joined.shape
    dims = (lax.psum(1, "z"), lax.psum(1, "x"), lax.psum(1, "c"))
    gathered, cache_blocks, tok_pieces = gather_wide(
        joined.reshape(-1, 128), jnp.concatenate([cache_keys, cache_values], axis=0), tokens_in,
        *dims, n_narrow)
    whole = jnp.concatenate([tok_pieces[q] for q in range(n_narrow)], axis=1)
    all_weights = gathered.reshape(-1, joined_width)
    qkv = all_weights[:, : sum(sizes[:3])]
    out_rows = all_weights[:, sum(sizes[:3]) :]

    normed = rms_normed(whole, norm_gain)
    tok_rows = whole.shape[0]
    query_width = query_weight.shape[1]
    kv_width = key_weight.shape[1]
    local_heads = query_width // HEAD_DIM
    local_groups = kv_width // HEAD_DIM
    repeats = local_heads // local_groups
    qkv_sum = jnp.dot(normed, qkv, preferred_element_type=jnp.float32)
    query_sum = qkv_sum[:, :query_width]
    key_sum = qkv_sum[:, query_width : query_width + kv_width]
    value_sum = qkv_sum[:, query_width + kv_width :]
    length = cached_len[request]
    offset = append_slot[request]
    owner = shard_owner[request]
    query_pos = length + place * tok_rows + jnp.arange(tok_rows, dtype=jnp.int32)
    queries = rotate(query_sum.reshape(tok_rows, local_heads, HEAD_DIM), query_pos).astype(
        jnp.bfloat16
    )
    queries = queries.reshape(tok_rows, local_groups, repeats, HEAD_DIM)
    new_keys = (
        rotate(key_sum.reshape(tok_rows, local_groups, HEAD_DIM), query_pos)
        .astype(jnp.bfloat16)
        .reshape(tok_rows, kv_width)
    )
    new_values = value_sum.astype(jnp.bfloat16)
    shard_rows = cache_keys.shape[1]

    old_both = jnp.concatenate([cache_blocks[q] for q in range(GROUP)], axis=1)
    old_keys = old_both[:kv_width]
    old_values = old_both[kv_width:]
    new_both = jnp.concatenate([new_keys, new_values], axis=1)
    new_both = in_member_order(group_route_pieces(new_both), place, lambda me, q: me ^ q, 0)
    new_keys = new_both[:, :kv_width]
    new_values = new_both[:, kv_width:]

    slot_index = jnp.arange(old_keys.shape[1], dtype=jnp.int32)
    cycle = (slot_index // shard_rows - owner) % GROUP * shard_rows + slot_index % shard_rows
    cached_pos = (cycle - offset + length) % WIN
    state = fold_keys(
        empty_state(tok_rows, local_groups, repeats),
        queries,
        query_pos,
        old_keys,
        old_values,
        cached_pos,
        cached_pos < length,
        512,
    )
    key_cols = new_keys.T
    value_cols = new_values.T
    new_count = key_cols.shape[1]
    new_pos = length + jnp.arange(new_count, dtype=jnp.int32)
    state = fold_keys(
        state,
        queries,
        query_pos,
        key_cols,
        value_cols,
        new_pos,
        jnp.ones((new_count,), dtype=bool),
        512,
    )
    accum, top_score, total = state
    attended = (accum / total[..., None]).astype(jnp.bfloat16).reshape(tok_rows, query_width)
    all_heads = lax.all_gather(attended, "narrow", axis=1, tiled=True)
    update = jnp.dot(all_heads, out_rows, preferred_element_type=jnp.float32).astype(jnp.bfloat16)

    first = ((place - owner) % GROUP * shard_rows - offset) % WIN
    keys_ext = jnp.concatenate(
        [key_cols, jnp.zeros((kv_width, WIN - new_count), key_cols.dtype), key_cols,
         jnp.zeros((kv_width, shard_rows - new_count), key_cols.dtype)], axis=1)
    values_ext = jnp.concatenate(
        [value_cols, jnp.zeros((kv_width, WIN - new_count), value_cols.dtype), value_cols,
         jnp.zeros((kv_width, shard_rows - new_count), value_cols.dtype)], axis=1)
    spot = (first + jnp.arange(shard_rows, dtype=jnp.int32)) % WIN
    written = spot < new_count
    put_keys = jnp.where(written[None, :], lax.dynamic_slice_in_dim(keys_ext, first, shard_rows, 1), cache_keys)
    put_values = jnp.where(written[None, :], lax.dynamic_slice_in_dim(values_ext, first, shard_rows, 1), cache_values)
    return (update, put_keys, put_values)


def solution(mesh):
    devices = mesh.devices
    wide_devices = devices[:, 0]
    xs = sorted({d.coords[0] for d in wide_devices})
    cores = sorted({getattr(d, "core_on_chip", 0) for d in wide_devices})
    n_x, n_c = len(xs), len(cores)
    n_z = devices.shape[0] // (n_x * n_c)
    fine = Mesh(devices.reshape(n_z, n_x, n_c, devices.shape[1]), ("z", "x", "c", "narrow"))
    rows = P(WIDE, "narrow")
    cols = P("narrow", WIDE)
    in_specs = (rows, P(), rows, rows, rows, rows, cols, cols, P(), P(), P())
    out_specs = (rows, cols, cols)
    return jax.shard_map(shards, mesh=fine, in_specs=in_specs, out_specs=out_specs, check_vma=False)
```

```python
import functools
import math

import numpy as np
import jax
import jax.numpy as jnp
from jax import lax
from jax.experimental import pallas as pl
from jax.experimental.pallas import tpu as pltpu
from jax.sharding import Mesh, PartitionSpec as P

MESH_ID = pl.DeviceIdType.MESH

HEAD_DIM = 80
WIN = 4096
GROUP_BITS = 2
GROUP = 4


EPSILON = 1e-05
ROPE_BASE = 10000.0
LOWEST = -1e30


def from_partner(block, axis, bit):
    count = lax.psum(1, axis)
    route = []
    for low in range(count):
        high = low | 1 << bit
        if high != low and high < count:
            route += [(low, high), (high, low)]
    return lax.ppermute(block, axis, route)


WIDE = ("z", "x", "c")
RING_SUBS = 4


def gather_kernel(nz, nx, nc, nn, blk_ref, cache_ref, tok_ref, out_ref, cache_out, tok_out,
                  plane_send, plane_recv, ring_send, ring_recv, die_send, die_recv, local_sem,
                  cache_send, cache_recv, tok_send, tok_recv):
    z = lax.axis_index("z")
    x = lax.axis_index("x")
    c = lax.axis_index("c")
    n = lax.axis_index("narrow")
    per_plane = nx * nc
    me_xc = x * nc + c
    me = z * per_plane + me_xc
    place = lax.rem(x, 2) * nc + c
    x_base = x - lax.rem(x, 2)
    half = nz // 2
    step_dir = 1 - 2 * c
    dst_z = lax.rem(z + step_dir + nz, nz)
    src_z = lax.rem(z - step_dir + nz, nz)
    partner = (z, x, 1 - c, n)

    def plane_slot(pz):
        return out_ref.at[pl.ds(pl.multiple_of(pz * per_plane, per_plane), per_plane)]

    def group_dev(p):
        return (z, x_base + p // nc, lax.rem(p, nc), n)

    barrier = pltpu.get_barrier_semaphore()
    for k in range(1, per_plane):
        peer = lax.rem(me_xc + k, per_plane)
        pl.semaphore_signal(barrier, inc=1, device_id=(z, peer // nc, lax.rem(peer, nc), n), device_id_type=MESH_ID)
    for zz in (dst_z, src_z):
        pl.semaphore_signal(barrier, inc=1, device_id=(zz, x, c, n), device_id_type=MESH_ID)
    for k in range(1, nn):
        pl.semaphore_signal(barrier, inc=1, device_id=(z, x, c, lax.rem(n + k, nn)), device_id_type=MESH_ID)
    pl.semaphore_wait(barrier, per_plane + 1 + nn - 1)

    sends = []
    locals_ = []
    for src, dst in ((blk_ref, out_ref.at[me]), (cache_ref, cache_out.at[place]), (tok_ref, tok_out.at[n])):
        cp = pltpu.make_async_copy(src, dst, local_sem.at[len(locals_)])
        cp.start()
        locals_.append(cp)
    for k in range(1, per_plane):
        peer = lax.rem(me_xc + k, per_plane)
        cp = pltpu.make_async_remote_copy(
            src_ref=blk_ref, dst_ref=out_ref.at[me],
            send_sem=plane_send.at[k], recv_sem=plane_recv.at[k],
            device_id=(z, peer // nc, lax.rem(peer, nc), n), device_id_type=MESH_ID)
        cp.start()
        sends.append(cp)
    locals_[0].wait()
    subs = RING_SUBS
    sub_len = per_plane // subs

    def sub_slot(pz, j):
        return out_ref.at[pl.ds(pl.multiple_of(pz * per_plane + j * sub_len, sub_len), sub_len)]

    def ring_copy(s, j, pz, device):
        return pltpu.make_async_remote_copy(
            src_ref=sub_slot(pz, j), dst_ref=sub_slot(pz, j),
            send_sem=ring_send.at[s - 1, j], recv_sem=ring_recv.at[s - 1, j],
            device_id=device, device_id_type=MESH_ID)

    def die_copy(s, j, pz):
        return pltpu.make_async_remote_copy(
            src_ref=sub_slot(pz, j), dst_ref=sub_slot(pz, j),
            send_sem=die_send.at[s - 1, j], recv_sem=die_recv.at[s - 1, j],
            device_id=partner, device_id_type=MESH_ID)

    for s in range(1, half + 1):
        send_z = lax.rem(z - step_dir * (s - 1) + 2 * nz, nz)
        for j in range(subs):
            if s == 1:
                for b in range(sub_len):
                    held = j * sub_len + b
                    k = lax.rem(me_xc - held + per_plane, per_plane)

                    @pl.when(k != 0)
                    def _():
                        pltpu.make_async_remote_copy(
                            src_ref=blk_ref, dst_ref=out_ref.at[z * per_plane + held],
                            send_sem=plane_send.at[k], recv_sem=plane_recv.at[k],
                            device_id=(z, x, c, n), device_id_type=MESH_ID).wait_recv()
            if s > 1:
                ring_copy(s - 1, j, send_z, (src_z, x, c, n)).wait_recv()
                if s - 1 < half:
                    dp = die_copy(s - 1, j, send_z)
                    dp.start()
                    sends.append(dp)
            cp = ring_copy(s, j, send_z, (dst_z, x, c, n))
            cp.start()
            sends.append(cp)
        if s == 1:
            for k in range(1, 2 * nc):
                cp = pltpu.make_async_remote_copy(
                    src_ref=cache_ref, dst_ref=cache_out.at[place],
                    send_sem=cache_send.at[k], recv_sem=cache_recv.at[k],
                    device_id=group_dev(place ^ k), device_id_type=MESH_ID)
                cp.start()
                sends.append(cp)
            for k in range(1, nn):
                cp = pltpu.make_async_remote_copy(
                    src_ref=tok_ref, dst_ref=tok_out.at[n],
                    send_sem=tok_send.at[k], recv_sem=tok_recv.at[k],
                    device_id=(z, x, c, lax.rem(n + k, nn)), device_id_type=MESH_ID)
                cp.start()
                sends.append(cp)
    last_z = lax.rem(z - step_dir * half + 2 * nz, nz)
    for j in range(subs):
        ring_copy(half, j, last_z, (src_z, x, c, n)).wait_recv()
    for s in range(1, half):
        other_z = lax.rem(z + step_dir * s + 2 * nz, nz)
        for j in range(subs):
            die_copy(s, j, other_z).wait_recv()
    for k in range(1, 2 * nc):
        pltpu.make_async_remote_copy(
            src_ref=cache_ref, dst_ref=cache_out.at[place ^ k],
            send_sem=cache_send.at[k], recv_sem=cache_recv.at[k],
            device_id=(z, x, c, n), device_id_type=MESH_ID).wait_recv()
    for k in range(1, nn):
        pltpu.make_async_remote_copy(
            src_ref=tok_ref, dst_ref=tok_out.at[lax.rem(n - k + nn, nn)],
            send_sem=tok_send.at[k], recv_sem=tok_recv.at[k],
            device_id=(z, x, c, n), device_id_type=MESH_ID).wait_recv()
    for cp in locals_[1:]:
        cp.wait()
    for cp in sends:
        cp.wait_send()


def gather_wide(block, cache, tokens, nz, nx, nc, nn):
    count = nz * nx * nc
    half = nz // 2
    per_plane = nx * nc
    group = 2 * nc
    nbytes = block.size * block.dtype.itemsize
    return pl.pallas_call(
        functools.partial(gather_kernel, nz, nx, nc, nn),
        out_shape=(
            jax.ShapeDtypeStruct((count,) + block.shape, block.dtype),
            jax.ShapeDtypeStruct((group,) + cache.shape, cache.dtype),
            jax.ShapeDtypeStruct((nn,) + tokens.shape, tokens.dtype),
        ),
        in_specs=[pl.BlockSpec(memory_space=pl.ANY)] * 3,
        out_specs=[pl.BlockSpec(memory_space=pl.ANY)] * 3,
        scratch_shapes=[
            pltpu.SemaphoreType.DMA((per_plane,)),
            pltpu.SemaphoreType.DMA((per_plane,)),
            pltpu.SemaphoreType.DMA((half, RING_SUBS)),
            pltpu.SemaphoreType.DMA((half, RING_SUBS)),
            pltpu.SemaphoreType.DMA((half, RING_SUBS)),
            pltpu.SemaphoreType.DMA((half, RING_SUBS)),
            pltpu.SemaphoreType.DMA((3,)),
            pltpu.SemaphoreType.DMA((group,)),
            pltpu.SemaphoreType.DMA((group,)),
            pltpu.SemaphoreType.DMA((nn,)),
            pltpu.SemaphoreType.DMA((nn,)),
        ],
        compiler_params=pltpu.CompilerParams(collective_id=0, has_side_effects=True),
        cost_estimate=pl.CostEstimate(flops=0, transcendentals=0, bytes_accessed=2 * count * nbytes),
    )(block, cache, tokens)


def gather_rows(block):
    rows = block.shape[0]
    plane = lax.all_gather(block, ("z", "x"), axis=0, tiled=False)
    both = lax.all_gather(plane, "c", axis=0, tiled=False)
    both = jnp.transpose(both, (1, 0, 2, 3))
    return both.reshape(-1, block.shape[1])


def rms_normed(rows_in, gain):
    values = rows_in.astype(jnp.float32)
    scaling = lax.rsqrt(jnp.mean(values * values, axis=-1, keepdims=True) + EPSILON)
    return (values * scaling * gain.astype(jnp.float32)).astype(jnp.bfloat16)


def rotate(values, positions):
    half_dim = values.shape[-1] // 2
    inverse = ROPE_BASE ** (-(jnp.arange(half_dim, dtype=jnp.float32) * (2.0 / values.shape[-1])))
    angles = positions.astype(jnp.float32)[:, None] * inverse[None, :]
    cos_part = jnp.cos(angles)[:, None, :]
    sin_part = jnp.sin(angles)[:, None, :]
    lower = values[..., :half_dim]
    higher = values[..., half_dim:]
    return jnp.concatenate(
        [lower * cos_part - higher * sin_part, higher * cos_part + lower * sin_part], axis=-1
    )


def ordered(mine, other, upper, along):
    first_half = jnp.where(upper, other, mine)
    second_half = jnp.where(upper, mine, other)
    return jnp.concatenate([first_half, second_half], axis=along)


def empty_state(row_count, groups, repeats):
    return (
        jnp.zeros((row_count, groups, repeats, HEAD_DIM), jnp.float32),
        jnp.full((row_count, groups, repeats), LOWEST, jnp.float32),
        jnp.zeros((row_count, groups, repeats), jnp.float32),
    )


def fold_keys(state, queries, query_pos, keys, values, key_pos, key_ok, widest):
    key_count = keys.shape[1]
    groups = queries.shape[1]
    block = math.gcd(key_count, widest)
    keys_split = keys.reshape(groups, HEAD_DIM, key_count)
    values_split = values.reshape(groups, HEAD_DIM, key_count)
    scale = HEAD_DIM ** (-0.5)

    def step(index, carry):
        accum, top_old, sum_old = carry
        start = index * block
        block_keys = lax.dynamic_slice_in_dim(keys_split, start, block, 2)
        block_values = lax.dynamic_slice_in_dim(values_split, start, block, 2)
        block_pos = lax.dynamic_slice_in_dim(key_pos, start, block, 0)
        block_ok = lax.dynamic_slice_in_dim(key_ok, start, block, 0)
        scores = (
            jnp.einsum("tgrd,gdk->tgrk", queries, block_keys, preferred_element_type=jnp.float32)
            * scale
        )
        allowed = (
            block_ok[None, :]
            & (block_pos[None, :] <= query_pos[:, None])
            & (query_pos[:, None] - block_pos[None, :] < WIN)
        )
        allowed = allowed[:, None, None, :]
        top_new = jnp.maximum(top_old, jnp.max(jnp.where(allowed, scores, LOWEST), axis=-1))
        weights = jnp.where(allowed, jnp.exp(scores - top_new[..., None]), 0.0)
        rescale = jnp.exp(top_old - top_new)
        sum_new = sum_old * rescale + jnp.sum(weights, axis=-1)
        mixed = jnp.einsum(
            "tgrk,gdk->tgrd",
            weights.astype(jnp.bfloat16),
            block_values,
            preferred_element_type=jnp.float32,
        )
        return (accum * rescale[..., None] + mixed, top_new, sum_new)

    return lax.fori_loop(0, key_count // block, step, state)


def exchange(block, axis, count, pairing):
    pieces = [block]
    for k in range(1, count):
        route = [(src, pairing(src, k)) for src in range(count)]
        route = [(dst, src) for src, dst in route]
        pieces.append(lax.ppermute(block, axis, [(pairing(d, k), d) for d in range(count)]))
    return jnp.stack(pieces)


def in_member_order(stacked, me, pairing, along):
    count = stacked.shape[0]
    parts = [stacked[pairing(me, q)] for q in range(count)]
    return jnp.concatenate(parts, axis=along)


def shift_pair(me, k):
    return (me - k) % 4


def xor_pair(me, k):
    return me ^ k


def shards(
    tokens_in,
    norm_gain,
    query_weight,
    key_weight,
    value_weight,
    out_weight,
    cache_keys,
    cache_values,
    cached_len,
    append_slot,
    shard_owner,
):
    n_narrow = lax.psum(1, "narrow")
    me_narrow = lax.axis_index("narrow")
    position = lax.axis_index(WIDE)
    request = position // GROUP
    place = position % GROUP

    def narrow_pair(me, k):
        return (me - k) % n_narrow

    def narrow_src(me, q):
        return (me - q) % n_narrow


    def group_pair(d, k):
        return d ^ k

    def group_route_pieces(block):
        pieces = [block]
        for k in range(1, GROUP):
            route = [(src, src ^ k) for src in range(lax.psum(1, WIDE))]
            pieces.append(lax.ppermute(block, WIDE, route))
        return jnp.stack(pieces)


    sizes = (query_weight.shape[1], key_weight.shape[1], value_weight.shape[1], out_weight.shape[1])
    joined = jnp.concatenate([query_weight, key_weight, value_weight, out_weight], axis=1)
    block_rows, joined_width = joined.shape
    dims = (lax.psum(1, "z"), lax.psum(1, "x"), lax.psum(1, "c"))
    gathered, cache_blocks, tok_pieces = gather_wide(
        joined.reshape(-1, 128), jnp.concatenate([cache_keys, cache_values], axis=0), tokens_in,
        *dims, n_narrow)
    whole = jnp.concatenate([tok_pieces[q] for q in range(n_narrow)], axis=1)
    all_weights = gathered.reshape(-1, joined_width)
    qkv = all_weights[:, : sum(sizes[:3])]
    out_rows = all_weights[:, sum(sizes[:3]) :]

    normed = rms_normed(whole, norm_gain)
    tok_rows = whole.shape[0]
    query_width = query_weight.shape[1]
    kv_width = key_weight.shape[1]
    local_heads = query_width // HEAD_DIM
    local_groups = kv_width // HEAD_DIM
    repeats = local_heads // local_groups
    qkv_sum = jnp.dot(normed, qkv, preferred_element_type=jnp.float32)
    query_sum = qkv_sum[:, :query_width]
    key_sum = qkv_sum[:, query_width : query_width + kv_width]
    value_sum = qkv_sum[:, query_width + kv_width :]
    length = cached_len[request]
    offset = append_slot[request]
    owner = shard_owner[request]
    query_pos = length + place * tok_rows + jnp.arange(tok_rows, dtype=jnp.int32)
    queries = rotate(query_sum.reshape(tok_rows, local_heads, HEAD_DIM), query_pos).astype(
        jnp.bfloat16
    )
    queries = queries.reshape(tok_rows, local_groups, repeats, HEAD_DIM)
    new_keys = (
        rotate(key_sum.reshape(tok_rows, local_groups, HEAD_DIM), query_pos)
        .astype(jnp.bfloat16)
        .reshape(tok_rows, kv_width)
    )
    new_values = value_sum.astype(jnp.bfloat16)
    shard_rows = cache_keys.shape[1]

    old_both = jnp.concatenate([cache_blocks[q] for q in range(GROUP)], axis=1)
    old_keys = old_both[:kv_width]
    old_values = old_both[kv_width:]
    new_both = jnp.concatenate([new_keys, new_values], axis=1)
    new_both = in_member_order(group_route_pieces(new_both), place, lambda me, q: me ^ q, 0)
    new_keys = new_both[:, :kv_width]
    new_values = new_both[:, kv_width:]

    slot_index = jnp.arange(old_keys.shape[1], dtype=jnp.int32)
    cycle = (slot_index // shard_rows - owner) % GROUP * shard_rows + slot_index % shard_rows
    cached_pos = (cycle - offset + length) % WIN
    state = fold_keys(
        empty_state(tok_rows, local_groups, repeats),
        queries,
        query_pos,
        old_keys,
        old_values,
        cached_pos,
        cached_pos < length,
        512,
    )
    key_cols = new_keys.T
    value_cols = new_values.T
    new_count = key_cols.shape[1]
    new_pos = length + jnp.arange(new_count, dtype=jnp.int32)
    state = fold_keys(
        state,
        queries,
        query_pos,
        key_cols,
        value_cols,
        new_pos,
        jnp.ones((new_count,), dtype=bool),
        512,
    )
    accum, top_score, total = state
    attended = (accum / total[..., None]).astype(jnp.bfloat16).reshape(tok_rows, query_width)
    all_heads = lax.all_gather(attended, "narrow", axis=1, tiled=True)
    update = jnp.dot(all_heads, out_rows, preferred_element_type=jnp.float32).astype(jnp.bfloat16)

    first = ((place - owner) % GROUP * shard_rows - offset) % WIN
    keys_ext = jnp.concatenate(
        [key_cols, jnp.zeros((kv_width, WIN - new_count), key_cols.dtype), key_cols,
         jnp.zeros((kv_width, shard_rows - new_count), key_cols.dtype)], axis=1)
    values_ext = jnp.concatenate(
        [value_cols, jnp.zeros((kv_width, WIN - new_count), value_cols.dtype), value_cols,
         jnp.zeros((kv_width, shard_rows - new_count), value_cols.dtype)], axis=1)
    spot = (first + jnp.arange(shard_rows, dtype=jnp.int32)) % WIN
    written = spot < new_count
    put_keys = jnp.where(written[None, :], lax.dynamic_slice_in_dim(keys_ext, first, shard_rows, 1), cache_keys)
    put_values = jnp.where(written[None, :], lax.dynamic_slice_in_dim(values_ext, first, shard_rows, 1), cache_values)
    return (update, put_keys, put_values)


def solution(mesh):
    devices = mesh.devices
    wide_devices = devices[:, 0]
    xs = sorted({d.coords[0] for d in wide_devices})
    cores = sorted({getattr(d, "core_on_chip", 0) for d in wide_devices})
    n_x, n_c = len(xs), len(cores)
    n_z = devices.shape[0] // (n_x * n_c)
    fine = Mesh(devices.reshape(n_z, n_x, n_c, devices.shape[1]), ("z", "x", "c", "narrow"))
    rows = P(WIDE, "narrow")
    cols = P("narrow", WIDE)
    in_specs = (rows, P(), rows, rows, rows, rows, cols, cols, P(), P(), P())
    out_specs = (rows, cols, cols)
    return jax.shard_map(shards, mesh=fine, in_specs=in_specs, out_specs=out_specs, check_vma=False)
```
